32 devices in a mesh: dp: 8 (over y, x, core), tensor: 4 (over z).
Axes of the slice: x: 2, y: 2, z: 4, core: 2. Of those that a mesh axis runs over, the one named last changes fastest.
Arguments:
- tokens: bfloat16 [16384, 1024], P(('dp', 'tensor')), may hold values from -6 to 6
- cotangent: bfloat16 [16384, 1024], P(('dp', 'tensor')), may hold values from -6 to 6
- lengths: int32 [32], replicated, may hold values from 1 to 1024, as said below
- deal: int32 [32], replicated, may hold values from 0 to 31, as said below
- w_qkv: bfloat16 [3, 1024, 1024], P(None, 'dp', 'tensor'), may hold values from -0.1875 to 0.1875
- w_o: bfloat16 [1024, 1024], P('tensor', 'dp'), may hold values from -0.1875 to 0.1875
- w_1: bfloat16 [1024, 4096], P('dp', 'tensor'), may hold values from -0.1875 to 0.1875
- w_2: bfloat16 [4096, 1024], P('tensor', 'dp'), may hold values from -0.09375 to 0.09375
- b_qv: float32 [2, 1024], P(None, 'tensor'), may hold values from -1.8 to 1.8
- b_o: float32 [1024], replicated, may hold values from -0.3 to 0.3
- b_1: float32 [4096], P('tensor'), may hold values from -1.8 to 1.8
- b_2: float32 [1024], replicated, may hold values from -1.2 to 1.2
- ln_gain: float32 [4, 1024], replicated, may hold values from 0.25 to 1.75
- ln_bias: float32 [4, 1024], replicated, may hold values from -1.8 to 1.8
Outputs:
- output: bfloat16 [16384, 1024], P(('dp', 'tensor'))
- input_grad: bfloat16 [16384, 1024], P(('dp', 'tensor'))
- w_qkv_grad: float32 [3, 1024, 1024], P(None, 'dp', 'tensor')
- w_o_grad: float32 [1024, 1024], P('tensor', 'dp')
- w_1_grad: float32 [1024, 4096], P('dp', 'tensor')
- w_2_grad: float32 [4096, 1024], P('tensor', 'dp')
- b_qv_grad: float32 [2, 1024], P(None, 'tensor')
- b_o_grad: float32 [1024], replicated
- b_1_grad: float32 [4096], P('tensor')
- b_2_grad: float32 [1024], replicated
- ln_gain_grad: float32 [4, 1024], replicated
- ln_bias_grad: float32 [4, 1024], replicated
The draws below stay inside these ranges and needn't reach their ends.
Inputs may be any that keep to these rules, and one draw needn't show every extreme that they name: The 4 sequences that deal gives to one data group have lengths that sum to 2048, and one of them has exactly 1024 tokens. `deal`: A permutation of the sequences; slots b * 4 to b * 4 + 3 belong to data group b.
All inputs are finite; a program needn't handle non-finite values. Where the reference program divides by a largest or mean magnitude, that divisor is 1e-20 or more.
Results may differ from the reference program's by a relative error of at most 0.015.
Values may be sent and summed in bfloat16 or wider, within the bound.
A program may use at most 192 MiB of HBM per device.

```python
import math
import jax
import jax.numpy as jnp
from jax import lax

D = 1024
HEADS = 16
DH = 64
FF = 4096
TOK_DEV = 512
MAXLEN = 1024
QBLK = 512
GTOK = 2048
SPG = 4
NSEQ = 32
TOKENS = 16384
N_DP = 8
N_TENSOR = 4


def deal_layout(key):
    base_key = jax.random.fold_in(key, 7)
    order_key = jax.random.fold_in(base_key, 1)
    size_key = jax.random.fold_in(base_key, 2)
    place_key = jax.random.fold_in(base_key, 3)
    group_count = NSEQ // SPG
    dealing = jax.random.permutation(order_key, NSEQ).astype(jnp.int32)
    peer_ranks = SPG - 1
    still_pending = GTOK - MAXLEN
    equal_quota = still_pending // peer_ranks
    excess_lines = still_pending - equal_quota * peer_ranks
    element_transfers = jax.random.randint(size_key, (group_count, peer_ranks), 0, equal_quota // 2 + 1).astype(jnp.int32)
    surplus_items = (jnp.arange(peer_ranks, dtype=jnp.int32) < excess_lines).astype(jnp.int32)
    residual_spans = equal_quota + surplus_items[None, :] + element_transfers - jnp.roll(element_transfers, 1, axis=1)
    dealt = jnp.concatenate([jnp.full((group_count, 1), MAXLEN, jnp.int32), residual_spans], axis=1)
    offsets = jax.random.randint(place_key, (group_count,), 0, SPG).astype(jnp.int32)
    columns = (jnp.arange(SPG, dtype=jnp.int32)[None, :] - offsets[:, None]) % SPG
    dealt = jnp.take_along_axis(dealt, columns, axis=1)
    seq_lens = jnp.zeros((NSEQ,), jnp.int32).at[dealing].set(dealt.reshape(-1))
    return (dealing, seq_lens)


def draw_deal(key, part):
    return deal_layout(key)[0]


def draw_lengths(key, part):
    return deal_layout(key)[1]


def block_scale(stream_key, shape, cuts, least, largest):
    level, own = 1.0, jax.random.fold_in(stream_key, 6)
    for dim, blocks in cuts:
        heights = jnp.exp(jax.random.uniform(jax.random.fold_in(own, dim), (blocks,), jnp.float32, least / len(cuts), largest / len(cuts)))
        level = level * jnp.repeat(heights, shape[dim] // blocks).reshape([-1 if axis == dim else 1 for axis in range(len(shape))])
    return level


def scatter_about(key, dims, deviation, reach, split=(), kind=jnp.bfloat16):
    entries = jax.random.normal(key, dims, jnp.float32) * deviation
    if len(split) > 0:
        entries = block_scale(key, dims, split, -0.22, 0.18) * entries
    return jnp.clip(entries, min=-reach, max=reach).astype(kind)


def setup_inputs(seed: int = 0) -> dict:
    arg_keys = jax.random.split(jax.random.key(seed), 15)
    return {
        "tokens": scatter_about(arg_keys[0], (TOKENS, D), 1.0, 6.0, ((0, 32),)),
        "cotangent": scatter_about(arg_keys[1], (TOKENS, D), 1.0, 6.0, ((0, 32),)),
        "lengths": draw_lengths(jax.random.fold_in(arg_keys[14], 71), 0),
        "deal": draw_deal(jax.random.fold_in(arg_keys[14], 71), 0),
        "w_qkv": scatter_about(arg_keys[4], (3, D, D), D ** -0.5, 0.1875, ((1, 8), (2, 4))),
        "w_o": scatter_about(arg_keys[5], (D, D), D ** -0.5, 0.1875, ((0, 4), (1, 8))),
        "w_1": scatter_about(arg_keys[6], (D, FF), D ** -0.5, 0.1875, ((0, 8), (1, 4))),
        "w_2": scatter_about(arg_keys[7], (FF, D), FF ** -0.5, 0.09375, ((0, 4), (1, 8))),
        "b_qv": scatter_about(arg_keys[8], (2, D), 0.3, 1.8, ((1, 4),), jnp.float32),
        "b_o": scatter_about(arg_keys[9], (D,), 0.05, 0.3, (), jnp.float32),
        "b_1": scatter_about(arg_keys[10], (FF,), 0.3, 1.8, ((0, 4),), jnp.float32),
        "b_2": scatter_about(arg_keys[11], (D,), 0.2, 1.2, (), jnp.float32),
        "ln_gain": jnp.clip(1.0 + 0.15 * jax.random.normal(arg_keys[12], (4, D), jnp.float32), 0.25, 1.75),
        "ln_bias": scatter_about(arg_keys[13], (4, D), 0.3, 1.8, (), jnp.float32),
    }


@jax.custom_vjp
def low(v):
    return lax.optimization_barrier(v.astype(jnp.bfloat16)).astype(jnp.float32)

@jax.custom_vjp
def low_back(v):
    return v

def low_keep(v):
    return (low(v), None)

def low_pass(kept, grad):
    return (grad,)

def back_keep(v):
    return (v, None)

def back_low(kept, grad):
    return (low(grad),)
low.defvjp(low_keep, low_pass)
low_back.defvjp(back_keep, back_low)
NORM_EPS = 1e-05
RELAX_FACTOR = 32.0
MASKED_OUT = -1000000000.0
HIGH = lax.Precision.HIGHEST

def scaled_norm(values, norm_gain, norm_shift):
    peak = lax.optimization_barrier(jnp.max(jnp.abs(values), axis=-1, keepdims=True)) + NORM_EPS
    scaled = values / peak
    centred = scaled - lax.optimization_barrier(jnp.mean(scaled, axis=-1, keepdims=True))
    spread = lax.optimization_barrier(jnp.mean(centred * centred, axis=-1, keepdims=True))
    return centred * lax.rsqrt(spread + NORM_EPS) * norm_gain + norm_shift

def segment_of(seq_lens, row_total):
    seq_ends = jnp.cumsum(seq_lens).astype(jnp.int32)
    token_positions = jnp.arange(row_total, dtype=jnp.int32)
    return lax.optimization_barrier(jnp.sum((token_positions[:, None] >= seq_ends[None, :]).astype(jnp.int32), axis=1)).astype(jnp.int32)

def attend(queries, key_rows, value_rows, segment):
    row_total = queries.shape[0]
    span = QBLK + MAXLEN
    factor = 1.0 / (RELAX_FACTOR * math.sqrt(DH))
    key_pad = jnp.concatenate([jnp.zeros((MAXLEN,) + key_rows.shape[1:], jnp.float32), key_rows], 0)
    value_pad = jnp.concatenate([jnp.zeros((MAXLEN,) + value_rows.shape[1:], jnp.float32), value_rows], 0)
    seg_pad = jnp.concatenate([jnp.full((MAXLEN,), -1, jnp.int32), segment])

    def one_block(block_index):
        first = block_index * QBLK
        query_block = lax.dynamic_slice_in_dim(queries, first, QBLK, 0)
        key_block = lax.dynamic_slice_in_dim(key_pad, first, span, 0)
        value_block = lax.dynamic_slice_in_dim(value_pad, first, span, 0)
        query_seg = lax.dynamic_slice_in_dim(segment, first, QBLK, 0)
        key_seg = lax.dynamic_slice_in_dim(seg_pad, first, span, 0)
        query_pos = first + jnp.arange(QBLK, dtype=jnp.int32)
        key_pos = first - MAXLEN + jnp.arange(span, dtype=jnp.int32)
        allowed = (key_pos[None, :] <= query_pos[:, None]) & (key_seg[None, :] == query_seg[:, None])
        raw_score = jnp.einsum('qhd,khd->hqk', query_block, key_block, precision=HIGH) * factor
        score = low_back(raw_score)
        masked = jnp.where(allowed[None], score, MASKED_OUT)
        row_peak = lax.optimization_barrier(jnp.max(masked, axis=-1, keepdims=True))
        exponent = jnp.exp(RELAX_FACTOR * (masked - row_peak))
        attn_prob = low(exponent / lax.optimization_barrier(jnp.sum(exponent, axis=-1, keepdims=True)))
        return jnp.einsum('hqk,khd->qhd', attn_prob, value_block, precision=HIGH)
    blocks = lax.map(jax.checkpoint(one_block), jnp.arange(row_total // QBLK, dtype=jnp.int32))
    return blocks.reshape(row_total, -1)

def layer(hidden, w_qkv, w_o, w_1, w_2, b_qv, b_o, b_1, b_2, ln_gain, ln_bias, segment):
    row_total = hidden.shape[0]
    normed_in = low(scaled_norm(hidden, ln_gain[0], ln_bias[0]))
    queries = low(low_back(jnp.dot(normed_in, w_qkv[0], precision=HIGH) + b_qv[0]))
    key_rows = low(low_back(jnp.dot(normed_in, w_qkv[1], precision=HIGH)))
    value_rows = low(low_back(jnp.dot(normed_in, w_qkv[2], precision=HIGH) + b_qv[1]))
    head_shape = (row_total, HEADS, DH)
    mixed = attend(queries.reshape(head_shape), key_rows.reshape(head_shape), value_rows.reshape(head_shape), segment)
    heads_out = low(low_back(mixed))
    attn_out = low_back(jnp.dot(heads_out, w_o, precision=HIGH) + b_o)
    first_sum = hidden + scaled_norm(attn_out, ln_gain[1], ln_bias[1])
    normed_mid = low(scaled_norm(first_sum, ln_gain[2], ln_bias[2]))
    pre_act = low_back(jnp.dot(normed_mid, w_1, precision=HIGH) + b_1)
    act = low(jax.nn.gelu(pre_act, approximate=False))
    feedforward_output = low_back(jnp.dot(act, w_2, precision=HIGH) + b_2)
    return first_sum + scaled_norm(feedforward_output, ln_gain[3], ln_bias[3])

def reference(tokens, cotangent, lengths, deal, w_qkv, w_o, w_1, w_2, b_qv, b_o, b_1, b_2, ln_gain, ln_bias):
    group_count = N_DP
    lane_count = N_TENSOR
    sent = TOK_DEV // group_count
    row_total = TOK_DEV * lane_count
    width_all = tokens.shape[1]

    def deal_rows(array):
        shaped = array.reshape(group_count, lane_count, group_count, sent, width_all)
        return shaped.transpose(2, 1, 0, 3, 4).reshape(group_count, row_total, width_all)

    def undeal_rows(array):
        shaped = array.reshape(group_count, lane_count, group_count, sent, width_all)
        return shaped.transpose(2, 1, 0, 3, 4).reshape(group_count * row_total, width_all)
    packs = deal_rows(tokens.astype(jnp.float32))
    cot_packs = deal_rows(cotangent.astype(jnp.float32))
    params = (w_qkv.astype(jnp.float32), w_o.astype(jnp.float32), w_1.astype(jnp.float32), w_2.astype(jnp.float32), b_qv, b_o, b_1, b_2, ln_gain, ln_bias)
    group_lens = lengths[deal].reshape(group_count, -1)

    def one_pack(totals, item):
        hidden, cot_rows, seq_lens = item
        segment = segment_of(seq_lens, row_total)

        def forward(hidden_in, *weights):
            return layer(hidden_in, *weights, segment)
        result, pull = jax.vjp(forward, hidden, *params)
        grads = pull(cot_rows)
        totals = tuple((accum + part for accum, part in zip(totals, grads[1:])))
        return (totals, (result, grads[0]))
    start_totals = tuple((jnp.zeros(p.shape, jnp.float32) for p in params))
    totals, (results, hidden_grads) = lax.scan(one_pack, start_totals, (packs, cot_packs, group_lens))
    output = undeal_rows(results).astype(jnp.bfloat16)
    input_grad = undeal_rows(hidden_grads).astype(jnp.bfloat16)
    return (output, input_grad, totals[0], totals[1], totals[2], totals[3], totals[4], totals[5], totals[6], totals[7], totals[8], totals[9])
```

```python
from functools import partial

import jax
import jax.numpy as jnp
from jax import lax
from jax.experimental import pallas as pl
from jax.experimental.pallas import tpu as pltpu
from jax.sharding import PartitionSpec as P

DH = 64
HALF = 1024
NORM_EPS = 1e-05
MASKED_OUT = -1e30
BF, F32 = jnp.bfloat16, jnp.float32
QB = 256


def scaled_norm(values, norm_gain, norm_shift):
    peak = jnp.max(jnp.abs(values), axis=-1, keepdims=True) + NORM_EPS
    scaled = values / peak
    centred = scaled - jnp.mean(scaled, axis=-1, keepdims=True)
    spread = jnp.mean(centred * centred, axis=-1, keepdims=True)
    return centred * lax.rsqrt(spread + NORM_EPS) * norm_gain + norm_shift


def norm_back(values, norm_gain, norm_shift, row_grad):
    result, pull = jax.vjp(scaled_norm, values, norm_gain, norm_shift)
    return pull(row_grad)


def attn_fwd_kernel(qpos_ref, qstart_ref, kpos_ref, q_ref, k_ref, v_ref, o_ref, lse_ref):
    kpos = kpos_ref[...]
    allowed = (kpos <= qpos_ref[...]) & (kpos >= qstart_ref[...])
    bias = jnp.where(allowed, 0.0, MASKED_OUT)
    lane = lax.broadcasted_iota(jnp.int32, (1, 2 * DH), 1)
    wide = lax.broadcasted_iota(jnp.int32, lse_ref.shape, 1)
    stats = jnp.zeros(lse_ref.shape, F32)
    for pair in range(q_ref.shape[1] // (2 * DH)):
        cols = slice(pair * 2 * DH, (pair + 1) * 2 * DH)
        query, key, value = q_ref[:, cols], k_ref[:, cols], v_ref[:, cols]
        total = jnp.zeros(query.shape, F32)
        for side in range(2):
            mine = (lane >= side * DH) & (lane < (side + 1) * DH)
            part = jnp.where(mine, query * 0.125, 0.0).astype(BF)
            score = lax.dot_general(part, key, (((1,), (1,)), ((), ())), preferred_element_type=F32) + bias
            peak = jnp.max(score, axis=-1, keepdims=True)
            expo = jnp.exp(score - peak)
            norm = jnp.sum(expo, axis=-1, keepdims=True)
            prob = (expo * (1.0 / norm)).astype(BF)
            total += jnp.dot(prob, jnp.where(mine, value, jnp.zeros_like(value)), preferred_element_type=F32)
            stats = jnp.where(wide == pair * 2 + side, peak + jnp.log(norm), stats)
        o_ref[:, cols] = total.astype(BF)
    lse_ref[...] = stats


def attn_forward(qpos, qstart, kpos, q, k, v):
    rows, width = q.shape
    col = pl.BlockSpec((QB, 1), lambda i: (i, 0))
    full = pl.BlockSpec((rows, width), lambda i: (0, 0))
    return pl.pallas_call(
        attn_fwd_kernel,
        grid=(rows // QB,),
        in_specs=[col, col, pl.BlockSpec((1, rows), lambda i: (0, 0)), pl.BlockSpec((QB, width), lambda i: (i, 0)), full, full],
        out_specs=[pl.BlockSpec((QB, width), lambda i: (i, 0)), pl.BlockSpec((QB, 128), lambda i: (i, 0))],
        out_shape=[jax.ShapeDtypeStruct((rows, width), BF), jax.ShapeDtypeStruct((rows, 128), F32)],
        cost_estimate=pl.CostEstimate(flops=4 * rows * rows * width, bytes_accessed=8 * rows * width, transcendentals=rows * rows * width // DH),
        compiler_params=pltpu.CompilerParams(vmem_limit_bytes=48 << 20),
        name="attn_fwd",
    )(qpos, qstart, kpos, q, k, v)


def attn_bwd_kernel(qpos_ref, qstart_ref, kpos_ref, lse_ref, q_ref, g_ref, k_ref, v_ref, dq_ref, dk_ref, dv_ref, dk_acc, dv_acc):
    step = pl.program_id(0)

    @pl.when(step == 0)
    def _():
        dk_acc[...] = jnp.zeros_like(dk_acc)
        dv_acc[...] = jnp.zeros_like(dv_acc)

    kpos = kpos_ref[...]
    allowed = (kpos <= qpos_ref[...]) & (kpos >= qstart_ref[...])
    bias = jnp.where(allowed, 0.0, MASKED_OUT)
    lane = lax.broadcasted_iota(jnp.int32, (1, 2 * DH), 1)
    for pair in range(q_ref.shape[1] // (2 * DH)):
        cols = slice(pair * 2 * DH, (pair + 1) * 2 * DH)
        query, grad, key, value = q_ref[:, cols], g_ref[:, cols], k_ref[:, cols], v_ref[:, cols]
        dq = jnp.zeros(query.shape, F32)
        dk = jnp.zeros(key.shape, F32)
        dv = jnp.zeros(key.shape, F32)
        for side in range(2):
            mine = (lane >= side * DH) & (lane < (side + 1) * DH)
            part = jnp.where(mine, query * 0.125, 0.0).astype(BF)
            gpart = jnp.where(mine, grad, jnp.zeros_like(grad))
            score = lax.dot_general(part, key, (((1,), (1,)), ((), ())), preferred_element_type=F32) + bias
            index = pair * 2 + side
            prob = jnp.exp(score - lse_ref[:, index:index + 1])
            gprob = lax.dot_general(gpart, value, (((1,), (1,)), ((), ())), preferred_element_type=F32)
            inner = jnp.sum(prob * gprob, axis=-1, keepdims=True)
            gscore = (prob * (gprob - inner)).astype(BF)
            dq += jnp.dot(gscore, jnp.where(mine, key, jnp.zeros_like(key)), preferred_element_type=F32)
            dk += lax.dot_general(gscore, part, (((0,), (0,)), ((), ())), preferred_element_type=F32)
            dv += lax.dot_general(prob.astype(BF), gpart, (((0,), (0,)), ((), ())), preferred_element_type=F32)
        dq_ref[:, cols] = (dq * 0.125).astype(BF)
        dk_acc[:, cols] += dk
        dv_acc[:, cols] += dv

    @pl.when(step == pl.num_programs(0) - 1)
    def _():
        dk_ref[...] = dk_acc[...].astype(BF)
        dv_ref[...] = dv_acc[...].astype(BF)


def attn_backward(qpos, qstart, kpos, lse, q, grad, k, v):
    rows, width = q.shape
    col = pl.BlockSpec((QB, 1), lambda i: (i, 0))
    blk = pl.BlockSpec((QB, width), lambda i: (i, 0))
    full = pl.BlockSpec((rows, width), lambda i: (0, 0))
    wide = jax.ShapeDtypeStruct((rows, width), BF)
    return pl.pallas_call(
        attn_bwd_kernel,
        grid=(rows // QB,),
        in_specs=[col, col, pl.BlockSpec((1, rows), lambda i: (0, 0)), pl.BlockSpec((QB, 128), lambda i: (i, 0)), blk, blk, full, full],
        out_specs=[blk, full, full],
        out_shape=[wide, wide, wide],
        scratch_shapes=[pltpu.VMEM((rows, width), F32), pltpu.VMEM((rows, width), F32)],
        cost_estimate=pl.CostEstimate(flops=10 * rows * rows * width, bytes_accessed=14 * rows * width, transcendentals=rows * rows * width // DH),
        compiler_params=pltpu.CompilerParams(vmem_limit_bytes=48 << 20),
        name="attn_bwd",
    )(qpos, qstart, kpos, lse, q, grad, k, v)


def swap_dp(x, bit):
    n = lax.axis_size("dp")
    return lax.ppermute(x, "dp", [(i, i ^ bit) for i in range(n)])


def turn(x, shift):
    n = lax.axis_size("tensor")
    return lax.ppermute(x, "tensor", [(i, (i + shift) % n) for i in range(n)])


def chip_bits():
    n = lax.axis_size("dp")
    return [1 << b for b in range(1, n.bit_length() - 1)]


def core_pair(mine, other):
    core = lax.axis_index("dp") % 2
    return jnp.where(core == 0, jnp.stack([mine, other]), jnp.stack([other, mine]))


def gather_weights(mine, other):
    pair = core_pair(mine, swap_dp(other, 1)).reshape(2 * mine.shape[0], mine.shape[1])
    lanes = lax.axis_size("tensor")
    column = jnp.stack([pair] + [turn(pair, k) for k in range(1, lanes)])
    bits = chip_bits()
    if len(bits) == 2:
        low, high = bits
        first, second = swap_dp(column, low), swap_dp(column, high)
        mid = lanes // 2
        far = jnp.concatenate([swap_dp(first[:mid], high), swap_dp(second[mid:], low)])
        return {0: column, low: first, high: second, low | high: far}
    blocks = {0: column}
    for bit in bits:
        got = swap_dp(jnp.stack([blocks[m] for m in sorted(blocks)]), bit)
        blocks.update({m | bit: got[i] for i, m in enumerate(sorted(blocks))})
    return blocks


def weight_of(blocks, start, width):
    out = []
    for mask in sorted(blocks):
        part = blocks[mask][:, :, start:start + width]
        out.append(jnp.concatenate([part[k] for k in range(part.shape[0])], axis=1))
    return jnp.concatenate(out, axis=0)


def scatter_grads(parts):
    lanes = lax.axis_size("tensor")
    bits = chip_bits()
    count = 1 << len(bits)
    feats = parts[0].shape[0]
    per = feats // count

    def block(mask_index, k):
        cut = []
        for p in parts:
            w = p.shape[1] // lanes
            cut.append(p[mask_index * per:(mask_index + 1) * per, k * w:(k + 1) * w])
        return jnp.concatenate(cut, axis=1) if len(cut) > 1 else cut[0]

    def col(mask_index, ks):
        return jnp.stack([block(mask_index, k) for k in ks])

    if len(bits) == 2:
        low, high = bits
        mid = lanes // 2
        ka, kb = list(range(mid)), list(range(mid, lanes))
        sent_a = jnp.stack([col(1, ka), col(3, ka)]).astype(BF)
        sent_b = jnp.stack([col(2, kb), col(3, kb)]).astype(BF)
        got_a, got_b = swap_dp(sent_a, low), swap_dp(sent_b, high)
        pass_a = (col(2, ka) + got_a[1].astype(F32)).astype(BF)
        pass_b = (col(1, kb) + got_b[1].astype(F32)).astype(BF)
        end_a, end_b = swap_dp(pass_a, high), swap_dp(pass_b, low)
        keep_a = col(0, ka) + got_a[0].astype(F32) + end_a.astype(F32)
        keep_b = col(0, kb) + got_b[0].astype(F32) + end_b.astype(F32)
        total = [keep_a[i] for i in range(mid)] + [keep_b[i] for i in range(lanes - mid)]
    else:
        sums = {m: col(m, range(lanes)) for m in range(count)}
        for level in reversed(range(len(bits))):
            keys = [m for m in sorted(sums) if m >> level & 1]
            got = swap_dp(jnp.stack([sums[m] for m in keys]).astype(BF), bits[level])
            sums = {m ^ (1 << level): sums[m ^ (1 << level)] + got[i].astype(F32) for i, m in enumerate(keys)}
        total = [sums[0][k] for k in range(lanes)]
    own = total[0]
    for k in range(1, lanes):
        own = own + turn(total[k].astype(BF), -k).astype(F32)
    rows = own.shape[0] // 2
    core = lax.axis_index("dp") % 2
    mine = lax.dynamic_slice_in_dim(own, core * rows, rows, 0)
    other = lax.dynamic_slice_in_dim(own, (1 - core) * rows, rows, 0)
    return core_pair(mine, swap_dp(other.astype(BF), 1).astype(F32))


def deal_perms(n_dp):
    near, far = [], []
    for chip in range(n_dp // 2):
        for c in range(2):
            for j in range(4):
                source = (chip * 2 + c) * 4 + j
                near.append((source, (chip * 2 + j % 2) * 4 + 2 * c + j // 2))
                far.append((source, (chip * 2 + j % 2) * 4 + 2 * c + 1 - j // 2))
    return near, far


def feature_turn(x):
    n = lax.axis_size("dp") // 2
    chip = lax.axis_index("dp") // 2
    lead = x.shape[:-1]
    width = x.shape[-1] // n
    bits = n.bit_length() - 1
    y = x.reshape(lead + (2,) * bits + (width,))
    for b in range(bits):
        axis = len(lead) + bits - 1 - b
        y = jnp.where((chip >> b) & 1 == 1, jnp.flip(y, axis), y)
    return y.reshape(x.shape)


def body(tokens, cotangent, lengths, deal, w_qkv, w_o, w_1, w_2, b_qv, b_o, b_1, b_2, ln_gain, ln_bias):
    n_dp, lanes = lax.axis_size("dp"), lax.axis_size("tensor")
    dp, lane = lax.axis_index("dp"), lax.axis_index("tensor")
    core, chip = dp % 2, dp // 2
    rows = tokens.shape[0]
    both = ("dp", "tensor")
    near, far = deal_perms(n_dp)
    back_near, back_far = [(b, a) for a, b in near], [(b, a) for a, b in far]

    per = lengths.shape[0] // n_dp

    def pack_ends(pack):
        picked = lax.dynamic_slice_in_dim(deal, pack * per, per)
        lookup = picked[:, None] == jnp.arange(lengths.shape[0], dtype=jnp.int32)[None, :]
        lens = jnp.sum(jnp.where(lookup, lengths[None, :], 0), axis=1)
        ends = jnp.sum(jnp.where(jnp.arange(per)[:, None] >= jnp.arange(per)[None, :], lens[None, :], 0), axis=1)
        return ends, ends - lens, jnp.sum(jnp.where(lens == HALF, ends - lens, 0))

    half = lane % 2
    ends, starts, cut = pack_ends(chip * 2 + lane // 2)
    _, _, cut_home = pack_ends(dp)
    index = jnp.arange(rows, dtype=jnp.int32)
    slots = jnp.concatenate([core * rows + index, (1 - core) * rows + index])
    place = jnp.where(slots >= cut, slots + HALF * half, slots + HALF * (1 - half))
    seg_start = jnp.max(jnp.where(place[:, None] >= starts[None, :], starts[None, :], 0), axis=1)
    qpos, qstart, kpos = place[:, None], seg_start[:, None], place[None, :]
    keep = ((core * rows + index) >= cut)[:, None]
    keep_home = (((lane % 2) * rows + index) >= cut_home)[:, None]

    def deal_in(x):
        moved = lax.all_to_all(x, "dp", split_axis=0, concat_axis=0, tiled=True)
        return jnp.where(keep, lax.ppermute(moved, both, near), lax.ppermute(moved, both, far))

    def deal_out(x):
        moved = jnp.where(keep_home, lax.ppermute(x, both, back_near), lax.ppermute(x, both, back_far))
        return lax.all_to_all(moved, "dp", split_axis=0, concat_axis=0, tiled=True)

    def halves(x):
        w = x.shape[-1] // 2
        return (lax.dynamic_slice_in_dim(x, core * w, w, x.ndim - 1), lax.dynamic_slice_in_dim(x, (1 - core) * w, w, x.ndim - 1))

    qm, qo = halves(w_qkv)
    flat = lambda x: jnp.concatenate([x[0], x[1], x[2]], axis=1)
    qkv_blocks = gather_weights(flat(qm), flat(qo))
    om, oo = halves(w_o.T)
    um, uo = halves(w_1)
    dm, do = halves(w_2.T)
    up_blocks = gather_weights(jnp.concatenate([om, um], axis=1), jnp.concatenate([oo, uo], axis=1))
    down_blocks = gather_weights(dm, do)
    hw, fw = om.shape[1], um.shape[1]

    biases = lax.all_gather(jnp.concatenate([b_qv.reshape(-1), b_1]), "tensor")
    order = (lane - jnp.arange(lanes)) % lanes
    biases = jnp.take(biases, order, axis=0)
    cut_bias = lambda x: lax.dynamic_slice_in_dim(x, core * (x.shape[1] // 2), x.shape[1] // 2, 1).reshape(-1)
    nq = b_qv.shape[1]
    bias_q, bias_v, bias_1 = cut_bias(biases[:, :nq]), cut_bias(biases[:, nq:2 * nq]), cut_bias(biases[:, 2 * nq:])
    gain, shift = feature_turn(ln_gain), feature_turn(ln_bias)
    bias_o, bias_2 = feature_turn(b_o[None])[0], feature_turn(b_2[None])[0]

    def join(x):
        return jnp.concatenate([x, swap_dp(x, 1)], axis=0)

    def fold(x):
        return x[:rows] + swap_dp(x[rows:].astype(BF), 1).astype(F32)

    hidden = feature_turn(deal_in(tokens)).astype(F32)
    normed_in = join(scaled_norm(hidden, gain[0], shift[0]).astype(BF))
    weights_q, weights_k, weights_v = (weight_of(qkv_blocks, i * hw, hw) for i in range(3))
    mm = partial(jnp.dot, preferred_element_type=F32)
    mm_t = lambda a, b: lax.dot_general(a, b, (((1,), (1,)), ((), ())), preferred_element_type=F32)
    mm_g = lambda a, b: lax.dot_general(a, b, (((0,), (0,)), ((), ())), preferred_element_type=F32)
    q = (mm(normed_in, weights_q) + bias_q).astype(BF)
    k = mm(normed_in, weights_k).astype(BF)
    v = (mm(normed_in, weights_v) + bias_v).astype(BF)
    heads_out, lse = attn_forward(qpos, qstart, kpos, q, k, v)
    weights_o = weight_of(up_blocks, 0, hw)
    attn_out = fold(mm_t(heads_out, weights_o)) + bias_o
    first_sum = hidden + scaled_norm(attn_out, gain[1], shift[1])
    normed_mid = join(scaled_norm(first_sum, gain[2], shift[2]).astype(BF))
    weights_1 = weight_of(up_blocks, hw, fw)
    pre_act = mm(normed_mid, weights_1) + bias_1
    act = jax.nn.gelu(pre_act, approximate=False).astype(BF)
    weights_2 = weight_of(down_blocks, 0, fw)
    ffn_out = fold(mm_t(act, weights_2)) + bias_2
    result = first_sum + scaled_norm(ffn_out, gain[3], shift[3])
    output = deal_out(feature_turn(result.astype(BF)))

    grad_result = feature_turn(deal_in(cotangent)).astype(F32)
    grad_ffn, gain_3, shift_3 = norm_back(ffn_out, gain[3], shift[3], grad_result)
    grad_ffn_low = grad_ffn.astype(BF)
    bias_2_grad = jnp.sum(grad_ffn_low.astype(F32), axis=0)
    grad_ffn_full = join(grad_ffn_low)
    grad_act = mm(grad_ffn_full, weights_2)
    down_grad = scatter_grads([mm_g(grad_ffn_full, act)])
    _, gelu_pull = jax.vjp(partial(jax.nn.gelu, approximate=False), pre_act)
    grad_pre = gelu_pull(grad_act)[0].astype(BF)
    bias_1_grad = jnp.sum(grad_pre.astype(F32), axis=0)
    grad_mid = fold(mm_t(grad_pre, weights_1))
    up_part = mm_g(normed_mid, grad_pre)
    grad_first_part, gain_2, shift_2 = norm_back(first_sum, gain[2], shift[2], grad_mid)
    grad_first = grad_result + grad_first_part
    grad_attn, gain_1, shift_1 = norm_back(attn_out, gain[1], shift[1], grad_first)
    grad_attn_low = grad_attn.astype(BF)
    bias_o_grad = jnp.sum(grad_attn_low.astype(F32), axis=0)
    grad_attn_full = join(grad_attn_low)
    grad_heads = mm(grad_attn_full, weights_o).astype(BF)
    out_up_grad = scatter_grads([mm_g(grad_attn_full, heads_out), up_part])
    grad_q, grad_k, grad_v = attn_backward(qpos, qstart, kpos, lse, q, grad_heads, k, v)
    bias_q_grad = jnp.sum(grad_q.astype(F32), axis=0)
    bias_v_grad = jnp.sum(grad_v.astype(F32), axis=0)
    grad_in = fold(mm_t(grad_q, weights_q) + mm_t(grad_k, weights_k) + mm_t(grad_v, weights_v))
    grad_hidden_part, gain_0, shift_0 = norm_back(hidden, gain[0], shift[0], grad_in)
    input_grad = deal_out(feature_turn((grad_first + grad_hidden_part).astype(BF)))
    qkv_grad = scatter_grads([mm_g(normed_in, g) for g in (grad_q, grad_k, grad_v)])

    def by_lane(x):
        x = jnp.take(x.reshape(lanes, -1), order, axis=0)
        both_halves = jnp.stack([jnp.where(core == 0, x, 0.0), jnp.where(core == 1, x, 0.0)], axis=1)
        return both_halves.reshape(-1)

    stack = jnp.stack([gain_0, gain_1, gain_2, gain_3, shift_0, shift_1, shift_2, shift_3, bias_o_grad, bias_2_grad])
    vector = jnp.concatenate([feature_turn(stack).reshape(-1), by_lane(bias_q_grad), by_lane(bias_v_grad), by_lane(bias_1_grad)])
    vector = lax.psum(vector, both)
    d = tokens.shape[1]
    gain_total, shift_total = vector[:4 * d].reshape(4, d), vector[4 * d:8 * d].reshape(4, d)
    bias_o_total, bias_2_total = vector[8 * d:9 * d], vector[9 * d:10 * d]
    e = d
    own = lambda x: lax.dynamic_slice_in_dim(x.reshape(lanes, -1), lane, 1, 0)[0]
    bias_qv_total = jnp.stack([own(vector[10 * d:10 * d + e]), own(vector[10 * d + e:10 * d + 2 * e])])
    bias_1_total = own(vector[10 * d + 2 * e:])

    spread = lambda x: jnp.concatenate([x[0], x[1]], axis=-1)
    qkv_out = jnp.stack([spread(qkv_grad[:, :, i * hw:(i + 1) * hw]) for i in range(3)])
    return (
        output, input_grad, qkv_out,
        spread(out_up_grad[:, :, :hw]).T, spread(out_up_grad[:, :, hw:]), spread(down_grad).T,
        bias_qv_total, bias_o_total, bias_1_total, bias_2_total, gain_total, shift_total,
    )


def solution(mesh):
    rows = P(("dp", "tensor"), None)
    weights = (P(None, "dp", "tensor"), P("tensor", "dp"), P("dp", "tensor"), P("tensor", "dp"))
    vectors = (P(None, "tensor"), P(), P("tensor"), P(), P(), P())
    return jax.shard_map(
        body,
        mesh=mesh,
        in_specs=(rows, rows, P(), P()) + weights + vectors,
        out_specs=(rows, rows) + weights + vectors,
        check_vma=False,
    )
```

```python
from functools import partial

import jax
import jax.numpy as jnp
from jax import lax
from jax.experimental import pallas as pl
from jax.experimental.pallas import tpu as pltpu
from jax.sharding import PartitionSpec as P

DH = 64
HALF = 1024
NORM_EPS = 1e-05
MASKED_OUT = -1e30
BF, F32 = jnp.bfloat16, jnp.float32
QB = 256


def scaled_norm(values, norm_gain, norm_shift):
    peak = jnp.max(jnp.abs(values), axis=-1, keepdims=True) + NORM_EPS
    scaled = values / peak
    centred = scaled - jnp.mean(scaled, axis=-1, keepdims=True)
    spread = jnp.mean(centred * centred, axis=-1, keepdims=True)
    return centred * lax.rsqrt(spread + NORM_EPS) * norm_gain + norm_shift


def norm_back(values, norm_gain, norm_shift, row_grad):
    result, pull = jax.vjp(scaled_norm, values, norm_gain, norm_shift)
    return pull(row_grad)


PAIR = 2 * DH


def attn_fwd_kernel(qpos_ref, qstart_ref, kpos_ref, qkv_ref, o_ref, lse_ref):
    first = pl.multiple_of(pl.program_id(0) * QB, QB)
    kpos = kpos_ref[...]
    allowed = (kpos <= qpos_ref[...]) & (kpos >= qstart_ref[...])
    bias = jnp.where(allowed, 0.0, MASKED_OUT)
    lane = lax.broadcasted_iota(jnp.int32, (1, PAIR), 1)
    wide = lax.broadcasted_iota(jnp.int32, lse_ref.shape, 1)
    stats = jnp.zeros(lse_ref.shape, F32)
    for pair in range(o_ref.shape[1] // PAIR):
        at = 3 * pair * PAIR
        query = qkv_ref[pl.ds(first, QB), at:at + PAIR]
        key, value = qkv_ref[:, at + PAIR:at + 2 * PAIR], qkv_ref[:, at + 2 * PAIR:at + 3 * PAIR]
        total = jnp.zeros(query.shape, F32)
        for side in range(2):
            mine = (lane >= side * DH) & (lane < (side + 1) * DH)
            part = jnp.where(mine, query * 0.125, 0.0).astype(BF)
            score = lax.dot_general(part, key, (((1,), (1,)), ((), ())), preferred_element_type=F32) + bias
            peak = jnp.max(score, axis=-1, keepdims=True)
            expo = jnp.exp(score - peak)
            norm = jnp.sum(expo, axis=-1, keepdims=True)
            prob = (expo * (1.0 / norm)).astype(BF)
            total += jnp.dot(prob, jnp.where(mine, value, jnp.zeros_like(value)), preferred_element_type=F32)
            stats = jnp.where(wide == pair * 2 + side, peak + jnp.log(norm), stats)
        o_ref[:, pair * PAIR:(pair + 1) * PAIR] = total.astype(BF)
    lse_ref[...] = stats


def attn_forward(qpos, qstart, kpos, qkv):
    rows, width = qkv.shape[0], qkv.shape[1] // 3
    col = pl.BlockSpec((QB, 1), lambda i: (i, 0))
    full = pl.BlockSpec(qkv.shape, lambda i: (0, 0))
    return pl.pallas_call(
        attn_fwd_kernel,
        grid=(rows // QB,),
        in_specs=[col, col, pl.BlockSpec((1, rows), lambda i: (0, 0)), full],
        out_specs=[pl.BlockSpec((QB, width), lambda i: (i, 0)), pl.BlockSpec((QB, 128), lambda i: (i, 0))],
        out_shape=[jax.ShapeDtypeStruct((rows, width), BF), jax.ShapeDtypeStruct((rows, 128), F32)],
        cost_estimate=pl.CostEstimate(flops=4 * rows * rows * width, bytes_accessed=8 * rows * width, transcendentals=rows * rows * width // DH),
        compiler_params=pltpu.CompilerParams(vmem_limit_bytes=48 << 20),
        name="attn_fwd",
    )(qpos, qstart, kpos, qkv)


def attn_bwd_kernel(qpos_ref, qstart_ref, kpos_ref, lse_ref, g_ref, qkv_ref, d_ref, dk_acc, dv_acc):
    step = pl.program_id(0)
    first = pl.multiple_of(step * QB, QB)

    @pl.when(step == 0)
    def _():
        dk_acc[...] = jnp.zeros_like(dk_acc)
        dv_acc[...] = jnp.zeros_like(dv_acc)

    kpos = kpos_ref[...]
    allowed = (kpos <= qpos_ref[...]) & (kpos >= qstart_ref[...])
    bias = jnp.where(allowed, 0.0, MASKED_OUT)
    lane = lax.broadcasted_iota(jnp.int32, (1, PAIR), 1)
    for pair in range(g_ref.shape[1] // PAIR):
        at = 3 * pair * PAIR
        query = qkv_ref[pl.ds(first, QB), at:at + PAIR]
        key, value = qkv_ref[:, at + PAIR:at + 2 * PAIR], qkv_ref[:, at + 2 * PAIR:at + 3 * PAIR]
        cols = slice(pair * PAIR, (pair + 1) * PAIR)
        grad = g_ref[:, cols]
        dq = jnp.zeros(query.shape, F32)
        dk = jnp.zeros(key.shape, F32)
        dv = jnp.zeros(key.shape, F32)
        for side in range(2):
            mine = (lane >= side * DH) & (lane < (side + 1) * DH)
            part = jnp.where(mine, query * 0.125, 0.0).astype(BF)
            gpart = jnp.where(mine, grad, jnp.zeros_like(grad))
            score = lax.dot_general(part, key, (((1,), (1,)), ((), ())), preferred_element_type=F32) + bias
            index = pair * 2 + side
            prob = jnp.exp(score - lse_ref[:, index:index + 1])
            gprob = lax.dot_general(gpart, value, (((1,), (1,)), ((), ())), preferred_element_type=F32)
            inner = jnp.sum(prob * gprob, axis=-1, keepdims=True)
            gscore = (prob * (gprob - inner)).astype(BF)
            dq += jnp.dot(gscore, jnp.where(mine, key, jnp.zeros_like(key)), preferred_element_type=F32)
            dk += lax.dot_general(gscore, part, (((0,), (0,)), ((), ())), preferred_element_type=F32)
            dv += lax.dot_general(prob.astype(BF), gpart, (((0,), (0,)), ((), ())), preferred_element_type=F32)
        d_ref[pl.ds(first, QB), at:at + PAIR] = (dq * 0.125).astype(BF)
        dk_acc[:, cols] += dk
        dv_acc[:, cols] += dv

    @pl.when(step == pl.num_programs(0) - 1)
    def _():
        for pair in range(g_ref.shape[1] // PAIR):
            at = 3 * pair * PAIR
            cols = slice(pair * PAIR, (pair + 1) * PAIR)
            d_ref[:, at + PAIR:at + 2 * PAIR] = dk_acc[:, cols].astype(BF)
            d_ref[:, at + 2 * PAIR:at + 3 * PAIR] = dv_acc[:, cols].astype(BF)


def attn_backward(qpos, qstart, kpos, lse, grad, qkv):
    rows, width = grad.shape
    col = pl.BlockSpec((QB, 1), lambda i: (i, 0))
    full = pl.BlockSpec(qkv.shape, lambda i: (0, 0))
    return pl.pallas_call(
        attn_bwd_kernel,
        grid=(rows // QB,),
        in_specs=[col, col, pl.BlockSpec((1, rows), lambda i: (0, 0)), pl.BlockSpec((QB, 128), lambda i: (i, 0)),
                  pl.BlockSpec((QB, width), lambda i: (i, 0)), full],
        out_specs=full,
        out_shape=jax.ShapeDtypeStruct(qkv.shape, BF),
        scratch_shapes=[pltpu.VMEM((rows, width), F32), pltpu.VMEM((rows, width), F32)],
        cost_estimate=pl.CostEstimate(flops=10 * rows * rows * width, bytes_accessed=14 * rows * width, transcendentals=rows * rows * width // DH),
        compiler_params=pltpu.CompilerParams(vmem_limit_bytes=48 << 20),
        name="attn_bwd",
    )(qpos, qstart, kpos, lse, grad, qkv)


def swap_dp(x, bit):
    n = lax.axis_size("dp")
    return lax.ppermute(x, "dp", [(i, i ^ bit) for i in range(n)])


def turn(x, shift):
    n = lax.axis_size("tensor")
    return lax.ppermute(x, "tensor", [(i, (i + shift) % n) for i in range(n)])


def chip_bits():
    n = lax.axis_size("dp")
    return [1 << b for b in range(1, n.bit_length() - 1)]


def core_pair(mine, other):
    core = lax.axis_index("dp") % 2
    return jnp.where(core == 0, jnp.stack([mine, other]), jnp.stack([other, mine]))


def gather_weights(mine, other):
    pair = core_pair(mine, swap_dp(other, 1)).reshape(2 * mine.shape[0], mine.shape[1])
    lanes = lax.axis_size("tensor")
    column = jnp.stack([pair] + [turn(pair, k) for k in range(1, lanes)])
    bits = chip_bits()
    if len(bits) == 2:
        low, high = bits
        first, second = swap_dp(column, low), swap_dp(column, high)
        mid = lanes // 2
        far = jnp.concatenate([swap_dp(first[:mid], high), swap_dp(second[mid:], low)])
        return {0: column, low: first, high: second, low | high: far}
    blocks = {0: column}
    for bit in bits:
        got = swap_dp(jnp.stack([blocks[m] for m in sorted(blocks)]), bit)
        blocks.update({m | bit: got[i] for i, m in enumerate(sorted(blocks))})
    return blocks


def weight_of(blocks, start, width):
    out = []
    for mask in sorted(blocks):
        part = blocks[mask][:, :, start:start + width]
        out.append(jnp.concatenate([part[k] for k in range(part.shape[0])], axis=1))
    return jnp.concatenate(out, axis=0)


def scatter_grads(parts):
    lanes = lax.axis_size("tensor")
    bits = chip_bits()
    count = 1 << len(bits)
    feats = parts[0].shape[0]
    per = feats // count

    def block(mask_index, k):
        cut = []
        for p in parts:
            w = p.shape[1] // lanes
            cut.append(p[mask_index * per:(mask_index + 1) * per, k * w:(k + 1) * w])
        return jnp.concatenate(cut, axis=1) if len(cut) > 1 else cut[0]

    def col(mask_index, ks):
        return jnp.stack([block(mask_index, k) for k in ks])

    if len(bits) == 2:
        low, high = bits
        mid = lanes // 2
        ka, kb = list(range(mid)), list(range(mid, lanes))
        sent_a = jnp.stack([col(1, ka), col(3, ka)]).astype(BF)
        sent_b = jnp.stack([col(2, kb), col(3, kb)]).astype(BF)
        got_a, got_b = swap_dp(sent_a, low), swap_dp(sent_b, high)
        pass_a = (col(2, ka) + got_a[1].astype(F32)).astype(BF)
        pass_b = (col(1, kb) + got_b[1].astype(F32)).astype(BF)
        end_a, end_b = swap_dp(pass_a, high), swap_dp(pass_b, low)
        keep_a = col(0, ka) + got_a[0].astype(F32) + end_a.astype(F32)
        keep_b = col(0, kb) + got_b[0].astype(F32) + end_b.astype(F32)
        total = [keep_a[i] for i in range(mid)] + [keep_b[i] for i in range(lanes - mid)]
    else:
        sums = {m: col(m, range(lanes)) for m in range(count)}
        for level in reversed(range(len(bits))):
            keys = [m for m in sorted(sums) if m >> level & 1]
            got = swap_dp(jnp.stack([sums[m] for m in keys]).astype(BF), bits[level])
            sums = {m ^ (1 << level): sums[m ^ (1 << level)] + got[i].astype(F32) for i, m in enumerate(keys)}
        total = [sums[0][k] for k in range(lanes)]
    own = total[0]
    for k in range(1, lanes):
        own = own + turn(total[k].astype(BF), -k).astype(F32)
    rows = own.shape[0] // 2
    core = lax.axis_index("dp") % 2
    mine = lax.dynamic_slice_in_dim(own, core * rows, rows, 0)
    other = lax.dynamic_slice_in_dim(own, (1 - core) * rows, rows, 0)
    return core_pair(mine, swap_dp(other.astype(BF), 1).astype(F32))


def deal_perms(n_dp):
    near, far = [], []
    for chip in range(n_dp // 2):
        for c in range(2):
            for j in range(4):
                source = (chip * 2 + c) * 4 + j
                near.append((source, (chip * 2 + j % 2) * 4 + 2 * c + j // 2))
                far.append((source, (chip * 2 + j % 2) * 4 + 2 * c + 1 - j // 2))
    return near, far


MESH = pl.DeviceIdType.MESH
LANES = 4
ANY = pl.BlockSpec(memory_space=pl.ANY)
IN_VMEM = pl.BlockSpec(memory_space=pltpu.VMEM)


def meet(dp, lane, n_dp):
    barrier = pltpu.get_barrier_semaphore()
    count = 0
    for d in range(1, n_dp):
        pl.semaphore_signal(barrier, inc=1, device_id=(dp ^ d, lane), device_id_type=MESH)
        count += 1
    for k in range(1, LANES):
        for c in range(2):
            pl.semaphore_signal(barrier, inc=1, device_id=(dp ^ c, lax.rem(lane + k, LANES)), device_id_type=MESH)
            count += 1
    pl.semaphore_wait(barrier, count)


def deal_route(dp, lane):
    chip, core = dp // 2, dp % 2
    spot = chip * 2 + lane % 2
    return (spot, 2 * core + lane // 2), (spot, 2 * core + 1 - lane // 2)


def home_route(dp, lane):
    chip, core = dp // 2, dp % 2
    pack, half = lane // 2, lane % 2
    return (chip * 2 + pack, core + 2 * half), (chip * 2 + pack, core + 2 * (1 - half))


def send(src, dst, send_sem, recv_sem, device):
    return pltpu.make_async_remote_copy(src_ref=src, dst_ref=dst, send_sem=send_sem, recv_sem=recv_sem, device_id=device, device_id_type=MESH)


def gather_kernel(widths, own, other, small, tok, cot, *rest):
    mats, (near_t, far_t, near_c, far_c, small_out), rest = rest[:4], rest[4:9], rest[9:]
    moved_t, moved_c, loc, s_c, r_c, s_z, r_z, s_p, r_p, s_d, r_d, s_t, r_t, s_b, r_b = rest
    dp, lane = lax.axis_index("dp"), lax.axis_index("tensor")
    n_dp = 8
    core = dp % 2
    wd = own.shape[0]
    up = lax.rem(lane + 1, LANES)
    meet(dp, lane, n_dp)
    block = tok.shape[0] // n_dp
    started, deals = [], []
    for i, (src, dst) in enumerate(((tok, moved_t), (cot, moved_c))):
        here = pl.ds(pl.multiple_of(dp * block, block), block)
        keep = pltpu.make_async_copy(src.at[here], dst.at[here], loc.at[i])
        keep.start()
        copies = []
        for d in range(1, n_dp):
            there = pl.ds(pl.multiple_of((dp ^ d) * block, block), block)
            copies.append(send(src.at[there], dst.at[here], s_t.at[i, d], r_t.at[i, d], (dp ^ d, lane)))
        deals.append((keep, copies))
    feat = pl.ds(pl.multiple_of(core * wd, wd), wd)
    at, locals_, firsts = 0, [], []
    for g, w in enumerate(widths):
        dst = mats[g].at[feat, 0:w]
        locals_.append(pltpu.make_async_copy(own.at[:, at:at + w], dst, loc.at[2 + g]))
        firsts.append(send(other.at[:, at:at + w], dst, s_c.at[g], r_c.at[g], (dp ^ 1, lane)))
        locals_[-1].start()
        firsts[-1].start()
        at += w
    for c in deals[0][1]:
        c.start()
    smalls = []
    for k in range(1, LANES):
        rows = small.shape[0]
        smalls.append(send(small, small_out.at[k * rows:(k + 1) * rows], s_b.at[k], r_b.at[k], (dp, lax.rem(lane + k, LANES))))
        smalls[-1].start()
    keep_small = pltpu.make_async_copy(small, small_out.at[0:small.shape[0]], loc.at[6])
    keep_small.start()

    def turn_copy(g, t):
        w = widths[g]
        return send(mats[g].at[0:2 * wd, t * w:(t + 1) * w], mats[g].at[0:2 * wd, (t + 1) * w:(t + 2) * w], s_z.at[g, t], r_z.at[g, t], (dp, up))

    def plane_copy(g, k, side):
        w = widths[g]
        return send(mats[g].at[0:2 * wd, k * w:(k + 1) * w], mats[g].at[2 * wd * side:2 * wd * (side + 1), k * w:(k + 1) * w],
                    s_p.at[g, k, side - 1], r_p.at[g, k, side - 1], (dp ^ (2 * side), lane))

    def far_copy(g, k):
        w = widths[g]
        side, via = (1, 2) if k < LANES // 2 else (2, 1)
        return send(mats[g].at[2 * wd * side:2 * wd * (side + 1), k * w:(k + 1) * w], mats[g].at[6 * wd:8 * wd, k * w:(k + 1) * w],
                    s_d.at[g, k], r_d.at[g, k], (dp ^ (2 * via), lane))

    n_g = len(widths)
    turns = [[turn_copy(g, t) for t in range(LANES - 1)] for g in range(n_g)]
    planes = [[[plane_copy(g, k, side) for side in (1, 2)] for k in range(LANES)] for g in range(n_g)]
    fars = [[far_copy(g, k) for k in range(LANES)] for g in range(n_g)]

    def ready(g, k):
        if k < LANES - 1:
            turns[g][k].start()
        for c in planes[g][k]:
            c.start()

    for g in range(n_g):
        locals_[g].wait()
        firsts[g].wait_recv()
        ready(g, 0)
    near, far = deal_route(dp, lane)
    is_self = (near[0] == dp) & (near[1] == lane)

    def deal_on(i, moved, near_out, far_out):
        deals[i][0].wait()
        for c in deals[i][1]:
            c.wait_recv()
        stay = pltpu.make_async_copy(moved, near_out, loc.at[7 + i])
        go = send(moved, near_out, s_t.at[i, 0], r_t.at[i, 0], near)
        off = send(moved, far_out, s_b.at[0 if i == 0 else 4], r_b.at[0 if i == 0 else 4], far)
        pl.when(is_self)(lambda: stay.start())
        pl.when(jnp.logical_not(is_self))(lambda: go.start())
        off.start()
        return stay, go, off

    routes = [deal_on(0, moved_t, near_t, far_t)]
    for t in range(LANES - 1):
        for g in range(n_g):
            turns[g][t].wait_recv()
            ready(g, t + 1)
        if t == 0:
            for c in deals[1][1]:
                c.start()
    for g in range(n_g):
        for k in range(LANES):
            side = 0 if k < LANES // 2 else 1
            planes[g][k][side].wait_recv()
            fars[g][k].start()
    routes.append(deal_on(1, moved_c, near_c, far_c))
    for g in range(n_g):
        for k in range(LANES):
            planes[g][k][1 if k < LANES // 2 else 0].wait_recv()
            fars[g][k].wait_recv()
    for stay, go, off in routes:
        pl.when(is_self)(lambda: stay.wait())
        pl.when(jnp.logical_not(is_self))(lambda: go.wait())
        off.wait()
    keep_small.wait()
    for c in smalls:
        c.wait()
    for i in range(2):
        for c in deals[i][1]:
            c.wait_send()
    for g in range(n_g):
        firsts[g].wait_send()
        for c in turns[g]:
            c.wait_send()
        for k in range(LANES):
            for c in planes[g][k]:
                c.wait_send()
            fars[g][k].wait_send()


def gather_call(widths, own, other, small, tok, cot):
    d = own.shape[0] * 8
    n = len(widths)
    tile = jax.ShapeDtypeStruct(tok.shape, BF)
    dma = pltpu.SemaphoreType.DMA
    return pl.pallas_call(
        partial(gather_kernel, widths),
        in_specs=[IN_VMEM, IN_VMEM, IN_VMEM, IN_VMEM, IN_VMEM],
        out_specs=[ANY] * n + [IN_VMEM] * 5,
        out_shape=[jax.ShapeDtypeStruct((d, LANES * w), BF) for w in widths] + [tile] * 4
        + [jax.ShapeDtypeStruct((LANES * small.shape[0], small.shape[1]), F32)],
        scratch_shapes=[pltpu.VMEM(tok.shape, BF), pltpu.VMEM(tok.shape, BF), dma((10,)), dma((n,)), dma((n,)), dma((n, 3)), dma((n, 3)),
                        dma((n, 4, 2)), dma((n, 4, 2)), dma((n, 4)), dma((n, 4)), dma((2, 8)), dma((2, 8)), dma((5,)), dma((5,))],
        compiler_params=pltpu.CompilerParams(collective_id=1, has_side_effects=True, vmem_limit_bytes=48 << 20),
        name="gather",
    )(own, other, small, tok, cot)


def scatter_kernel(widths, mask_ref, vec_ref, res, grd, *rest):
    n_g = len(widths)
    grads, rest = rest[:n_g], rest[n_g:]
    outs, (out_res, out_grd, out_vec), rest = rest[:n_g], rest[n_g:n_g + 3], rest[n_g + 3:]
    first, second, summed, turned, third, done = (rest[i * n_g:(i + 1) * n_g] for i in range(6))
    rest = rest[6 * n_g:]
    near_in, far_in, moved, vec_in, loc, s_1, r_1, s_2, r_2, s_z, r_z, s_c, r_c, s_t, r_t, s_v, r_v = rest
    dp, lane = lax.axis_index("dp"), lax.axis_index("tensor")
    n_dp = 8
    core = dp % 2
    per = grads[0].shape[0] // 4
    wd = per // 2
    meet(dp, lane, n_dp)
    near, far = home_route(dp, lane)
    is_self = (near[0] == dp) & (near[1] == lane)
    backs = []
    for i, src in enumerate((res, grd)):
        stay = pltpu.make_async_copy(src, near_in.at[i], loc.at[i])
        go = send(src, near_in.at[i], s_t.at[i, 0], r_t.at[i, 0], near)
        off = send(src, far_in.at[i], s_t.at[i, 8], r_t.at[i, 8], far)
        pl.when(is_self)(lambda: stay.start())
        pl.when(jnp.logical_not(is_self))(lambda: go.start())
        off.start()
        backs.append((stay, go, off))

    def first_copies(g, k):
        w = widths[g]
        cols = slice(k * w, (k + 1) * w)
        side = 1 if k < 2 else 2
        return [send(grads[g].at[q * per:(q + 1) * per, cols], first[g].at[i, :, cols], s_1.at[g, k, i], r_1.at[g, k, i], (dp ^ (2 * side), lane))
                for i, q in enumerate((3, side))]

    def second_copy(g, k):
        w = widths[g]
        cols = slice(k * w, (k + 1) * w)
        side = 2 if k < 2 else 1
        return send(summed[g].at[:, cols], second[g].at[:, cols], s_2.at[g, k], r_2.at[g, k], (dp ^ (2 * side), lane))

    def turn_copy(g, k):
        w = widths[g]
        return send(summed[g].at[:, k * w:(k + 1) * w], turned[g].at[k], s_z.at[g, k], r_z.at[g, k], (dp, lax.rem(lane + LANES - k, LANES)))

    firsts = [[first_copies(g, k) for k in range(LANES)] for g in range(n_g)]
    seconds = [[second_copy(g, k) for k in range(LANES)] for g in range(n_g)]
    turns = [[None] + [turn_copy(g, k) for k in range(1, LANES)] for g in range(n_g)]
    for g in range(n_g):
        for i in range(2):
            for k in range(LANES):
                firsts[g][k][i].start()

    out_vec[...] = vec_ref[...]
    partners = [(dp ^ 1, lane), (dp ^ 2, lane), (dp ^ 4, lane), (dp, lane ^ 1), (dp, lane ^ 2)]

    def vec_round(i):
        c = send(out_vec, vec_in.at[i], s_v.at[i], r_v.at[i], partners[i])
        c.start()
        return c

    def vec_end(c, i):
        c.wait()
        out_vec[...] = out_vec[...] + vec_in[i]

    rounds = 0
    for g in range(n_g):
        for k in range(LANES):
            w = widths[g]
            cols = slice(k * w, (k + 1) * w)
            firsts[g][k][0].wait_recv()
            q = 2 if k < 2 else 1
            summed[g][:, cols] = (grads[g][q * per:(q + 1) * per, cols].astype(F32) + first[g][0, :, cols].astype(F32)).astype(BF)
            seconds[g][k].start()
        if rounds < 5:
            c = vec_round(rounds)
            vec_end(c, rounds)
            rounds += 1
    while rounds < 5:
        c = vec_round(rounds)
        vec_end(c, rounds)
        rounds += 1

    block = res.shape[0] // n_dp
    here = pl.ds(pl.multiple_of(dp * block, block), block)
    deals = []
    for i, dst in enumerate((out_res, out_grd)):
        stay, go, off = backs[i]
        pl.when(is_self)(lambda: stay.wait())
        pl.when(jnp.logical_not(is_self))(lambda: go.wait())
        off.wait()
        moved[i] = jnp.where(mask_ref[...] > 0, near_in[i].astype(F32), far_in[i].astype(F32)).astype(BF)
        keep = pltpu.make_async_copy(moved.at[i, here], dst.at[here], loc.at[2 + i])
        keep.start()
        copies = []
        for d in range(1, n_dp):
            there = pl.ds(pl.multiple_of((dp ^ d) * block, block), block)
            copies.append(send(moved.at[i, there], dst.at[here], s_t.at[i, d], r_t.at[i, d], (dp ^ d, lane)))
            copies[-1].start()
        deals.append((keep, copies))

    for g in range(n_g):
        for k in (1, 2, 3, 0):
            w = widths[g]
            cols = slice(k * w, (k + 1) * w)
            firsts[g][k][1].wait_recv()
            seconds[g][k].wait()
            summed[g][:, cols] = (grads[g][0:per, cols].astype(F32) + first[g][1, :, cols].astype(F32) + second[g][:, cols].astype(F32)).astype(BF)
            if k:
                turns[g][k].start()

    lasts = []
    for g in range(n_g):
        w = widths[g]
        for k in range(1, LANES):
            turns[g][k].wait_recv()
        done[g][...] = summed[g][:, 0:w].astype(F32) + turned[g][1].astype(F32) + turned[g][2].astype(F32) + turned[g][3].astype(F32)
        mine = pl.ds(pl.multiple_of(core * wd, wd), wd)
        other = pl.ds(pl.multiple_of((1 - core) * wd, wd), wd)
        third[g][0] = done[g][other, :].astype(BF)
        outs[g][core] = done[g][mine, :]
        c = send(third[g].at[0], third[g].at[1], s_c.at[g], r_c.at[g], (dp ^ 1, lane))
        c.start()
        lasts.append(c)
    for g in range(n_g):
        lasts[g].wait()
        outs[g][1 - core] = third[g][1].astype(F32)
    for keep, copies in deals:
        keep.wait()
        for c in copies:
            c.wait()
    for g in range(n_g):
        for k in range(LANES):
            for c in firsts[g][k]:
                c.wait_send()
            if k:
                turns[g][k].wait_send()


def scatter_call(widths, mask, vec, res, grd, grads):
    n = len(widths)
    d = grads[0].shape[0]
    per = d // 4
    dma = pltpu.SemaphoreType.DMA
    vm = pltpu.VMEM
    tile = jax.ShapeDtypeStruct(res.shape, BF)
    scratch = (
        [vm((2, per, LANES * w), BF) for w in widths] + [vm((per, LANES * w), BF) for w in widths] + [vm((per, LANES * w), BF) for w in widths]
        + [vm((LANES, per, w), BF) for w in widths] + [vm((2, per // 2, w), BF) for w in widths] + [vm((per, w), F32) for w in widths]
        + [vm((2,) + res.shape, BF)] * 3 + [vm((5,) + vec.shape, F32)]
        + [dma((4,)), dma((n, 4, 2)), dma((n, 4, 2)), dma((n, 4)), dma((n, 4)), dma((n, 4)), dma((n, 4)), dma((n,)), dma((n,)),
           dma((2, 9)), dma((2, 9)), dma((5,)), dma((5,))]
    )
    return pl.pallas_call(
        partial(scatter_kernel, widths),
        in_specs=[IN_VMEM] * (4 + n),
        out_specs=[IN_VMEM] * (n + 3),
        out_shape=[jax.ShapeDtypeStruct((2, per // 2, w), F32) for w in widths] + [tile, tile, jax.ShapeDtypeStruct(vec.shape, F32)],
        scratch_shapes=scratch,
        compiler_params=pltpu.CompilerParams(collective_id=2, has_side_effects=True, vmem_limit_bytes=62 << 20),
        name="scatter",
    )(mask, vec, res, grd, *grads)


def feature_turn(x):
    n = lax.axis_size("dp") // 2
    chip = lax.axis_index("dp") // 2
    lead = x.shape[:-1]
    width = x.shape[-1] // n
    bits = n.bit_length() - 1
    y = x.reshape(lead + (2,) * bits + (width,))
    for b in range(bits):
        axis = len(lead) + bits - 1 - b
        y = jnp.where((chip >> b) & 1 == 1, jnp.flip(y, axis), y)
    return y.reshape(x.shape)


def body(tokens, cotangent, lengths, deal, w_qkv, w_o, w_1, w_2, b_qv, b_o, b_1, b_2, ln_gain, ln_bias):
    n_dp, lanes = lax.axis_size("dp"), lax.axis_size("tensor")
    dp, lane = lax.axis_index("dp"), lax.axis_index("tensor")
    core, chip = dp % 2, dp // 2
    rows = tokens.shape[0]
    both = ("dp", "tensor")
    near, far = deal_perms(n_dp)
    back_near, back_far = [(b, a) for a, b in near], [(b, a) for a, b in far]

    per = lengths.shape[0] // n_dp

    def pack_ends(pack):
        picked = lax.dynamic_slice_in_dim(deal, pack * per, per)
        lookup = picked[:, None] == jnp.arange(lengths.shape[0], dtype=jnp.int32)[None, :]
        lens = jnp.sum(jnp.where(lookup, lengths[None, :], 0), axis=1)
        ends = jnp.sum(jnp.where(jnp.arange(per)[:, None] >= jnp.arange(per)[None, :], lens[None, :], 0), axis=1)
        return ends, ends - lens, jnp.sum(jnp.where(lens == HALF, ends - lens, 0))

    half = lane % 2
    ends, starts, cut = pack_ends(chip * 2 + lane // 2)
    _, _, cut_home = pack_ends(dp)
    index = jnp.arange(rows, dtype=jnp.int32)
    slots = jnp.concatenate([core * rows + index, (1 - core) * rows + index])
    place = jnp.where(slots >= cut, slots + HALF * half, slots + HALF * (1 - half))
    seg_start = jnp.max(jnp.where(place[:, None] >= starts[None, :], starts[None, :], 0), axis=1)
    qpos, qstart, kpos = place[:, None], seg_start[:, None], place[None, :]
    keep = ((core * rows + index) >= cut)[:, None]
    keep_home = (((lane % 2) * rows + index) >= cut_home)[:, None]

    def deal_in(x):
        moved = lax.all_to_all(x, "dp", split_axis=0, concat_axis=0, tiled=True)
        return jnp.where(keep, lax.ppermute(moved, both, near), lax.ppermute(moved, both, far))

    def deal_out(x):
        moved = jnp.where(keep_home, lax.ppermute(x, both, back_near), lax.ppermute(x, both, back_far))
        return lax.all_to_all(moved, "dp", split_axis=0, concat_axis=0, tiled=True)

    def halves(x):
        w = x.shape[-1] // 2
        return (lax.dynamic_slice_in_dim(x, core * w, w, x.ndim - 1), lax.dynamic_slice_in_dim(x, (1 - core) * w, w, x.ndim - 1))

    qm, qo = halves(w_qkv)
    om, oo = halves(w_o.T)
    um, uo = halves(w_1)
    dm, do = halves(w_2.T)
    own = jnp.concatenate([qm[0], qm[1], qm[2], om, um, dm], axis=1)
    other = jnp.concatenate([qo[0], qo[1], qo[2], oo, uo, do], axis=1)
    hw, fw = om.shape[1], um.shape[1]
    widths = (3 * hw, hw, fw, fw)
    small = jnp.concatenate([halves(b_qv[0:1])[0], halves(b_qv[1:2])[0], halves(b_1[None])[0]], axis=1)
    small = jnp.concatenate([small, jnp.zeros((7, small.shape[1]), F32)])
    order = (lane - jnp.arange(lanes)) % lanes
    kernels = n_dp == 8 and lanes == LANES
    if kernels:
        wq, wo, w1, w2, near_t, far_t, near_c, far_c, smalls = gather_call(widths, own, other, small, tokens, cotangent)
        smalls = smalls[::8]
        dealt_tok, dealt_cot = jnp.where(keep, near_t, far_t), jnp.where(keep, near_c, far_c)
    else:
        blocks = gather_weights(own, other)
        wq, wo, w1, w2 = (weight_of(blocks, sum(widths[:i]), w) for i, w in enumerate(widths))
        dealt_tok, dealt_cot = deal_in(tokens), deal_in(cotangent)
        smalls = jnp.take(lax.all_gather(small[0], "tensor"), order, axis=0)
    bias_q, bias_v, bias_1 = smalls[:, :hw], smalls[:, hw:2 * hw], smalls[:, 2 * hw:].reshape(-1)
    bias_qkv = jnp.concatenate([bias_q, jnp.zeros_like(bias_q), bias_v], axis=1).reshape(-1)
    gain, shift = feature_turn(ln_gain), feature_turn(ln_bias)
    bias_o, bias_2 = feature_turn(b_o[None])[0], feature_turn(b_2[None])[0]

    def join(x):
        return jnp.concatenate([x, swap_dp(x, 1)], axis=0)

    def fold(x):
        return x[:rows] + swap_dp(x[rows:].astype(BF), 1).astype(F32)

    mm = partial(jnp.dot, preferred_element_type=F32)
    mm_t = lambda a, b: lax.dot_general(a, b, (((1,), (1,)), ((), ())), preferred_element_type=F32)
    mm_g = lambda a, b: lax.dot_general(a, b, (((0,), (0,)), ((), ())), preferred_element_type=F32)
    hidden = feature_turn(dealt_tok).astype(F32)
    normed_in = join(scaled_norm(hidden, gain[0], shift[0]).astype(BF))
    qkv = (mm(normed_in, wq) + bias_qkv).astype(BF)
    heads_out, lse = attn_forward(qpos, qstart, kpos, qkv)
    attn_out = fold(mm_t(heads_out, wo)) + bias_o
    first_sum = hidden + scaled_norm(attn_out, gain[1], shift[1])
    normed_mid = join(scaled_norm(first_sum, gain[2], shift[2]).astype(BF))
    pre_act = mm(normed_mid, w1) + bias_1
    act = jax.nn.gelu(pre_act, approximate=False).astype(BF)
    ffn_out = fold(mm_t(act, w2)) + bias_2
    result = feature_turn((first_sum + scaled_norm(ffn_out, gain[3], shift[3])).astype(BF))

    grad_result = feature_turn(dealt_cot).astype(F32)
    grad_ffn, gain_3, shift_3 = norm_back(ffn_out, gain[3], shift[3], grad_result)
    grad_ffn_low = grad_ffn.astype(BF)
    bias_2_grad = jnp.sum(grad_ffn_low.astype(F32), axis=0)
    grad_ffn_full = join(grad_ffn_low)
    grad_act = mm(grad_ffn_full, w2)
    down_part = mm_g(grad_ffn_full, act).astype(BF)
    _, gelu_pull = jax.vjp(partial(jax.nn.gelu, approximate=False), pre_act)
    grad_pre = gelu_pull(grad_act)[0].astype(BF)
    bias_1_grad = jnp.sum(grad_pre.astype(F32), axis=0)
    grad_mid = fold(mm_t(grad_pre, w1))
    up_part = mm_g(normed_mid, grad_pre).astype(BF)
    grad_first_part, gain_2, shift_2 = norm_back(first_sum, gain[2], shift[2], grad_mid)
    grad_first = grad_result + grad_first_part
    grad_attn, gain_1, shift_1 = norm_back(attn_out, gain[1], shift[1], grad_first)
    grad_attn_low = grad_attn.astype(BF)
    bias_o_grad = jnp.sum(grad_attn_low.astype(F32), axis=0)
    grad_attn_full = join(grad_attn_low)
    grad_heads = mm(grad_attn_full, wo).astype(BF)
    out_part = mm_g(grad_attn_full, heads_out).astype(BF)
    grad_qkv = attn_backward(qpos, qstart, kpos, lse, grad_heads, qkv)
    bias_qkv_grad = jnp.sum(grad_qkv.astype(F32), axis=0).reshape(lanes, 3, hw)
    grad_in = fold(mm_t(grad_qkv, wq))
    qkv_part = mm_g(normed_in, grad_qkv).astype(BF)
    grad_hidden_part, gain_0, shift_0 = norm_back(hidden, gain[0], shift[0], grad_in)
    grad_hidden = feature_turn((grad_first + grad_hidden_part).astype(BF))

    def by_lane(x):
        x = jnp.take(x.reshape(lanes, -1), order, axis=0)
        both_halves = jnp.stack([jnp.where(core == 0, x, 0.0), jnp.where(core == 1, x, 0.0)], axis=1)
        return both_halves.reshape(-1)

    d = tokens.shape[1]
    stack = jnp.stack([gain_0, gain_1, gain_2, gain_3, shift_0, shift_1, shift_2, shift_3, bias_o_grad, bias_2_grad])
    vector = jnp.concatenate([feature_turn(stack).reshape(-1), by_lane(bias_qkv_grad[:, 0]), by_lane(bias_qkv_grad[:, 2]), by_lane(bias_1_grad)])
    parts = [qkv_part, out_part, up_part, down_part]
    if kernels:
        mask = jnp.broadcast_to(keep_home.astype(jnp.int32), (rows, 128))[:, :1]
        *shards, output, input_grad, vector = scatter_call(widths, mask, vector.reshape(-1, 128), result, grad_hidden, parts)
        vector = vector.reshape(-1)
    else:
        output, input_grad = deal_out(result), deal_out(grad_hidden)
        vector = lax.psum(vector, both)
        shards = [scatter_grads([p.astype(F32)]) for p in parts]
    gain_total, shift_total = vector[:4 * d].reshape(4, d), vector[4 * d:8 * d].reshape(4, d)
    bias_o_total, bias_2_total = vector[8 * d:9 * d], vector[9 * d:10 * d]
    mine = lambda x: lax.dynamic_slice_in_dim(x.reshape(lanes, -1), lane, 1, 0)[0]
    bias_qv_total = jnp.stack([mine(vector[10 * d:11 * d]), mine(vector[11 * d:12 * d])])
    bias_1_total = mine(vector[12 * d:])

    spread = lambda x: jnp.concatenate([x[0], x[1]], axis=-1)
    qkv_grad, out_grad, up_grad, down_grad = shards
    qkv_out = jnp.stack([spread(qkv_grad[:, :, i * hw:(i + 1) * hw]) for i in range(3)])
    return (
        output, input_grad, qkv_out, spread(out_grad).T, spread(up_grad), spread(down_grad).T,
        bias_qv_total, bias_o_total, bias_1_total, bias_2_total, gain_total, shift_total,
    )


def solution(mesh):
    rows = P(("dp", "tensor"), None)
    weights = (P(None, "dp", "tensor"), P("tensor", "dp"), P("dp", "tensor"), P("tensor", "dp"))
    vectors = (P(None, "tensor"), P(), P("tensor"), P(), P(), P())
    return jax.shard_map(
        body,
        mesh=mesh,
        in_specs=(rows, rows, P(), P()) + weights + vectors,
        out_specs=(rows, rows) + weights + vectors,
        check_vma=False,
    )
```

```python
from functools import partial

import jax
import jax.numpy as jnp
from jax import lax
from jax.experimental import pallas as pl
from jax.experimental.pallas import tpu as pltpu
from jax.sharding import PartitionSpec as P

DH = 64
HALF = 1024
NORM_EPS = 1e-05
MASKED_OUT = -1e30
BF, F32 = jnp.bfloat16, jnp.float32
QB = 256


def scaled_norm(values, norm_gain, norm_shift):
    peak = jnp.max(jnp.abs(values), axis=-1, keepdims=True) + NORM_EPS
    scaled = values / peak
    centred = scaled - jnp.mean(scaled, axis=-1, keepdims=True)
    spread = jnp.mean(centred * centred, axis=-1, keepdims=True)
    return centred * lax.rsqrt(spread + NORM_EPS) * norm_gain + norm_shift


def norm_back(values, norm_gain, norm_shift, row_grad):
    result, pull = jax.vjp(scaled_norm, values, norm_gain, norm_shift)
    return pull(row_grad)


PAIR = 2 * DH


def attn_fwd_kernel(qpos_ref, qstart_ref, kpos_ref, qkv_ref, o_ref, lse_ref):
    first = pl.multiple_of(pl.program_id(0) * QB, QB)
    kpos = kpos_ref[...]
    allowed = (kpos <= qpos_ref[...]) & (kpos >= qstart_ref[...])
    bias = jnp.where(allowed, 0.0, MASKED_OUT)
    lane = lax.broadcasted_iota(jnp.int32, (1, PAIR), 1)
    wide = lax.broadcasted_iota(jnp.int32, lse_ref.shape, 1)
    stats = jnp.zeros(lse_ref.shape, F32)
    for pair in range(o_ref.shape[1] // PAIR):
        at = 3 * pair * PAIR
        query = qkv_ref[pl.ds(first, QB), at:at + PAIR]
        key, value = qkv_ref[:, at + PAIR:at + 2 * PAIR], qkv_ref[:, at + 2 * PAIR:at + 3 * PAIR]
        total = jnp.zeros(query.shape, F32)
        for side in range(2):
            mine = (lane >= side * DH) & (lane < (side + 1) * DH)
            part = jnp.where(mine, query * 0.125, 0.0).astype(BF)
            score = lax.dot_general(part, key, (((1,), (1,)), ((), ())), preferred_element_type=F32) + bias
            peak = jnp.max(score, axis=-1, keepdims=True)
            expo = jnp.exp(score - peak)
            norm = jnp.sum(expo, axis=-1, keepdims=True)
            prob = (expo * (1.0 / norm)).astype(BF)
            total += jnp.dot(prob, jnp.where(mine, value, jnp.zeros_like(value)), preferred_element_type=F32)
            stats = jnp.where(wide == pair * 2 + side, peak + jnp.log(norm), stats)
        o_ref[:, pair * PAIR:(pair + 1) * PAIR] = total.astype(BF)
    lse_ref[...] = stats


def attn_forward(qpos, qstart, kpos, qkv):
    rows, width = qkv.shape[0], qkv.shape[1] // 3
    col = pl.BlockSpec((QB, 1), lambda i: (i, 0))
    full = pl.BlockSpec(qkv.shape, lambda i: (0, 0))
    return pl.pallas_call(
        attn_fwd_kernel,
        grid=(rows // QB,),
        in_specs=[col, col, pl.BlockSpec((1, rows), lambda i: (0, 0)), full],
        out_specs=[pl.BlockSpec((QB, width), lambda i: (i, 0)), pl.BlockSpec((QB, 128), lambda i: (i, 0))],
        out_shape=[jax.ShapeDtypeStruct((rows, width), BF), jax.ShapeDtypeStruct((rows, 128), F32)],
        cost_estimate=pl.CostEstimate(flops=4 * rows * rows * width, bytes_accessed=8 * rows * width, transcendentals=rows * rows * width // DH),
        compiler_params=pltpu.CompilerParams(vmem_limit_bytes=48 << 20),
        name="attn_fwd",
    )(qpos, qstart, kpos, qkv)


def attn_bwd_kernel(qpos_ref, qstart_ref, kpos_ref, lse_ref, g_ref, qkv_ref, d_ref, dk_acc, dv_acc):
    step = pl.program_id(0)
    first = pl.multiple_of(step * QB, QB)

    @pl.when(step == 0)
    def _():
        dk_acc[...] = jnp.zeros_like(dk_acc)
        dv_acc[...] = jnp.zeros_like(dv_acc)

    kpos = kpos_ref[...]
    allowed = (kpos <= qpos_ref[...]) & (kpos >= qstart_ref[...])
    bias = jnp.where(allowed, 0.0, MASKED_OUT)
    lane = lax.broadcasted_iota(jnp.int32, (1, PAIR), 1)
    for pair in range(g_ref.shape[1] // PAIR):
        at = 3 * pair * PAIR
        query = qkv_ref[pl.ds(first, QB), at:at + PAIR]
        key, value = qkv_ref[:, at + PAIR:at + 2 * PAIR], qkv_ref[:, at + 2 * PAIR:at + 3 * PAIR]
        cols = slice(pair * PAIR, (pair + 1) * PAIR)
        grad = g_ref[:, cols]
        dq = jnp.zeros(query.shape, F32)
        dk = jnp.zeros(key.shape, F32)
        dv = jnp.zeros(key.shape, F32)
        for side in range(2):
            mine = (lane >= side * DH) & (lane < (side + 1) * DH)
            part = jnp.where(mine, query * 0.125, 0.0).astype(BF)
            gpart = jnp.where(mine, grad, jnp.zeros_like(grad))
            score = lax.dot_general(part, key, (((1,), (1,)), ((), ())), preferred_element_type=F32) + bias
            index = pair * 2 + side
            prob = jnp.exp(score - lse_ref[:, index:index + 1])
            gprob = lax.dot_general(gpart, value, (((1,), (1,)), ((), ())), preferred_element_type=F32)
            inner = jnp.sum(prob * gprob, axis=-1, keepdims=True)
            gscore = (prob * (gprob - inner)).astype(BF)
            dq += jnp.dot(gscore, jnp.where(mine, key, jnp.zeros_like(key)), preferred_element_type=F32)
            dk += lax.dot_general(gscore, part, (((0,), (0,)), ((), ())), preferred_element_type=F32)
            dv += lax.dot_general(prob.astype(BF), gpart, (((0,), (0,)), ((), ())), preferred_element_type=F32)
        d_ref[pl.ds(first, QB), at:at + PAIR] = (dq * 0.125).astype(BF)
        dk_acc[:, cols] += dk
        dv_acc[:, cols] += dv

    @pl.when(step == pl.num_programs(0) - 1)
    def _():
        for pair in range(g_ref.shape[1] // PAIR):
            at = 3 * pair * PAIR
            cols = slice(pair * PAIR, (pair + 1) * PAIR)
            d_ref[:, at + PAIR:at + 2 * PAIR] = dk_acc[:, cols].astype(BF)
            d_ref[:, at + 2 * PAIR:at + 3 * PAIR] = dv_acc[:, cols].astype(BF)


def attn_backward(qpos, qstart, kpos, lse, grad, qkv):
    rows, width = grad.shape
    col = pl.BlockSpec((QB, 1), lambda i: (i, 0))
    full = pl.BlockSpec(qkv.shape, lambda i: (0, 0))
    return pl.pallas_call(
        attn_bwd_kernel,
        grid=(rows // QB,),
        in_specs=[col, col, pl.BlockSpec((1, rows), lambda i: (0, 0)), pl.BlockSpec((QB, 128), lambda i: (i, 0)),
                  pl.BlockSpec((QB, width), lambda i: (i, 0)), full],
        out_specs=full,
        out_shape=jax.ShapeDtypeStruct(qkv.shape, BF),
        scratch_shapes=[pltpu.VMEM((rows, width), F32), pltpu.VMEM((rows, width), F32)],
        cost_estimate=pl.CostEstimate(flops=10 * rows * rows * width, bytes_accessed=14 * rows * width, transcendentals=rows * rows * width // DH),
        compiler_params=pltpu.CompilerParams(vmem_limit_bytes=48 << 20),
        name="attn_bwd",
    )(qpos, qstart, kpos, lse, grad, qkv)


def swap_dp(x, bit):
    n = lax.axis_size("dp")
    return lax.ppermute(x, "dp", [(i, i ^ bit) for i in range(n)])


def turn(x, shift):
    n = lax.axis_size("tensor")
    return lax.ppermute(x, "tensor", [(i, (i + shift) % n) for i in range(n)])


def chip_bits():
    n = lax.axis_size("dp")
    return [1 << b for b in range(1, n.bit_length() - 1)]


def core_pair(mine, other):
    core = lax.axis_index("dp") % 2
    return jnp.where(core == 0, jnp.stack([mine, other]), jnp.stack([other, mine]))


def gather_weights(mine, other):
    pair = core_pair(mine, swap_dp(other, 1)).reshape(2 * mine.shape[0], mine.shape[1])
    lanes = lax.axis_size("tensor")
    column = jnp.stack([pair] + [turn(pair, k) for k in range(1, lanes)])
    bits = chip_bits()
    if len(bits) == 2:
        low, high = bits
        first, second = swap_dp(column, low), swap_dp(column, high)
        mid = lanes // 2
        far = jnp.concatenate([swap_dp(first[:mid], high), swap_dp(second[mid:], low)])
        return {0: column, low: first, high: second, low | high: far}
    blocks = {0: column}
    for bit in bits:
        got = swap_dp(jnp.stack([blocks[m] for m in sorted(blocks)]), bit)
        blocks.update({m | bit: got[i] for i, m in enumerate(sorted(blocks))})
    return blocks


def weight_of(blocks, start, width):
    out = []
    for mask in sorted(blocks):
        part = blocks[mask][:, :, start:start + width]
        out.append(jnp.concatenate([part[k] for k in range(part.shape[0])], axis=1))
    return jnp.concatenate(out, axis=0)


def scatter_grads(parts):
    lanes = lax.axis_size("tensor")
    bits = chip_bits()
    count = 1 << len(bits)
    feats = parts[0].shape[0]
    per = feats // count

    def block(mask_index, k):
        cut = []
        for p in parts:
            w = p.shape[1] // lanes
            cut.append(p[mask_index * per:(mask_index + 1) * per, k * w:(k + 1) * w])
        return jnp.concatenate(cut, axis=1) if len(cut) > 1 else cut[0]

    def col(mask_index, ks):
        return jnp.stack([block(mask_index, k) for k in ks])

    if len(bits) == 2:
        low, high = bits
        mid = lanes // 2
        ka, kb = list(range(mid)), list(range(mid, lanes))
        sent_a = jnp.stack([col(1, ka), col(3, ka)]).astype(BF)
        sent_b = jnp.stack([col(2, kb), col(3, kb)]).astype(BF)
        got_a, got_b = swap_dp(sent_a, low), swap_dp(sent_b, high)
        pass_a = (col(2, ka) + got_a[1].astype(F32)).astype(BF)
        pass_b = (col(1, kb) + got_b[1].astype(F32)).astype(BF)
        end_a, end_b = swap_dp(pass_a, high), swap_dp(pass_b, low)
        keep_a = col(0, ka) + got_a[0].astype(F32) + end_a.astype(F32)
        keep_b = col(0, kb) + got_b[0].astype(F32) + end_b.astype(F32)
        total = [keep_a[i] for i in range(mid)] + [keep_b[i] for i in range(lanes - mid)]
    else:
        sums = {m: col(m, range(lanes)) for m in range(count)}
        for level in reversed(range(len(bits))):
            keys = [m for m in sorted(sums) if m >> level & 1]
            got = swap_dp(jnp.stack([sums[m] for m in keys]).astype(BF), bits[level])
            sums = {m ^ (1 << level): sums[m ^ (1 << level)] + got[i].astype(F32) for i, m in enumerate(keys)}
        total = [sums[0][k] for k in range(lanes)]
    own = total[0]
    for k in range(1, lanes):
        own = own + turn(total[k].astype(BF), -k).astype(F32)
    rows = own.shape[0] // 2
    core = lax.axis_index("dp") % 2
    mine = lax.dynamic_slice_in_dim(own, core * rows, rows, 0)
    other = lax.dynamic_slice_in_dim(own, (1 - core) * rows, rows, 0)
    return core_pair(mine, swap_dp(other.astype(BF), 1).astype(F32))


def deal_perms(n_dp):
    near, far = [], []
    for chip in range(n_dp // 2):
        for c in range(2):
            for j in range(4):
                source = (chip * 2 + c) * 4 + j
                near.append((source, (chip * 2 + j % 2) * 4 + 2 * c + j // 2))
                far.append((source, (chip * 2 + j % 2) * 4 + 2 * c + 1 - j // 2))
    return near, far


MESH = pl.DeviceIdType.MESH
LANES = 4
ANY = pl.BlockSpec(memory_space=pl.ANY)
IN_VMEM = pl.BlockSpec(memory_space=pltpu.VMEM)


def meet(dp, lane, n_dp):
    barrier = pltpu.get_barrier_semaphore()
    count = 0
    for d in range(1, n_dp):
        pl.semaphore_signal(barrier, inc=1, device_id=(dp ^ d, lane), device_id_type=MESH)
        count += 1
    for k in range(1, LANES):
        for c in range(2):
            pl.semaphore_signal(barrier, inc=1, device_id=(dp ^ c, lax.rem(lane + k, LANES)), device_id_type=MESH)
            count += 1
    pl.semaphore_wait(barrier, count)


def deal_route(dp, lane):
    chip, core = dp // 2, dp % 2
    spot = chip * 2 + lane % 2
    return (spot, 2 * core + lane // 2), (spot, 2 * core + 1 - lane // 2)


def home_route(dp, lane):
    chip, core = dp // 2, dp % 2
    pack, half = lane // 2, lane % 2
    return (chip * 2 + pack, core + 2 * half), (chip * 2 + pack, core + 2 * (1 - half))


def send(src, dst, send_sem, recv_sem, device):
    return pltpu.make_async_remote_copy(src_ref=src, dst_ref=dst, send_sem=send_sem, recv_sem=recv_sem, device_id=device, device_id_type=MESH)


DEAL_CUTS = 4


def norm_parts(x):
    peak = jnp.max(jnp.abs(x), axis=-1, keepdims=True) + NORM_EPS
    u = x * (1.0 / peak)
    c = u - jnp.mean(u, axis=-1, keepdims=True)
    return c, lax.rsqrt(jnp.mean(c * c, axis=-1, keepdims=True) + NORM_EPS)


def norm_rows(x, gain, shift):
    c, r = norm_parts(x)
    return c * r * gain + shift


def dot_t(a, b):
    return lax.dot_general(a, b, (((1,), (1,)), ((), ())), preferred_element_type=F32)


class Sems:
    def __init__(self, ref):
        self.ref, self.used = ref, 0

    def take(self, count=1):
        self.used += count
        return self.used - count


FWD_SEMS = 320


def forward_kernel(widths, own, other, small, tok, cot, keep, qpos, qstart, kpos, vec, *rest):
    outs, rest = rest[:18], rest[18:]
    (wq_o, wo_o, w1_o, w2_o, h_o, xin_o, qkv_o, heads_o, lse_o, attn_o, first_o, xmid_o, act_o, dg_o, ffn_o, res_o, grd_o, small_o) = outs
    (wq, wo, w1, w2, moved, cand, h, xin, qkv, heads, lse, part, sbuf, rbuf, first, xmid, act, dg, stage, small_in, sem_ref) = rest
    mats = (wq, wo, w1, w2)
    sems = Sems(sem_ref)
    dp, lane = lax.axis_index("dp"), lax.axis_index("tensor")
    n_dp = 8
    core, chip = dp % 2, dp // 2
    rows, d = tok.shape
    wd = own.shape[0]
    quarter = d // 4
    up = lax.rem(lane + 1, LANES)
    n_g = len(widths)
    mate = (dp ^ 1, lane)
    ends = []

    def local(src, dst):
        c = pltpu.make_async_copy(src, dst, sem_ref.at[sems.take()])
        return c

    def remote(src, dst, device):
        s, r = sems.take(), sems.take()
        c = send(src, dst, sem_ref.at[s], sem_ref.at[r], device)
        ends.append(c.wait_send)
        return c

    meet(dp, lane, n_dp)
    block = rows // n_dp
    here = pl.ds(pl.multiple_of(dp * block, block), block)
    deals = []
    for i, src in enumerate((tok, cot)):
        stay = local(src.at[here], moved.at[i, here])
        copies = []
        for k in range(1, n_dp):
            there = pl.ds(pl.multiple_of((dp ^ k) * block, block), block)
            copies.append(remote(src.at[there], moved.at[i, here], (dp ^ k, lane)))
        deals.append((stay, copies))

    def deal_start(i):
        deals[i][0].start()
        for c in deals[i][1]:
            c.start()

    deal_start(0)
    feat = pl.ds(pl.multiple_of(core * wd, wd), wd)
    at, stays, pairs = 0, [], []
    for g, w in enumerate(widths):
        dst = mats[g].at[feat, 0:w]
        stays.append(local(own.at[:, at:at + w], dst))
        pairs.append(remote(other.at[:, at:at + w], dst, mate))
        stays[g].start()
        pairs[g].start()
        at += w
    n_s = small.shape[0]
    smalls = [remote(small, small_in.at[k], (dp, lax.rem(lane + k, LANES))) for k in range(1, LANES)]
    for c in smalls:
        c.start()
    small_in[0] = small[...]

    def area(g, q, k):
        w = widths[g]
        return mats[g].at[2 * wd * q:2 * wd * (q + 1), k * w:(k + 1) * w]

    turns = [[remote(area(g, 0, t), area(g, 0, t + 1), (dp, up)) for t in range(LANES - 1)] for g in range(n_g)]
    planes = [[[remote(area(g, 0, k), area(g, side, k), (dp ^ (2 * side), lane)) for side in (1, 2)] for k in range(LANES)] for g in range(n_g)]
    fars = []
    for g in range(n_g):
        fars.append([])
        for k in range(LANES):
            side, via = (1, 2) if k < LANES // 2 else (2, 1)
            fars[g].append(remote(area(g, side, k), area(g, 3, k), (dp ^ (2 * via), lane)))

    def ready(g, k):
        if k < LANES - 1:
            turns[g][k].start()
        for c in planes[g][k]:
            c.start()

    def pair_in(g):
        stays[g].wait()
        pairs[g].wait_recv()
        ready(g, 0)

    def turn_in(g, t):
        turns[g][t].wait_recv()
        ready(g, t + 1)

    def far_go(g, k):
        planes[g][k][0 if k < LANES // 2 else 1].wait_recv()
        fars[g][k].start()

    def all_in(g):
        for k in range(LANES):
            planes[g][k][1 if k < LANES // 2 else 0].wait_recv()
            fars[g][k].wait_recv()

    pack = lane // 2
    spot = chip * 2 + lane % 2
    to_near, to_far = (spot, core + 1), (spot, 3 * core)
    same_side = lane // 2 == core
    slot = jnp.where(same_side, 1, 0)
    is_self = (lane == 3 * core) & (spot == dp)
    to_far_remote = same_side & jnp.logical_not(is_self)
    is_near = lane == pack + 1
    cut = rows // DEAL_CUTS

    class Route:
        def __init__(self, i):
            a0, b0, f0 = sems.take(DEAL_CUTS), sems.take(DEAL_CUTS), sems.take(DEAL_CUTS)
            got = sems.take(2 * DEAL_CUTS)
            self.got = got
            self.near, self.far, self.self_, self.hand, self.wait0, self.wait1 = [], [], [], [], [], []
            for n in range(DEAL_CUTS):
                rs = slice(n * cut, (n + 1) * cut)
                src = moved.at[i, rs]
                self.near.append(send(src, cand.at[i, slot, rs], sem_ref.at[a0 + n], sem_ref.at[got + n * 2 + slot], to_near))
                self.far.append(send(src, cand.at[i, 0, rs], sem_ref.at[b0 + n], sem_ref.at[got + n * 2], to_far))
                self.self_.append(pltpu.make_async_copy(src, cand.at[i, 0, rs], sem_ref.at[got + n * 2]))
                self.hand.append(send(cand.at[i, 0, rs], cand.at[i, 1, rs], sem_ref.at[f0 + n], sem_ref.at[got + n * 2 + 1], (dp, 3 * pack)))
                self.wait0.append(send(src, cand.at[i, 0, rs], sem_ref.at[b0 + n], sem_ref.at[got + n * 2], to_far))
                self.wait1.append(send(src, cand.at[i, 1, rs], sem_ref.at[b0 + n], sem_ref.at[got + n * 2 + 1], to_far))

        def start(self):
            for n in range(DEAL_CUTS):
                self.near[n].start()
                pl.when(to_far_remote)(lambda: self.far[n].start())
                pl.when(is_self)(lambda: self.self_[n].start())

        def arrive(self, n):
            pl.when(is_self)(lambda: self.self_[n].wait())
            pl.when(jnp.logical_not(is_self))(lambda: self.wait0[n].wait_recv())
            pl.when(is_near)(lambda: self.hand[n].start())
            self.wait1[n].wait_recv()

        def finish(self):
            for n in range(DEAL_CUTS):
                self.near[n].wait_send()
                pl.when(to_far_remote)(lambda: self.far[n].wait_send())
                pl.when(is_near)(lambda: self.hand[n].wait_send())

    routes = [Route(0), Route(1)]

    def deal_on(i):
        deals[i][0].wait()
        for c in deals[i][1]:
            c.wait_recv()
        routes[i].start()

    def choose(i, n):
        rs = slice(n * cut, (n + 1) * cut)
        on = keep[rs, :] > 0
        parts = []
        for q in range(4):
            cols = pl.ds(pl.multiple_of((chip ^ q) * quarter, quarter), quarter)
            parts.append(jnp.where(on, cand[i, 0, rs, cols].astype(F32), cand[i, 1, rs, cols].astype(F32)))
        return jnp.concatenate(parts, axis=1)

    out_copies = []

    def put(src, dst):
        c = local(src, dst)
        c.start()
        out_copies.append(c)

    pair_in(0)
    turn_in(0, 0)
    turn_in(0, 1)
    deal_on(0)
    turn_in(0, 2)
    pending = []
    for g in (1, 2, 3):
        pending.append((lambda g=g: pair_in(g)))
    for t in range(LANES - 1):
        for g in (1, 2, 3):
            pending.append((lambda g=g, t=t: turn_in(g, t)))
    for g in (1, 2, 3):
        for k in range(LANES):
            pending.append((lambda g=g, k=k: far_go(g, k)))
    pending.append(lambda: deal_start(1))
    pending.append(lambda: deal_on(1))

    def pump(count):
        for _ in range(min(count, len(pending))):
            pending.pop(0)()

    for k in range(LANES):
        far_go(0, k)
    pump(3)
    joins = []

    def join_send(x, n, size):
        c = remote(x.at[n * size:(n + 1) * size], x.at[rows + n * size:rows + (n + 1) * size], mate)
        c.start()
        joins.append(c)

    gains = lambda i: vec[i:i + 1, :]
    for n in range(DEAL_CUTS):
        rs = slice(n * cut, (n + 1) * cut)
        routes[0].arrive(n)
        x = choose(0, n)
        h[rs, :] = x.astype(BF)
        xin[rs, :] = norm_rows(x, gains(0), gains(4)).astype(BF)
        join_send(xin, n, cut)
    pump(3)
    for c in smalls:
        c.wait_recv()
    all_in(0)
    for c in joins:
        c.wait_recv()
    put(wq, wq_o)
    put(h, h_o)
    put(xin, xin_o)
    w = widths[0]
    third = w // 3
    for k in range(LANES):
        cols = slice(k * w, (k + 1) * w)
        row = small_in[k, 0:1, :]
        bias = jnp.concatenate([row[:, 0:third], jnp.zeros((1, third), F32), row[:, third:2 * third]], axis=1)

        def project(r, carry, cols=cols, bias=bias):
            rs = pl.ds(pl.multiple_of(r * QB, QB), QB)
            qkv[rs, cols] = (jnp.dot(xin[rs, :], wq[:, cols], preferred_element_type=F32) + bias).astype(BF)
            return carry

        lax.fori_loop(0, 2 * rows // QB, project, 0)
    put(qkv, qkv_o)
    pump(3)

    def attend(i, carry):
        begin = pl.multiple_of(i * QB, QB)
        rs = pl.ds(begin, QB)
        allowed = (kpos[...] <= qpos[rs, :]) & (kpos[...] >= qstart[rs, :])
        bias = jnp.where(allowed, 0.0, MASKED_OUT)
        attn_block(rs, bias, qkv, heads, lse)
        return carry

    for i in range(2):
        lax.fori_loop(2 * i, 2 * i + 2, attend, 0)
        pump(6)
    put(heads, heads_o)
    put(lse, lse_o)
    all_in(1)
    put(wo, wo_o)

    def fold(x, w_ref, which):
        copies = []
        per = 2
        size = rows // per
        for n in range(per):
            rs = slice(rows + n * size, rows + (n + 1) * size)
            sbuf[which, n * size:(n + 1) * size] = dot_t(x[rs, :], w_ref[...]).astype(BF)
            c = remote(sbuf.at[which, n * size:(n + 1) * size], rbuf.at[which, n * size:(n + 1) * size], mate)
            c.start()
            copies.append(c)
        for n in range(per):
            rs = slice(n * size, (n + 1) * size)
            part[rs, :] = dot_t(x[rs, :], w_ref[...])
        return copies

    copies = fold(heads, wo, 0)
    pump(3)
    joins.clear()
    size = rows // 2
    for n in range(2):
        copies[n].wait_recv()

        def middle(m, carry, n=n):
            rs = pl.ds(pl.multiple_of(n * size + m * cut, cut), cut)
            y = part[rs, :] + rbuf[0, rs].astype(F32) + gains(8)
            part[rs, :] = y
            f = h[rs, :].astype(F32) + norm_rows(y, gains(1), gains(5))
            first[rs, :] = f
            xmid[rs, :] = norm_rows(f, gains(2), gains(6)).astype(BF)
            return carry

        lax.fori_loop(0, size // cut, middle, 0)
        join_send(xmid, n, size)
    attn_put = local(part, attn_o)
    attn_put.start()
    put(first, first_o)
    pump(4)
    all_in(2)
    put(w1, w1_o)
    for c in joins:
        c.wait_recv()
    put(xmid, xmid_o)
    w = widths[2]
    for k in range(LANES):
        cols = slice(k * w, (k + 1) * w)
        bias = small_in[k, 0:1, 2 * third:2 * third + w]

        def hidden_units(r, carry, cols=cols, bias=bias):
            rs = pl.ds(pl.multiple_of(r * QB, QB), QB)
            pre = jnp.dot(xmid[rs, :], w1[:, cols], preferred_element_type=F32) + bias
            cdf = 0.5 + 0.5 * lax.erf(pre * 0.7071067811865476)
            act[rs, cols] = (pre * cdf).astype(BF)
            dg[rs, cols] = (cdf + pre * (0.3989422804014327 * jnp.exp(-0.5 * pre * pre))).astype(BF)
            return carry

        lax.fori_loop(0, 2 * rows // QB, hidden_units, 0)
        pump(3)
    pump(len(pending))
    put(act, act_o)
    put(dg, dg_o)
    all_in(3)
    put(w2, w2_o)
    attn_put.wait()
    copies = fold(act, w2, 1)
    for n in range(DEAL_CUTS):
        routes[1].arrive(n)
        rs = slice(n * cut, (n + 1) * cut)
        stage[1, rs] = choose(1, n).astype(BF)
    put(stage.at[1], grd_o)
    for n in range(2):
        copies[n].wait_recv()

        def last(m, carry, n=n):
            rs = pl.ds(pl.multiple_of(n * size + m * cut, cut), cut)
            y = part[rs, :] + rbuf[1, rs].astype(F32) + gains(9)
            part[rs, :] = y
            out = first[rs, :] + norm_rows(y, gains(3), gains(7))
            for q in range(4):
                cols = pl.ds(pl.multiple_of((chip ^ q) * quarter, quarter), quarter)
                stage[0, rs, cols] = out[:, q * quarter:(q + 1) * quarter].astype(BF)
            return carry

        lax.fori_loop(0, size // cut, last, 0)
    put(part, ffn_o)
    put(stage.at[0], res_o)
    put(small_in, small_o)
    for c in out_copies:
        c.wait()
    for i in range(2):
        routes[i].finish()
    for wait in ends:
        wait()


def attn_block(rs, bias, qkv, heads, lse):
    lane = lax.broadcasted_iota(jnp.int32, (1, PAIR), 1)
    wide = lax.broadcasted_iota(jnp.int32, (QB, 128), 1)
    stats = jnp.zeros((QB, 128), F32)
    for pair in range(heads.shape[1] // PAIR):
        at = 3 * pair * PAIR
        query = qkv[rs, at:at + PAIR]
        key, value = qkv[:, at + PAIR:at + 2 * PAIR], qkv[:, at + 2 * PAIR:at + 3 * PAIR]
        total = jnp.zeros(query.shape, F32)
        for side in range(2):
            mine = (lane >= side * DH) & (lane < (side + 1) * DH)
            piece = jnp.where(mine, query * 0.125, 0.0).astype(BF)
            score = dot_t(piece, key) + bias
            peak = jnp.max(score, axis=-1, keepdims=True)
            expo = jnp.exp(score - peak)
            norm = jnp.sum(expo, axis=-1, keepdims=True)
            prob = (expo * (1.0 / norm)).astype(BF)
            total += jnp.dot(prob, jnp.where(mine, value, jnp.zeros_like(value)), preferred_element_type=F32)
            stats = jnp.where(wide == pair * 2 + side, peak + jnp.log(norm), stats)
        heads[rs, pair * PAIR:(pair + 1) * PAIR] = total.astype(BF)
    lse[rs, :] = stats


def forward_call(widths, own, other, small, tok, cot, keep, qpos, qstart, kpos, vec):
    rows, d = tok.shape
    both = 2 * rows
    vm = pltpu.VMEM
    hidden = LANES * widths[2]
    mats = [(d, LANES * w) for w in widths]
    shape = jax.ShapeDtypeStruct
    out = [shape(m, BF) for m in mats] + [
        shape((rows, d), BF), shape((both, d), BF), shape((both, LANES * widths[0]), BF), shape((both, LANES * widths[1]), BF), shape((both, 128), F32),
        shape((rows, d), F32), shape((rows, d), F32), shape((both, d), BF), shape((both, hidden), BF), shape((both, hidden), BF),
        shape((rows, d), F32), shape((rows, d), BF), shape((rows, d), BF), shape((LANES,) + small.shape, F32)]
    scratch = [vm(m, BF) for m in mats] + [
        vm((2, rows, d), BF), vm((2, 2, rows, d), BF), vm((rows, d), BF), vm((both, d), BF), vm((both, LANES * widths[0]), BF),
        vm((both, LANES * widths[1]), BF), vm((both, 128), F32), vm((rows, d), F32), vm((2, rows, d), BF), vm((2, rows, d), BF),
        vm((rows, d), F32), vm((both, d), BF), vm((both, hidden), BF), vm((both, hidden), BF), vm((2, rows, d), BF),
        vm((LANES,) + small.shape, F32), pltpu.SemaphoreType.DMA((FWD_SEMS,))]
    return pl.pallas_call(
        partial(forward_kernel, widths),
        in_specs=[IN_VMEM] * 10,
        out_specs=[ANY] * len(out),
        out_shape=out,
        scratch_shapes=scratch,
        compiler_params=pltpu.CompilerParams(collective_id=1, has_side_effects=True, vmem_limit_bytes=67043328),
        name="forward",
    )(own, other, small, tok, cot, keep, qpos, qstart, kpos, vec)


def scatter_kernel(widths, mask_ref, vec_ref, res, grd, *rest):
    n_g = len(widths)
    grads, rest = rest[:n_g], rest[n_g:]
    outs, (out_res, out_grd, out_vec), rest = rest[:n_g], rest[n_g:n_g + 3], rest[n_g + 3:]
    first, second, summed, turned, third, done = (rest[i * n_g:(i + 1) * n_g] for i in range(6))
    rest = rest[6 * n_g:]
    near_in, far_in, moved, vec_in, loc, s_1, r_1, s_2, r_2, s_z, r_z, s_c, r_c, s_t, r_t, s_v, r_v = rest
    dp, lane = lax.axis_index("dp"), lax.axis_index("tensor")
    n_dp = 8
    core = dp % 2
    per = grads[0].shape[0] // 4
    wd = per // 2
    meet(dp, lane, n_dp)
    near, far = home_route(dp, lane)
    is_self = (near[0] == dp) & (near[1] == lane)
    backs = []
    for i, src in enumerate((res, grd)):
        stay = pltpu.make_async_copy(src, near_in.at[i], loc.at[i])
        go = send(src, near_in.at[i], s_t.at[i, 0], r_t.at[i, 0], near)
        off = send(src, far_in.at[i], s_t.at[i, 8], r_t.at[i, 8], far)
        pl.when(is_self)(lambda: stay.start())
        pl.when(jnp.logical_not(is_self))(lambda: go.start())
        off.start()
        backs.append((stay, go, off))

    def first_copies(g, k):
        w = widths[g]
        cols = slice(k * w, (k + 1) * w)
        side = 1 if k < 2 else 2
        return [send(grads[g].at[q * per:(q + 1) * per, cols], first[g].at[i, :, cols], s_1.at[g, k, i], r_1.at[g, k, i], (dp ^ (2 * side), lane))
                for i, q in enumerate((3, side))]

    def second_copy(g, k):
        w = widths[g]
        cols = slice(k * w, (k + 1) * w)
        side = 2 if k < 2 else 1
        return send(summed[g].at[:, cols], second[g].at[:, cols], s_2.at[g, k], r_2.at[g, k], (dp ^ (2 * side), lane))

    def turn_copy(g, k):
        w = widths[g]
        return send(summed[g].at[:, k * w:(k + 1) * w], turned[g].at[k], s_z.at[g, k], r_z.at[g, k], (dp, lax.rem(lane + LANES - k, LANES)))

    firsts = [[first_copies(g, k) for k in range(LANES)] for g in range(n_g)]
    seconds = [[second_copy(g, k) for k in range(LANES)] for g in range(n_g)]
    turns = [[None] + [turn_copy(g, k) for k in range(1, LANES)] for g in range(n_g)]
    for g in range(n_g):
        for i in range(2):
            for k in range(LANES):
                firsts[g][k][i].start()

    out_vec[...] = vec_ref[...]
    partners = [(dp ^ 1, lane), (dp ^ 2, lane), (dp ^ 4, lane), (dp, lane ^ 1), (dp, lane ^ 2)]

    def vec_round(i):
        c = send(out_vec, vec_in.at[i], s_v.at[i], r_v.at[i], partners[i])
        c.start()
        return c

    def vec_end(c, i):
        c.wait()
        out_vec[...] = out_vec[...] + vec_in[i]

    rounds = 0
    for g in range(n_g):
        for k in range(LANES):
            w = widths[g]
            cols = slice(k * w, (k + 1) * w)
            firsts[g][k][0].wait_recv()
            q = 2 if k < 2 else 1
            summed[g][:, cols] = (grads[g][q * per:(q + 1) * per, cols].astype(F32) + first[g][0, :, cols].astype(F32)).astype(BF)
            seconds[g][k].start()
        if rounds < 5:
            c = vec_round(rounds)
            vec_end(c, rounds)
            rounds += 1
    while rounds < 5:
        c = vec_round(rounds)
        vec_end(c, rounds)
        rounds += 1

    block = res.shape[0] // n_dp
    here = pl.ds(pl.multiple_of(dp * block, block), block)
    deals = []
    for i, dst in enumerate((out_res, out_grd)):
        stay, go, off = backs[i]
        pl.when(is_self)(lambda: stay.wait())
        pl.when(jnp.logical_not(is_self))(lambda: go.wait())
        off.wait()
        moved[i] = jnp.where(mask_ref[...] > 0, near_in[i].astype(F32), far_in[i].astype(F32)).astype(BF)
        keep = pltpu.make_async_copy(moved.at[i, here], dst.at[here], loc.at[2 + i])
        keep.start()
        copies = []
        for d in range(1, n_dp):
            there = pl.ds(pl.multiple_of((dp ^ d) * block, block), block)
            copies.append(send(moved.at[i, there], dst.at[here], s_t.at[i, d], r_t.at[i, d], (dp ^ d, lane)))
            copies[-1].start()
        deals.append((keep, copies))

    for g in range(n_g):
        for k in (1, 2, 3, 0):
            w = widths[g]
            cols = slice(k * w, (k + 1) * w)
            firsts[g][k][1].wait_recv()
            seconds[g][k].wait()
            summed[g][:, cols] = (grads[g][0:per, cols].astype(F32) + first[g][1, :, cols].astype(F32) + second[g][:, cols].astype(F32)).astype(BF)
            if k:
                turns[g][k].start()

    lasts = []
    for g in range(n_g):
        w = widths[g]
        for k in range(1, LANES):
            turns[g][k].wait_recv()
        done[g][...] = summed[g][:, 0:w].astype(F32) + turned[g][1].astype(F32) + turned[g][2].astype(F32) + turned[g][3].astype(F32)
        mine = pl.ds(pl.multiple_of(core * wd, wd), wd)
        other = pl.ds(pl.multiple_of((1 - core) * wd, wd), wd)
        third[g][0] = done[g][other, :].astype(BF)
        outs[g][core] = done[g][mine, :]
        c = send(third[g].at[0], third[g].at[1], s_c.at[g], r_c.at[g], (dp ^ 1, lane))
        c.start()
        lasts.append(c)
    for g in range(n_g):
        lasts[g].wait()
        outs[g][1 - core] = third[g][1].astype(F32)
    for keep, copies in deals:
        keep.wait()
        for c in copies:
            c.wait()
    for g in range(n_g):
        for k in range(LANES):
            for c in firsts[g][k]:
                c.wait_send()
            if k:
                turns[g][k].wait_send()


def scatter_call(widths, mask, vec, res, grd, grads):
    n = len(widths)
    d = grads[0].shape[0]
    per = d // 4
    dma = pltpu.SemaphoreType.DMA
    vm = pltpu.VMEM
    tile = jax.ShapeDtypeStruct(res.shape, BF)
    scratch = (
        [vm((2, per, LANES * w), BF) for w in widths] + [vm((per, LANES * w), BF) for w in widths] + [vm((per, LANES * w), BF) for w in widths]
        + [vm((LANES, per, w), BF) for w in widths] + [vm((2, per // 2, w), BF) for w in widths] + [vm((per, w), F32) for w in widths]
        + [vm((2,) + res.shape, BF)] * 3 + [vm((5,) + vec.shape, F32)]
        + [dma((4,)), dma((n, 4, 2)), dma((n, 4, 2)), dma((n, 4)), dma((n, 4)), dma((n, 4)), dma((n, 4)), dma((n,)), dma((n,)),
           dma((2, 9)), dma((2, 9)), dma((5,)), dma((5,))]
    )
    return pl.pallas_call(
        partial(scatter_kernel, widths),
        in_specs=[IN_VMEM] * (4 + n),
        out_specs=[IN_VMEM] * (n + 3),
        out_shape=[jax.ShapeDtypeStruct((2, per // 2, w), F32) for w in widths] + [tile, tile, jax.ShapeDtypeStruct(vec.shape, F32)],
        scratch_shapes=scratch,
        compiler_params=pltpu.CompilerParams(collective_id=2, has_side_effects=True, vmem_limit_bytes=62 << 20),
        name="scatter",
    )(mask, vec, res, grd, *grads)


def feature_turn(x):
    n = lax.axis_size("dp") // 2
    chip = lax.axis_index("dp") // 2
    lead = x.shape[:-1]
    width = x.shape[-1] // n
    bits = n.bit_length() - 1
    y = x.reshape(lead + (2,) * bits + (width,))
    for b in range(bits):
        axis = len(lead) + bits - 1 - b
        y = jnp.where((chip >> b) & 1 == 1, jnp.flip(y, axis), y)
    return y.reshape(x.shape)


def body(tokens, cotangent, lengths, deal, w_qkv, w_o, w_1, w_2, b_qv, b_o, b_1, b_2, ln_gain, ln_bias):
    n_dp, lanes = lax.axis_size("dp"), lax.axis_size("tensor")
    dp, lane = lax.axis_index("dp"), lax.axis_index("tensor")
    core, chip = dp % 2, dp // 2
    rows = tokens.shape[0]
    both = ("dp", "tensor")
    near, far = deal_perms(n_dp)
    back_near, back_far = [(b, a) for a, b in near], [(b, a) for a, b in far]

    per = lengths.shape[0] // n_dp

    def pack_ends(pack):
        picked = lax.dynamic_slice_in_dim(deal, pack * per, per)
        lookup = picked[:, None] == jnp.arange(lengths.shape[0], dtype=jnp.int32)[None, :]
        lens = jnp.sum(jnp.where(lookup, lengths[None, :], 0), axis=1)
        ends = jnp.sum(jnp.where(jnp.arange(per)[:, None] >= jnp.arange(per)[None, :], lens[None, :], 0), axis=1)
        return ends, ends - lens, jnp.sum(jnp.where(lens == HALF, ends - lens, 0))

    half = lane % 2
    ends, starts, cut = pack_ends(chip * 2 + lane // 2)
    _, _, cut_home = pack_ends(dp)
    index = jnp.arange(rows, dtype=jnp.int32)
    slots = jnp.concatenate([core * rows + index, (1 - core) * rows + index])
    place = jnp.where(slots >= cut, slots + HALF * half, slots + HALF * (1 - half))
    seg_start = jnp.max(jnp.where(place[:, None] >= starts[None, :], starts[None, :], 0), axis=1)
    qpos, qstart, kpos = place[:, None], seg_start[:, None], place[None, :]
    keep = ((core * rows + index) >= cut)[:, None]
    keep_home = (((lane % 2) * rows + index) >= cut_home)[:, None]

    def deal_in(x):
        moved = lax.all_to_all(x, "dp", split_axis=0, concat_axis=0, tiled=True)
        return jnp.where(keep, lax.ppermute(moved, both, near), lax.ppermute(moved, both, far))

    def deal_out(x):
        moved = jnp.where(keep_home, lax.ppermute(x, both, back_near), lax.ppermute(x, both, back_far))
        return lax.all_to_all(moved, "dp", split_axis=0, concat_axis=0, tiled=True)

    def halves(x):
        w = x.shape[-1] // 2
        return (lax.dynamic_slice_in_dim(x, core * w, w, x.ndim - 1), lax.dynamic_slice_in_dim(x, (1 - core) * w, w, x.ndim - 1))

    qm, qo = halves(w_qkv)
    om, oo = halves(w_o.T)
    um, uo = halves(w_1)
    dm, do = halves(w_2.T)
    own = jnp.concatenate([qm[0], qm[1], qm[2], om, um, dm], axis=1)
    other = jnp.concatenate([qo[0], qo[1], qo[2], oo, uo, do], axis=1)
    hw, fw = om.shape[1], um.shape[1]
    widths = (3 * hw, hw, fw, fw)
    small = jnp.concatenate([halves(b_qv[0:1])[0], halves(b_qv[1:2])[0], halves(b_1[None])[0]], axis=1)
    small = jnp.concatenate([small, jnp.zeros((7, small.shape[1]), F32)])
    order = (lane - jnp.arange(lanes)) % lanes
    kernels = n_dp == 8 and lanes == LANES
    gain, shift = feature_turn(ln_gain), feature_turn(ln_bias)
    bias_o, bias_2 = feature_turn(b_o[None])[0], feature_turn(b_2[None])[0]

    def join(x):
        return jnp.concatenate([x, swap_dp(x, 1)], axis=0)

    def fold(x):
        return x[:rows] + swap_dp(x[rows:].astype(BF), 1).astype(F32)

    mm = partial(jnp.dot, preferred_element_type=F32)
    mm_t = lambda a, b: lax.dot_general(a, b, (((1,), (1,)), ((), ())), preferred_element_type=F32)
    mm_g = lambda a, b: lax.dot_general(a, b, (((0,), (0,)), ((), ())), preferred_element_type=F32)
    if kernels:
        vec = jnp.concatenate([gain, shift, bias_o[None], bias_2[None], jnp.zeros((6, tokens.shape[1]), F32)])
        (wq, wo, w1, w2, hid, normed_in, qkv, heads_out, lse, attn_out, first_sum, normed_mid, act, dgelu, ffn_out, result, dealt_cot,
         _) = forward_call(widths, own, other, small, tokens, cotangent, keep.astype(jnp.int32), qpos, qstart, kpos, vec)
        hidden = hid.astype(F32)
        grad_result = dealt_cot.astype(F32)
    else:
        blocks = gather_weights(own, other)
        wq, wo, w1, w2 = (weight_of(blocks, sum(widths[:i]), w) for i, w in enumerate(widths))
        smalls = jnp.take(lax.all_gather(small[0], "tensor"), order, axis=0)
        bias_q, bias_v, bias_1 = smalls[:, :hw], smalls[:, hw:2 * hw], smalls[:, 2 * hw:].reshape(-1)
        bias_qkv = jnp.concatenate([bias_q, jnp.zeros_like(bias_q), bias_v], axis=1).reshape(-1)
        hidden = feature_turn(deal_in(tokens)).astype(F32)
        normed_in = join(scaled_norm(hidden, gain[0], shift[0]).astype(BF))
        qkv = (mm(normed_in, wq) + bias_qkv).astype(BF)
        heads_out, lse = attn_forward(qpos, qstart, kpos, qkv)
        attn_out = fold(mm_t(heads_out, wo)) + bias_o
        first_sum = hidden + scaled_norm(attn_out, gain[1], shift[1])
        normed_mid = join(scaled_norm(first_sum, gain[2], shift[2]).astype(BF))
        pre_act = mm(normed_mid, w1) + bias_1
        cdf = 0.5 + 0.5 * lax.erf(pre_act * 0.7071067811865476)
        act = (pre_act * cdf).astype(BF)
        dgelu = (cdf + pre_act * (0.3989422804014327 * jnp.exp(-0.5 * pre_act * pre_act))).astype(BF)
        ffn_out = fold(mm_t(act, w2)) + bias_2
        result = feature_turn((first_sum + scaled_norm(ffn_out, gain[3], shift[3])).astype(BF))
        grad_result = feature_turn(deal_in(cotangent)).astype(F32)

    grad_ffn, gain_3, shift_3 = norm_back(ffn_out, gain[3], shift[3], grad_result)
    grad_ffn_low = grad_ffn.astype(BF)
    bias_2_grad = jnp.sum(grad_ffn_low.astype(F32), axis=0)
    grad_ffn_full = join(grad_ffn_low)
    grad_act = mm(grad_ffn_full, w2)
    down_part = mm_g(grad_ffn_full, act).astype(BF)
    grad_pre = (grad_act * dgelu.astype(F32)).astype(BF)
    bias_1_grad = jnp.sum(grad_pre.astype(F32), axis=0)
    grad_mid = fold(mm_t(grad_pre, w1))
    up_part = mm_g(normed_mid, grad_pre).astype(BF)
    grad_first_part, gain_2, shift_2 = norm_back(first_sum, gain[2], shift[2], grad_mid)
    grad_first = grad_result + grad_first_part
    grad_attn, gain_1, shift_1 = norm_back(attn_out, gain[1], shift[1], grad_first)
    grad_attn_low = grad_attn.astype(BF)
    bias_o_grad = jnp.sum(grad_attn_low.astype(F32), axis=0)
    grad_attn_full = join(grad_attn_low)
    grad_heads = mm(grad_attn_full, wo).astype(BF)
    out_part = mm_g(grad_attn_full, heads_out).astype(BF)
    grad_qkv = attn_backward(qpos, qstart, kpos, lse, grad_heads, qkv)
    bias_qkv_grad = jnp.sum(grad_qkv.astype(F32), axis=0).reshape(lanes, 3, hw)
    grad_in = fold(mm_t(grad_qkv, wq))
    qkv_part = mm_g(normed_in, grad_qkv).astype(BF)
    grad_hidden_part, gain_0, shift_0 = norm_back(hidden, gain[0], shift[0], grad_in)
    grad_hidden = feature_turn((grad_first + grad_hidden_part).astype(BF))

    def by_lane(x):
        x = jnp.take(x.reshape(lanes, -1), order, axis=0)
        both_halves = jnp.stack([jnp.where(core == 0, x, 0.0), jnp.where(core == 1, x, 0.0)], axis=1)
        return both_halves.reshape(-1)

    d = tokens.shape[1]
    stack = jnp.stack([gain_0, gain_1, gain_2, gain_3, shift_0, shift_1, shift_2, shift_3, bias_o_grad, bias_2_grad])
    vector = jnp.concatenate([feature_turn(stack).reshape(-1), by_lane(bias_qkv_grad[:, 0]), by_lane(bias_qkv_grad[:, 2]), by_lane(bias_1_grad)])
    parts = [qkv_part, out_part, up_part, down_part]
    if kernels:
        mask = jnp.broadcast_to(keep_home.astype(jnp.int32), (rows, 128))[:, :1]
        *shards, output, input_grad, vector = scatter_call(widths, mask, vector.reshape(-1, 128), result, grad_hidden, parts)
        vector = vector.reshape(-1)
    else:
        output, input_grad = deal_out(result), deal_out(grad_hidden)
        vector = lax.psum(vector, both)
        shards = [scatter_grads([p.astype(F32)]) for p in parts]
    gain_total, shift_total = vector[:4 * d].reshape(4, d), vector[4 * d:8 * d].reshape(4, d)
    bias_o_total, bias_2_total = vector[8 * d:9 * d], vector[9 * d:10 * d]
    mine = lambda x: lax.dynamic_slice_in_dim(x.reshape(lanes, -1), lane, 1, 0)[0]
    bias_qv_total = jnp.stack([mine(vector[10 * d:11 * d]), mine(vector[11 * d:12 * d])])
    bias_1_total = mine(vector[12 * d:])

    spread = lambda x: jnp.concatenate([x[0], x[1]], axis=-1)
    qkv_grad, out_grad, up_grad, down_grad = shards
    qkv_out = jnp.stack([spread(qkv_grad[:, :, i * hw:(i + 1) * hw]) for i in range(3)])
    return (
        output, input_grad, qkv_out, spread(out_grad).T, spread(up_grad), spread(down_grad).T,
        bias_qv_total, bias_o_total, bias_1_total, bias_2_total, gain_total, shift_total,
    )


def solution(mesh):
    rows = P(("dp", "tensor"), None)
    weights = (P(None, "dp", "tensor"), P("tensor", "dp"), P("dp", "tensor"), P("tensor", "dp"))
    vectors = (P(None, "tensor"), P(), P("tensor"), P(), P(), P())
    return jax.shard_map(
        body,
        mesh=mesh,
        in_specs=(rows, rows, P(), P()) + weights + vectors,
        out_specs=(rows, rows) + weights + vectors,
        check_vma=False,
    )
```

```python
from functools import partial

import jax
import jax.numpy as jnp
from jax import lax
from jax.experimental import pallas as pl
from jax.experimental.pallas import tpu as pltpu
from jax.sharding import PartitionSpec as P

DH = 64
HALF = 1024
NORM_EPS = 1e-05
MASKED_OUT = -1e30
BF, F32 = jnp.bfloat16, jnp.float32
QB = 256


def scaled_norm(values, norm_gain, norm_shift):
    peak = jnp.max(jnp.abs(values), axis=-1, keepdims=True) + NORM_EPS
    scaled = values / peak
    centred = scaled - jnp.mean(scaled, axis=-1, keepdims=True)
    spread = jnp.mean(centred * centred, axis=-1, keepdims=True)
    return centred * lax.rsqrt(spread + NORM_EPS) * norm_gain + norm_shift


def norm_back(values, norm_gain, norm_shift, row_grad):
    result, pull = jax.vjp(scaled_norm, values, norm_gain, norm_shift)
    return pull(row_grad)


PAIR = 2 * DH


def attn_fwd_kernel(qpos_ref, qstart_ref, kpos_ref, qkv_ref, o_ref, lse_ref):
    first = pl.multiple_of(pl.program_id(0) * QB, QB)
    kpos = kpos_ref[...]
    allowed = (kpos <= qpos_ref[...]) & (kpos >= qstart_ref[...])
    bias = jnp.where(allowed, 0.0, MASKED_OUT)
    lane = lax.broadcasted_iota(jnp.int32, (1, PAIR), 1)
    wide = lax.broadcasted_iota(jnp.int32, lse_ref.shape, 1)
    stats = jnp.zeros(lse_ref.shape, F32)
    for pair in range(o_ref.shape[1] // PAIR):
        at = 3 * pair * PAIR
        query = qkv_ref[pl.ds(first, QB), at:at + PAIR]
        key, value = qkv_ref[:, at + PAIR:at + 2 * PAIR], qkv_ref[:, at + 2 * PAIR:at + 3 * PAIR]
        total = jnp.zeros(query.shape, F32)
        for side in range(2):
            mine = (lane >= side * DH) & (lane < (side + 1) * DH)
            part = jnp.where(mine, query * 0.125, 0.0).astype(BF)
            score = lax.dot_general(part, key, (((1,), (1,)), ((), ())), preferred_element_type=F32) + bias
            peak = jnp.max(score, axis=-1, keepdims=True)
            expo = jnp.exp(score - peak)
            norm = jnp.sum(expo, axis=-1, keepdims=True)
            prob = (expo * (1.0 / norm)).astype(BF)
            total += jnp.dot(prob, jnp.where(mine, value, jnp.zeros_like(value)), preferred_element_type=F32)
            stats = jnp.where(wide == pair * 2 + side, peak + jnp.log(norm), stats)
        o_ref[:, pair * PAIR:(pair + 1) * PAIR] = total.astype(BF)
    lse_ref[...] = stats


def attn_forward(qpos, qstart, kpos, qkv):
    rows, width = qkv.shape[0], qkv.shape[1] // 3
    col = pl.BlockSpec((QB, 1), lambda i: (i, 0))
    full = pl.BlockSpec(qkv.shape, lambda i: (0, 0))
    return pl.pallas_call(
        attn_fwd_kernel,
        grid=(rows // QB,),
        in_specs=[col, col, pl.BlockSpec((1, rows), lambda i: (0, 0)), full],
        out_specs=[pl.BlockSpec((QB, width), lambda i: (i, 0)), pl.BlockSpec((QB, 128), lambda i: (i, 0))],
        out_shape=[jax.ShapeDtypeStruct((rows, width), BF), jax.ShapeDtypeStruct((rows, 128), F32)],
        cost_estimate=pl.CostEstimate(flops=4 * rows * rows * width, bytes_accessed=8 * rows * width, transcendentals=rows * rows * width // DH),
        compiler_params=pltpu.CompilerParams(vmem_limit_bytes=48 << 20),
        name="attn_fwd",
    )(qpos, qstart, kpos, qkv)


def attn_bwd_kernel(qpos_ref, qstart_ref, kpos_ref, lse_ref, g_ref, qkv_ref, d_ref, dk_acc, dv_acc):
    step = pl.program_id(0)
    first = pl.multiple_of(step * QB, QB)

    @pl.when(step == 0)
    def _():
        dk_acc[...] = jnp.zeros_like(dk_acc)
        dv_acc[...] = jnp.zeros_like(dv_acc)

    kpos = kpos_ref[...]
    allowed = (kpos <= qpos_ref[...]) & (kpos >= qstart_ref[...])
    bias = jnp.where(allowed, 0.0, MASKED_OUT)
    lane = lax.broadcasted_iota(jnp.int32, (1, PAIR), 1)
    for pair in range(g_ref.shape[1] // PAIR):
        at = 3 * pair * PAIR
        query = qkv_ref[pl.ds(first, QB), at:at + PAIR]
        key, value = qkv_ref[:, at + PAIR:at + 2 * PAIR], qkv_ref[:, at + 2 * PAIR:at + 3 * PAIR]
        cols = slice(pair * PAIR, (pair + 1) * PAIR)
        grad = g_ref[:, cols]
        dq = jnp.zeros(query.shape, F32)
        dk = jnp.zeros(key.shape, F32)
        dv = jnp.zeros(key.shape, F32)
        for side in range(2):
            mine = (lane >= side * DH) & (lane < (side + 1) * DH)
            part = jnp.where(mine, query * 0.125, 0.0).astype(BF)
            gpart = jnp.where(mine, grad, jnp.zeros_like(grad))
            score = lax.dot_general(part, key, (((1,), (1,)), ((), ())), preferred_element_type=F32) + bias
            index = pair * 2 + side
            prob = jnp.exp(score - lse_ref[:, index:index + 1])
            gprob = lax.dot_general(gpart, value, (((1,), (1,)), ((), ())), preferred_element_type=F32)
            inner = jnp.sum(prob * gprob, axis=-1, keepdims=True)
            gscore = (prob * (gprob - inner)).astype(BF)
            dq += jnp.dot(gscore, jnp.where(mine, key, jnp.zeros_like(key)), preferred_element_type=F32)
            dk += lax.dot_general(gscore, part, (((0,), (0,)), ((), ())), preferred_element_type=F32)
            dv += lax.dot_general(prob.astype(BF), gpart, (((0,), (0,)), ((), ())), preferred_element_type=F32)
        d_ref[pl.ds(first, QB), at:at + PAIR] = (dq * 0.125).astype(BF)
        dk_acc[:, cols] += dk
        dv_acc[:, cols] += dv

    @pl.when(step == pl.num_programs(0) - 1)
    def _():
        for pair in range(g_ref.shape[1] // PAIR):
            at = 3 * pair * PAIR
            cols = slice(pair * PAIR, (pair + 1) * PAIR)
            d_ref[:, at + PAIR:at + 2 * PAIR] = dk_acc[:, cols].astype(BF)
            d_ref[:, at + 2 * PAIR:at + 3 * PAIR] = dv_acc[:, cols].astype(BF)


def attn_backward(qpos, qstart, kpos, lse, grad, qkv):
    rows, width = grad.shape
    col = pl.BlockSpec((QB, 1), lambda i: (i, 0))
    full = pl.BlockSpec(qkv.shape, lambda i: (0, 0))
    return pl.pallas_call(
        attn_bwd_kernel,
        grid=(rows // QB,),
        in_specs=[col, col, pl.BlockSpec((1, rows), lambda i: (0, 0)), pl.BlockSpec((QB, 128), lambda i: (i, 0)),
                  pl.BlockSpec((QB, width), lambda i: (i, 0)), full],
        out_specs=full,
        out_shape=jax.ShapeDtypeStruct(qkv.shape, BF),
        scratch_shapes=[pltpu.VMEM((rows, width), F32), pltpu.VMEM((rows, width), F32)],
        cost_estimate=pl.CostEstimate(flops=10 * rows * rows * width, bytes_accessed=14 * rows * width, transcendentals=rows * rows * width // DH),
        compiler_params=pltpu.CompilerParams(vmem_limit_bytes=48 << 20),
        name="attn_bwd",
    )(qpos, qstart, kpos, lse, grad, qkv)


def swap_dp(x, bit):
    n = lax.axis_size("dp")
    return lax.ppermute(x, "dp", [(i, i ^ bit) for i in range(n)])


def turn(x, shift):
    n = lax.axis_size("tensor")
    return lax.ppermute(x, "tensor", [(i, (i + shift) % n) for i in range(n)])


def chip_bits():
    n = lax.axis_size("dp")
    return [1 << b for b in range(1, n.bit_length() - 1)]


def core_pair(mine, other):
    core = lax.axis_index("dp") % 2
    return jnp.where(core == 0, jnp.stack([mine, other]), jnp.stack([other, mine]))


def gather_weights(mine, other):
    pair = core_pair(mine, swap_dp(other, 1)).reshape(2 * mine.shape[0], mine.shape[1])
    lanes = lax.axis_size("tensor")
    column = jnp.stack([pair] + [turn(pair, k) for k in range(1, lanes)])
    bits = chip_bits()
    if len(bits) == 2:
        low, high = bits
        first, second = swap_dp(column, low), swap_dp(column, high)
        mid = lanes // 2
        far = jnp.concatenate([swap_dp(first[:mid], high), swap_dp(second[mid:], low)])
        return {0: column, low: first, high: second, low | high: far}
    blocks = {0: column}
    for bit in bits:
        got = swap_dp(jnp.stack([blocks[m] for m in sorted(blocks)]), bit)
        blocks.update({m | bit: got[i] for i, m in enumerate(sorted(blocks))})
    return blocks


def weight_of(blocks, start, width):
    out = []
    for mask in sorted(blocks):
        part = blocks[mask][:, :, start:start + width]
        out.append(jnp.concatenate([part[k] for k in range(part.shape[0])], axis=1))
    return jnp.concatenate(out, axis=0)


def scatter_grads(parts):
    lanes = lax.axis_size("tensor")
    bits = chip_bits()
    count = 1 << len(bits)
    feats = parts[0].shape[0]
    per = feats // count

    def block(mask_index, k):
        cut = []
        for p in parts:
            w = p.shape[1] // lanes
            cut.append(p[mask_index * per:(mask_index + 1) * per, k * w:(k + 1) * w])
        return jnp.concatenate(cut, axis=1) if len(cut) > 1 else cut[0]

    def col(mask_index, ks):
        return jnp.stack([block(mask_index, k) for k in ks])

    if len(bits) == 2:
        low, high = bits
        mid = lanes // 2
        ka, kb = list(range(mid)), list(range(mid, lanes))
        sent_a = jnp.stack([col(1, ka), col(3, ka)]).astype(BF)
        sent_b = jnp.stack([col(2, kb), col(3, kb)]).astype(BF)
        got_a, got_b = swap_dp(sent_a, low), swap_dp(sent_b, high)
        pass_a = (col(2, ka) + got_a[1].astype(F32)).astype(BF)
        pass_b = (col(1, kb) + got_b[1].astype(F32)).astype(BF)
        end_a, end_b = swap_dp(pass_a, high), swap_dp(pass_b, low)
        keep_a = col(0, ka) + got_a[0].astype(F32) + end_a.astype(F32)
        keep_b = col(0, kb) + got_b[0].astype(F32) + end_b.astype(F32)
        total = [keep_a[i] for i in range(mid)] + [keep_b[i] for i in range(lanes - mid)]
    else:
        sums = {m: col(m, range(lanes)) for m in range(count)}
        for level in reversed(range(len(bits))):
            keys = [m for m in sorted(sums) if m >> level & 1]
            got = swap_dp(jnp.stack([sums[m] for m in keys]).astype(BF), bits[level])
            sums = {m ^ (1 << level): sums[m ^ (1 << level)] + got[i].astype(F32) for i, m in enumerate(keys)}
        total = [sums[0][k] for k in range(lanes)]
    own = total[0]
    for k in range(1, lanes):
        own = own + turn(total[k].astype(BF), -k).astype(F32)
    rows = own.shape[0] // 2
    core = lax.axis_index("dp") % 2
    mine = lax.dynamic_slice_in_dim(own, core * rows, rows, 0)
    other = lax.dynamic_slice_in_dim(own, (1 - core) * rows, rows, 0)
    return core_pair(mine, swap_dp(other.astype(BF), 1).astype(F32))


def deal_perms(n_dp):
    near, far = [], []
    for chip in range(n_dp // 2):
        for c in range(2):
            for j in range(4):
                source = (chip * 2 + c) * 4 + j
                near.append((source, (chip * 2 + j % 2) * 4 + 2 * c + j // 2))
                far.append((source, (chip * 2 + j % 2) * 4 + 2 * c + 1 - j // 2))
    return near, far


MESH = pl.DeviceIdType.MESH
LANES = 4
ANY = pl.BlockSpec(memory_space=pl.ANY)
IN_VMEM = pl.BlockSpec(memory_space=pltpu.VMEM)


def greet(dp, lane, n_dp):
    barrier = pltpu.get_barrier_semaphore()
    count = 0
    for d in range(1, n_dp):
        pl.semaphore_signal(barrier, inc=1, device_id=(dp ^ d, lane), device_id_type=MESH)
        count += 1
    for k in range(1, LANES):
        for c in range(2):
            pl.semaphore_signal(barrier, inc=1, device_id=(dp ^ c, lax.rem(lane + k, LANES)), device_id_type=MESH)
            count += 1
    return barrier, count


def send(src, dst, send_sem, recv_sem, device):
    return pltpu.make_async_remote_copy(src_ref=src, dst_ref=dst, send_sem=send_sem, recv_sem=recv_sem, device_id=device, device_id_type=MESH)


DEAL_CUTS = 4
SMEM = pl.BlockSpec(memory_space=pltpu.SMEM)


class Pack:
    def __init__(self, lengths, deal, dp, lane, rows):
        core = dp % 2
        per = lengths.shape[0] // 8
        first = ((dp // 2) * 2 + lane // 2) * per
        self.starts, end, self.cut = [], 0, 0
        for j in range(per):
            size = lengths[deal[first + j]]
            self.starts.append(end)
            self.cut = self.cut + jnp.where(size == HALF, end, 0)
            end = end + size
        self.half, self.offset, self.rows = lane % 2, core * rows, rows

    def slots(self, begin, count, axis):
        shape = (count, 1) if axis == 0 else (1, count)
        return (self.offset + begin + lax.broadcasted_iota(jnp.int32, shape, axis)) & (2 * self.rows - 1)

    def places(self, begin, count, axis):
        slot = self.slots(begin, count, axis)
        return slot + HALF * jnp.where(slot >= self.cut, self.half, 1 - self.half)

    def seen_from(self, places):
        out = jnp.zeros(places.shape, jnp.int32)
        for start in self.starts:
            out = jnp.maximum(out, jnp.where(places >= start, start, 0))
        return out

    def bias(self, begin, kpos):
        at = self.places(begin, QB, 0)
        return jnp.where((kpos <= at) & (kpos >= self.seen_from(at)), 0.0, MASKED_OUT)


def relative(vec, chip, sources):
    quarter = vec.shape[1] // 4
    for q in range(4):
        cols = pl.ds(pl.multiple_of((chip ^ q) * quarter, quarter), quarter)
        at = 0
        for src in sources:
            count = src.shape[0]
            vec[at:at + count, q * quarter:(q + 1) * quarter] = src[:, cols]
            at += count


def norm_parts(x):
    peak = jnp.max(jnp.abs(x), axis=-1, keepdims=True) + NORM_EPS
    u = x * (1.0 / peak)
    c = u - jnp.mean(u, axis=-1, keepdims=True)
    return c, lax.rsqrt(jnp.mean(c * c, axis=-1, keepdims=True) + NORM_EPS)


def norm_rows(x, gain, shift):
    c, r = norm_parts(x)
    return c * r * gain + shift


def dot_t(a, b):
    return lax.dot_general(a, b, (((1,), (1,)), ((), ())), preferred_element_type=F32)


class Sems:
    def __init__(self, ref):
        self.ref, self.used = ref, 0

    def take(self, count=1):
        self.used += count
        return self.used - count


FWD_SEMS = 320


def forward_kernel(widths, lengths, deal, w_qkv, w_o, w_1, w_2, b_qv, b_1, b_o, b_2, ln_gain, ln_bias, tok, cot, *rest):
    outs, rest = rest[:18], rest[18:]
    (wq_o, wo_o, w1_o, w2_o, h_o, xin_o, qkv_o, heads_o, lse_o, attn_o, first_o, xmid_o, act_o, dg_o, ffn_o, res_o, grd_o, small_o) = outs
    (wq, wo, w1, w2, moved, cand, h, xin, qkv, heads, lse, part, sbuf, rbuf, first, xmid, act, dg, stage, small_in, own, other, small, vec, sem_ref) = rest
    mats = (wq, wo, w1, w2)
    sems = Sems(sem_ref)
    dp, lane = lax.axis_index("dp"), lax.axis_index("tensor")
    n_dp = 8
    core, chip = dp % 2, dp // 2
    rows, d = tok.shape
    wd = own.shape[0]
    quarter = d // 4
    up = lax.rem(lane + 1, LANES)
    n_g = len(widths)
    mate = (dp ^ 1, lane)
    ends = []

    def local(src, dst):
        c = pltpu.make_async_copy(src, dst, sem_ref.at[sems.take()])
        return c

    def remote(src, dst, device):
        s, r = sems.take(), sems.take()
        c = send(src, dst, sem_ref.at[s], sem_ref.at[r], device)
        ends.append(c.wait_send)
        return c

    barrier, count = greet(dp, lane, n_dp)
    rows_of = lambda x: jnp.transpose(x.astype(F32)).astype(BF)
    for half, dst in ((core, own), (1 - core, other)):
        at = 0
        part_of = lambda w: pl.ds(pl.multiple_of(half * w, w), w)
        for t in range(3):
            dst[:, at:at + widths[1]] = w_qkv[t, :, part_of(widths[1])]
            at += widths[1]
        for src, w, turned in ((w_o, widths[1], True), (w_1, widths[2], False), (w_2, widths[3], True)):
            dst[:, at:at + w] = rows_of(src[part_of(w), :]) if turned else src[:, part_of(w)]
            at += w
    at = 0
    small[...] = jnp.zeros_like(small)
    for src, w in ((b_qv.at[0:1], widths[1]), (b_qv.at[1:2], widths[1]), (b_1, widths[2])):
        small[0:1, at:at + w] = src[:, pl.ds(pl.multiple_of(core * w, w), w)]
        at += w
    relative(vec, chip, (ln_gain, ln_bias, b_o, b_2))
    held = Pack(lengths, deal, dp, lane, rows)
    pl.semaphore_wait(barrier, count)
    block = rows // n_dp
    here = pl.ds(pl.multiple_of(dp * block, block), block)
    deals = []
    for i, src in enumerate((tok, cot)):
        stay = local(src.at[here], moved.at[i, here])
        copies = []
        for k in range(1, n_dp):
            there = pl.ds(pl.multiple_of((dp ^ k) * block, block), block)
            copies.append(remote(src.at[there], moved.at[i, here], (dp ^ k, lane)))
        deals.append((stay, copies))

    def deal_start(i):
        deals[i][0].start()
        for c in deals[i][1]:
            c.start()

    deal_start(0)
    feat = pl.ds(pl.multiple_of(core * wd, wd), wd)
    at, stays, pairs = 0, [], []
    for g, w in enumerate(widths):
        dst = mats[g].at[feat, 0:w]
        stays.append(local(own.at[:, at:at + w], dst))
        pairs.append(remote(other.at[:, at:at + w], dst, mate))
        stays[g].start()
        pairs[g].start()
        at += w
    n_s = small.shape[0]
    smalls = [remote(small, small_in.at[k], (dp, lax.rem(lane + k, LANES))) for k in range(1, LANES)]
    for c in smalls:
        c.start()
    small_in[0] = small[...]

    def area(g, q, k):
        w = widths[g]
        return mats[g].at[2 * wd * q:2 * wd * (q + 1), k * w:(k + 1) * w]

    turns = [[remote(area(g, 0, t), area(g, 0, t + 1), (dp, up)) for t in range(LANES - 1)] for g in range(n_g)]
    planes = [[[remote(area(g, 0, k), area(g, side, k), (dp ^ (2 * side), lane)) for side in (1, 2)] for k in range(LANES)] for g in range(n_g)]
    fars = []
    for g in range(n_g):
        fars.append([])
        for k in range(LANES):
            side, via = (1, 2) if k < LANES // 2 else (2, 1)
            fars[g].append(remote(area(g, side, k), area(g, 3, k), (dp ^ (2 * via), lane)))

    def plane(g, k):
        for c in planes[g][k]:
            c.start()

    def pair_in(g):
        stays[g].wait()
        pairs[g].wait_recv()
        turns[g][0].start()

    def turn_in(g, t):
        turns[g][t].wait_recv()
        if t < LANES - 2:
            turns[g][t + 1].start()

    def far_go(g, k):
        planes[g][k][0 if k < LANES // 2 else 1].wait_recv()
        fars[g][k].start()

    def all_in(g):
        for k in range(LANES):
            planes[g][k][1 if k < LANES // 2 else 0].wait_recv()
            fars[g][k].wait_recv()

    pack = lane // 2
    spot = chip * 2 + lane % 2
    to_near = (spot, core + 1)
    slot = jnp.where(lane // 2 == core, 1, 0)
    is_self = (lane == 3 * core) & (spot == dp)
    is_near = lane == pack + 1
    straight = core == pack
    split = jnp.where(jnp.logical_not(is_near) & jnp.logical_not(straight), 2 * HALF, held.cut)
    cut = rows // DEAL_CUTS

    class Route:
        def __init__(self, i):
            self.i = i
            a0, f0 = sems.take(DEAL_CUTS), sems.take(DEAL_CUTS)
            got = sems.take(2 * DEAL_CUTS)
            self.near, self.self_, self.hand, self.pick, self.wait0, self.wait1 = [], [], [], [], [], []
            for n in range(DEAL_CUTS):
                rs = slice(n * cut, (n + 1) * cut)
                src = moved.at[i, rs]
                last = (dp, 3 * pack)
                self.near.append(send(src, cand.at[i, slot, rs], sem_ref.at[a0 + n], sem_ref.at[got + n * 2 + slot], to_near))
                self.self_.append(pltpu.make_async_copy(src, cand.at[i, 0, rs], sem_ref.at[got + n * 2]))
                self.hand.append(send(cand.at[i, 0, rs], cand.at[i, 1, rs], sem_ref.at[f0 + n], sem_ref.at[got + n * 2 + 1], last))
                self.pick.append(send(stage.at[0, rs], cand.at[i, 1, rs], sem_ref.at[f0 + n], sem_ref.at[got + n * 2 + 1], last))
                self.wait0.append(send(src, cand.at[i, 0, rs], sem_ref.at[a0 + n], sem_ref.at[got + n * 2], to_near))
                self.wait1.append(send(src, cand.at[i, 1, rs], sem_ref.at[a0 + n], sem_ref.at[got + n * 2 + 1], to_near))

        def start(self):
            for n in range(DEAL_CUTS):
                self.near[n].start()
                pl.when(is_self)(lambda: self.self_[n].start())

        def arrive(self, n):
            pl.when(is_self)(lambda: self.self_[n].wait())
            pl.when(is_near)(lambda: self.wait0[n].wait_recv())
            pl.when(is_near & straight)(lambda: self.hand[n].start())
            self.wait1[n].wait_recv()

            def choose_far():
                rs = slice(n * cut, (n + 1) * cut)
                on = held.slots(n * cut, cut, 0) >= held.cut
                stage[0, rs] = jnp.where(on, cand[self.i, 1, rs].astype(F32), cand[self.i, 0, rs].astype(F32)).astype(BF)
                self.pick[n].start()

            pl.when(is_near & jnp.logical_not(straight))(choose_far)

        def finish(self, picked=True):
            for n in range(DEAL_CUTS):
                self.near[n].wait_send()
                pl.when(is_near & straight)(lambda: self.hand[n].wait_send())
                if picked:
                    pl.when(is_near & jnp.logical_not(straight))(lambda: self.pick[n].wait_send())

    routes = [Route(0), Route(1)]

    def deal_on(i):
        deals[i][0].wait()
        for c in deals[i][1]:
            c.wait_recv()
        routes[i].start()

    def choose(i, n):
        rs = slice(n * cut, (n + 1) * cut)
        on = held.slots(n * cut, cut, 0) >= split
        parts = []
        for q in range(4):
            cols = pl.ds(pl.multiple_of((chip ^ q) * quarter, quarter), quarter)
            parts.append(jnp.where(on, cand[i, 0, rs, cols].astype(F32), cand[i, 1, rs, cols].astype(F32)))
        return jnp.concatenate(parts, axis=1)

    out_copies = []

    def put(src, dst):
        c = local(src, dst)
        c.start()
        out_copies.append(c)

    early = (0, 1)

    def forward_on(groups, t):
        for g in groups:
            turn_in(g, t)
        for g in groups:
            plane(g, t + 1)

    for g in (0, 1, 2):
        pair_in(g)
        plane(g, 0)
    forward_on(early, 0)
    forward_on((2,), 0)
    forward_on(early, 1)
    deal_on(0)
    forward_on((2,), 1)
    forward_on(early, 2)
    for k in range(LANES):
        for g in early:
            far_go(g, k)
    pair_in(3)
    plane(3, 0)
    deal_start(1)
    joins = []

    def join_send(x, n, size):
        c = remote(x.at[n * size:(n + 1) * size], x.at[rows + n * size:rows + (n + 1) * size], mate)
        c.start()
        joins.append(c)

    gains = lambda i: vec[i:i + 1, :]
    for n in range(DEAL_CUTS):
        rs = slice(n * cut, (n + 1) * cut)
        routes[0].arrive(n)
        x = choose(0, n)
        h[rs, :] = x.astype(BF)
        xin[rs, :] = norm_rows(x, gains(0), gains(4)).astype(BF)
        join_send(xin, n, cut)
        if n == 2:
            forward_on((2,), 2)
    forward_on((3,), 0)
    for c in smalls:
        c.wait_recv()
    all_in(0)
    for c in joins:
        c.wait_recv()
    put(wq, wq_o)
    put(h, h_o)
    put(xin, xin_o)
    w = widths[0]
    third = w // 3
    for k in range(LANES):
        cols = slice(k * w, (k + 1) * w)
        row = small_in[k, 0:1, :]
        bias = jnp.concatenate([row[:, 0:third], jnp.zeros((1, third), F32), row[:, third:2 * third]], axis=1)

        def project(r, carry, cols=cols, bias=bias):
            rs = pl.ds(pl.multiple_of(r * QB, QB), QB)
            qkv[rs, cols] = (jnp.dot(xin[rs, :], wq[:, cols], preferred_element_type=F32) + bias).astype(BF)
            return carry

        lax.fori_loop(0, 2 * rows // QB, project, 0)
        far_go(2, k)
    put(qkv, qkv_o)
    forward_on((3,), 1)

    kpos = held.places(0, 2 * rows, 1)

    def beside(i):
        if i == 0:
            deal_on(1)
        elif i == 1:
            forward_on((3,), 2)
        elif i == 2:
            far_go(3, 0)
            far_go(3, 1)

    def attend(i, carry):
        begin = pl.multiple_of(i * QB, QB)
        attn_block(pl.ds(begin, QB), held.bias(begin, kpos), qkv, heads, lse)
        for n in range(3):
            pl.when(i == n)(lambda: beside(n))
        return carry

    lax.fori_loop(0, 2 * rows // QB, attend, 0)
    put(heads, heads_o)
    put(lse, lse_o)
    all_in(1)
    put(wo, wo_o)

    def fold(x, w_ref, which):
        copies = []
        per = 2
        size = rows // per
        for n in range(per):
            rs = slice(rows + n * size, rows + (n + 1) * size)
            sbuf[which, n * size:(n + 1) * size] = dot_t(x[rs, :], w_ref[...]).astype(BF)
            c = remote(sbuf.at[which, n * size:(n + 1) * size], rbuf.at[which, n * size:(n + 1) * size], mate)
            c.start()
            copies.append(c)
        for n in range(per):
            rs = slice(n * size, (n + 1) * size)
            part[rs, :] = dot_t(x[rs, :], w_ref[...])
        return copies

    copies = fold(heads, wo, 0)
    joins.clear()
    size = rows // 2
    for n in range(2):
        copies[n].wait_recv()

        def middle(m, carry, n=n):
            rs = pl.ds(pl.multiple_of(n * size + m * cut, cut), cut)
            y = part[rs, :] + rbuf[0, rs].astype(F32) + gains(8)
            part[rs, :] = y
            f = h[rs, :].astype(F32) + norm_rows(y, gains(1), gains(5))
            first[rs, :] = f
            xmid[rs, :] = norm_rows(f, gains(2), gains(6)).astype(BF)
            return carry

        lax.fori_loop(0, size // cut, middle, 0)
        join_send(xmid, n, size)
    attn_put = local(part, attn_o)
    attn_put.start()
    put(first, first_o)
    all_in(2)
    put(w1, w1_o)
    for c in joins:
        c.wait_recv()
    put(xmid, xmid_o)
    w = widths[2]
    for k in range(LANES):
        cols = slice(k * w, (k + 1) * w)
        bias = small_in[k, 0:1, 2 * third:2 * third + w]

        def hidden_units(r, carry, cols=cols, bias=bias):
            rs = pl.ds(pl.multiple_of(r * QB, QB), QB)
            pre = jnp.dot(xmid[rs, :], w1[:, cols], preferred_element_type=F32) + bias
            cdf = 0.5 + 0.5 * lax.erf(pre * 0.7071067811865476)
            act[rs, cols] = (pre * cdf).astype(BF)
            dg[rs, cols] = (cdf + pre * (0.3989422804014327 * jnp.exp(-0.5 * pre * pre))).astype(BF)
            return carry

        lax.fori_loop(0, 2 * rows // QB, hidden_units, 0)
        if k < 2:
            far_go(3, k + 2)
        if k == 1:
            routes[0].finish()
        if k > 1:
            routes[1].arrive(2 * k - 4)
            routes[1].arrive(2 * k - 3)
    put(act, act_o)
    put(dg, dg_o)
    all_in(3)
    put(w2, w2_o)
    attn_put.wait()
    copies = fold(act, w2, 1)
    for n in range(DEAL_CUTS):
        rs = slice(n * cut, (n + 1) * cut)
        stage[1, rs] = choose(1, n).astype(BF)
    put(stage.at[1], grd_o)
    for n in range(DEAL_CUTS):
        pl.when(is_near & jnp.logical_not(straight))(lambda: routes[1].pick[n].wait_send())
    for n in range(2):
        copies[n].wait_recv()

        def last(m, carry, n=n):
            rs = pl.ds(pl.multiple_of(n * size + m * cut, cut), cut)
            y = part[rs, :] + rbuf[1, rs].astype(F32) + gains(9)
            part[rs, :] = y
            out = first[rs, :] + norm_rows(y, gains(3), gains(7))
            for q in range(4):
                cols = pl.ds(pl.multiple_of((chip ^ q) * quarter, quarter), quarter)
                stage[0, rs, cols] = out[:, q * quarter:(q + 1) * quarter].astype(BF)
            return carry

        lax.fori_loop(0, size // cut, last, 0)
    put(part, ffn_o)
    put(stage.at[0], res_o)
    put(small_in, small_o)
    for c in out_copies:
        c.wait()
    routes[1].finish(False)
    for wait in ends:
        wait()


def attn_block(rs, bias, qkv, heads, lse):
    lane = lax.broadcasted_iota(jnp.int32, (1, PAIR), 1)
    wide = lax.broadcasted_iota(jnp.int32, (QB, 128), 1)
    stats = jnp.zeros((QB, 128), F32)
    for pair in range(heads.shape[1] // PAIR):
        at = 3 * pair * PAIR
        query = qkv[rs, at:at + PAIR]
        key, value = qkv[:, at + PAIR:at + 2 * PAIR], qkv[:, at + 2 * PAIR:at + 3 * PAIR]
        total = jnp.zeros(query.shape, F32)
        for side in range(2):
            mine = (lane >= side * DH) & (lane < (side + 1) * DH)
            piece = jnp.where(mine, query * 0.125, 0.0).astype(BF)
            score = dot_t(piece, key) + bias
            peak = jnp.max(score, axis=-1, keepdims=True)
            expo = jnp.exp(score - peak)
            norm = jnp.sum(expo, axis=-1, keepdims=True)
            prob = (expo * (1.0 / norm)).astype(BF)
            total += jnp.dot(prob, jnp.where(mine, value, jnp.zeros_like(value)), preferred_element_type=F32)
            stats = jnp.where(wide == pair * 2 + side, peak + jnp.log(norm), stats)
        heads[rs, pair * PAIR:(pair + 1) * PAIR] = total.astype(BF)
    lse[rs, :] = stats


def forward_call(widths, tok, cot, lengths, deal, w_qkv, w_o, w_1, w_2, b_qv, b_1, b_o, b_2, ln_gain, ln_bias):
    rows, d = tok.shape
    both = 2 * rows
    vm = pltpu.VMEM
    hidden = LANES * widths[2]
    small = (8, 2 * widths[1] + widths[2])
    mats = [(d, LANES * w) for w in widths]
    shape = jax.ShapeDtypeStruct
    out = [shape(m, BF) for m in mats] + [
        shape((rows, d), BF), shape((both, d), BF), shape((both, LANES * widths[0]), BF), shape((both, LANES * widths[1]), BF), shape((both, 128), F32),
        shape((rows, d), F32), shape((rows, d), F32), shape((both, d), BF), shape((both, hidden), BF), shape((both, hidden), BF),
        shape((rows, d), F32), shape((rows, d), BF), shape((rows, d), BF), shape((LANES,) + small, F32)]
    scratch = [vm(m, BF) for m in mats] + [
        vm((2, rows, d), BF), vm((2, 2, rows, d), BF), vm((rows, d), BF), vm((both, d), BF), vm((both, LANES * widths[0]), BF),
        vm((both, LANES * widths[1]), BF), vm((both, 128), F32), vm((rows, d), F32), vm((2, rows, d), BF), vm((2, rows, d), BF),
        vm((rows, d), F32), vm((both, d), BF), vm((both, hidden), BF), vm((both, hidden), BF), vm((2, rows, d), BF),
        vm((LANES,) + small, F32), vm((d // 8, sum(widths)), BF), vm((d // 8, sum(widths)), BF), vm(small, F32), vm((16, d), F32),
        pltpu.SemaphoreType.DMA((FWD_SEMS,))]
    return pl.pallas_call(
        partial(forward_kernel, widths),
        in_specs=[SMEM, SMEM] + [IN_VMEM] * 10 + [ANY, ANY],
        out_specs=[ANY] * len(out),
        out_shape=out,
        scratch_shapes=scratch,
        compiler_params=pltpu.CompilerParams(collective_id=1, has_side_effects=True, vmem_limit_bytes=67043328),
        name="forward",
    )(lengths, deal, w_qkv, w_o, w_1, w_2, b_qv, b_1, b_o, b_2, ln_gain, ln_bias, tok, cot)


def norm_back_rows(x, grad, gain):
    mag = jnp.abs(x)
    top = jnp.max(mag, axis=-1, keepdims=True)
    inv = 1.0 / (top + NORM_EPS)
    u = x * inv
    c = u - jnp.mean(u, axis=-1, keepdims=True)
    r = lax.rsqrt(jnp.mean(c * c, axis=-1, keepdims=True) + NORM_EPS)
    xhat = c * r
    t = grad * gain
    gx = grad * xhat
    along = jnp.mean(t * xhat, axis=-1, keepdims=True)
    du = r * (t - jnp.mean(t, axis=-1, keepdims=True) - xhat * along)
    at_top = mag == top
    ties = jnp.sum(jnp.where(at_top, 1.0, 0.0), axis=-1, keepdims=True)
    pull = x.shape[-1] * NORM_EPS * along * r * r * inv / ties
    side = jnp.where(x > 0, -pull, jnp.where(x < 0, pull, 0.0))
    return du * inv + jnp.where(at_top, side, 0.0), gx


BWD_SEMS = 420


def dot_g(a, b):
    return lax.dot_general(a, b, (((0,), (0,)), ((), ())), preferred_element_type=F32)


def column_sums(x):
    return jnp.sum(x, axis=0, keepdims=True)


def backward_kernel(widths, lengths, deal, ln_gain, *rest):
    ins, rest = rest[:17], rest[17:]
    (wq_i, wo_i, w1_i, w2_i, h_i, xin_i, qkv_i, heads_i, lse_i, attn_i, first_i, xmid_i, act_i, dg_i, ffn_i, res_i, grd_i) = ins
    outs, rest = rest[:9], rest[9:]
    (qkv_o, wo_o, w1_o, w2_o, out_o, ig_o, vec_o, home_o, _) = outs
    (wq, wo, w1, w2, part, grd, act, dg, xmid, first, attn, heads, qkv, lse, dfull, res, dqkv, dkv, sbuf, rbuf, zin,
     fl3, fl2, fl1, sl3, sl2, sl1, tl3, tl2, tl1, third0, third1, third2, third3, tall, wide_o, sums, sums_in, vec_all, vec, room, free, sem_ref) = rest
    xin, h = dfull, res
    mats = (dg, wo, w1, w2)
    thirds = (third0, third1, third2, third3)
    n_g = len(widths)
    sems = Sems(sem_ref)
    dp, lane = lax.axis_index("dp"), lax.axis_index("tensor")
    n_dp = 8
    core, chip = dp % 2, dp // 2
    rows, d = grd.shape
    quarter = d // 4
    per = 2 * (d // n_dp)
    wd = d // n_dp
    mate = (dp ^ 1, lane)
    cut = rows // DEAL_CUTS
    ends = []

    def local(src, dst):
        return pltpu.make_async_copy(src, dst, sem_ref.at[sems.take()])

    def remote(src, dst, device):
        a, b = sems.take(), sems.take()
        c = send(src, dst, sem_ref.at[a], sem_ref.at[b], device)
        ends.append(c)
        return c

    loads = {}
    for name, src, dst in (("ffn", ffn_i, part), ("grd", grd_i, grd), ("res", res_i, res), ("w2", w2_i, w2), ("dg", dg_i, dg), ("act", act_i, act),
                           ("w1", w1_i, w1), ("xmid", xmid_i, xmid), ("first", first_i, first), ("attn", attn_i, attn), ("wo", wo_i, wo),
                           ("heads", heads_i, heads), ("qkv", qkv_i, qkv), ("lse", lse_i, lse), ("wq", wq_i, wq), ("xin", xin_i, xin), ("h", h_i, h)):
        loads[name] = local(src, dst)
        if name not in ("xin", "h"):
            loads[name].start()
    barrier, count = greet(dp, lane, n_dp)
    held = Pack(lengths, deal, dp, lane, rows)
    relative(vec, chip, (ln_gain,))
    pl.semaphore_wait(barrier, count)
    gains = lambda i: vec[i:i + 1, :]
    sums[...] = jnp.zeros_like(sums)
    pack = lane // 2
    is_near = lane == pack + 1
    is_far = lane == 3 * pack
    block = rows // n_dp

    class Back:
        def __init__(self, i, src, same, other, out):
            self.i, self.src, self.same, self.other = i, src, same, other
            self.out = out
            z0, z1, m0, o0, h0 = [sems.take(DEAL_CUTS) for _ in range(5)]
            a0, a1 = sems.take(n_dp), sems.take(n_dp)
            self.a0, self.a1 = a0, a1
            spot = chip * 2 + pack
            kappa = core
            self.up_, self.keep_, self.give_ = [], [], []
            for n in range(DEAL_CUTS):
                rs = slice(n * cut, (n + 1) * cut)
                self.up_.append(send(src.at[rs], zin.at[i, rs], sem_ref.at[z0 + n], sem_ref.at[z1 + n], (dp, pack + 1)))
                self.keep_.append(send(same.at[rs], home_o.at[i, rs], sem_ref.at[m0 + n], sem_ref.at[h0 + n], (spot, kappa + 2 * pack)))
                self.give_.append(send(other.at[rs], home_o.at[i, rs], sem_ref.at[o0 + n], sem_ref.at[h0 + n], (spot, kappa + 2 * (1 - pack))))
            here = pl.ds(pl.multiple_of(dp * block, block), block)
            self.go_, self.stay_, self.got_ = [], [], []
            for a in range(n_dp):
                src_rows = home_o.at[i, a * block:(a + 1) * block]
                self.go_.append(send(src_rows, out.at[here], sem_ref.at[a0 + a], sem_ref.at[a1 + dp], (a, lane)))
                self.stay_.append(pltpu.make_async_copy(src_rows, out.at[here], sem_ref.at[a0 + a]))
                self.got_.append(send(src_rows, out.at[a * block:(a + 1) * block], sem_ref.at[a0 + a], sem_ref.at[a1 + a], (a, lane)))

        def start(self, n):
            pl.when(is_far)(lambda: self.up_[n].start())

        def merge(self, n):
            rs = slice(n * cut, (n + 1) * cut)

            def work():
                self.up_[n].wait_recv()
                on = held.slots(n * cut, cut, 0) >= held.cut
                mine, theirs = self.src[rs, :].astype(F32), zin[self.i, rs].astype(F32)
                self.same[rs, :] = jnp.where(on, theirs, mine).astype(BF)
                self.other[rs, :] = jnp.where(on, mine, theirs).astype(BF)
                self.keep_[n].start()
                self.give_[n].start()

            pl.when(is_near)(work)

        def home(self, n):
            self.keep_[n].wait_recv()
            for a in range(n * cut // block, (n + 1) * cut // block):
                pl.when(dp != a)(lambda: self.go_[a].start())
                pl.when(dp == a)(lambda: self.stay_[a].start())

        def sent(self):
            for n in range(DEAL_CUTS):
                pl.when(is_far)(lambda: self.up_[n].wait_send())

                def both(n=n):
                    self.keep_[n].wait_send()
                    self.give_[n].wait_send()

                pl.when(is_near)(both)

        def finish(self):
            for a in range(n_dp):
                pl.when(dp == a)(lambda: self.stay_[a].wait())

                def other(a=a):
                    self.go_[a].wait_send()
                    self.got_[a].wait_recv()

                pl.when(dp != a)(other)

    res_back = Back(0, res, dqkv.at[0:rows, 0:d], dqkv.at[rows:2 * rows, 0:d], out_o)
    grad_back = Back(1, h, act.at[0:rows, 0:d], act.at[rows:2 * rows, 0:d], ig_o)

    fls, sls, tls = (None, fl1, fl2, fl3), (None, sl1, sl2, sl3), (tl3, tl1, tl2, tl3)

    def first_place(g, i, k):
        w = widths[g]
        if g:
            return fls[g].at[i, :, k * w:(k + 1) * w]
        at = per * (2 * i + k // 2)
        return act.at[at:at + per, d + (k % 2) * w:d + (k % 2 + 1) * w]

    def second_place(g, k):
        w = widths[g]
        return sls[g].at[:, k * w:(k + 1) * w] if g else xmid.at[per * k:per * (k + 1), d // 2:d // 2 + w]

    def area(g, q, k):
        w = widths[g]
        return mats[g].at[per * q:per * (q + 1), k * w:(k + 1) * w]

    def first_pair(g, k):
        side = 1 if k < 2 else 2
        return [remote(area(g, q, k), first_place(g, i, k), (dp ^ (2 * side), lane)) for i, q in enumerate((3, side))]

    firsts = [[first_pair(g, k) for k in range(LANES)] for g in range(n_g)]
    seconds = [[remote(area(g, 2 if k < 2 else 1, k), second_place(g, k), (dp ^ (4 if k < 2 else 2), lane)) for k in range(LANES)]
               for g in range(n_g)]
    turns = [[None] + [remote(area(g, 0, k), tls[g].at[k - 1, :, 0:widths[g]], (dp, lax.rem(lane + LANES - k, LANES))) for k in range(1, LANES)]
             for g in range(n_g)]
    lasts = [remote(thirds[g].at[0], thirds[g].at[1], mate) for g in range(n_g)]

    def pass_on(g, k):
        firsts[g][k][0].wait_recv()
        here = area(g, 2 if k < 2 else 1, k)
        here[...] = (here[...].astype(F32) + first_place(g, 0, k)[...].astype(F32)).astype(BF)
        seconds[g][k].start()

    def settle(g, k):
        firsts[g][k][1].wait_recv()
        seconds[g][k].wait_recv()
        here = area(g, 0, k)
        here[...] = (here[...].astype(F32) + first_place(g, 1, k)[...].astype(F32) + second_place(g, k)[...].astype(F32)).astype(BF)
        if k:
            turns[g][k].start()

    out_copies = []

    def put(src, dst):
        c = local(src, dst)
        c.start()
        out_copies.append(c)

    mine = pl.ds(pl.multiple_of(core * wd, wd), wd)
    theirs = pl.ds(pl.multiple_of((1 - core) * wd, wd), wd)

    def lay(g, half, value):
        w = widths[g]
        if g == 3:
            tall[pl.ds(pl.multiple_of(half * w, w), w), :] = jnp.transpose(value)
        elif g == 1:
            wide_o[pl.ds(pl.multiple_of(half * w, w), w), :] = jnp.transpose(value)
        elif g == 2:
            attn[0:wd, pl.ds(pl.multiple_of(half * w, w), w)] = value
        else:
            for t in range(3):
                attn[wd * (t + 1):wd * (t + 2), pl.ds(pl.multiple_of(half * (w // 3), w // 3), w // 3)] = value[:, t * (w // 3):(t + 1) * (w // 3)]

    def total(g):
        w = widths[g]
        for k in range(1, LANES):
            turns[g][k].wait_recv()

        def add(rs):
            v = mats[g][rs, 0:w].astype(F32)
            for k in range(LANES - 1):
                v = v + tls[g][k, rs, 0:w].astype(F32)
            return v

        thirds[g][0] = add(theirs).astype(BF)
        lasts[g].start()
        lay(g, core, add(mine))

    def close(g):
        lasts[g].wait_recv()
        lay(g, 1 - core, thirds[g][1].astype(F32))
        if g == 3:
            put(tall, w2_o)
        elif g == 1:
            put(wide_o, wo_o)
        elif g == 2:
            put(attn.at[0:wd, 0:2 * widths[2]], w1_o)
        else:
            for t in range(3):
                put(attn.at[wd * (t + 1):wd * (t + 2), 0:2 * widths[1]], qkv_o.at[t])

    def blocks(g, a, b, q):
        w = widths[g]

        def one(k, carry):
            cols = pl.ds(pl.multiple_of(k * w, w), w)
            mats[g][per * q:per * (q + 1), cols] = dot_g(a[:, per * q:per * (q + 1)], b[:, cols]).astype(BF)
            return carry

        lax.fori_loop(0, LANES, one, 0)

    def grads(g, a, b, between=None):
        for q in (3, 1, 2, 0):
            blocks(g, a, b, q)
            if between:
                between(q)
            if q:
                for k in range(LANES):
                    if q == 3:
                        firsts[g][k][0].start()
                    elif (q == 1) == (k < 2):
                        firsts[g][k][1].start()

    def join(x, size, n):
        c = remote(x.at[n * size:(n + 1) * size, 0:d], x.at[rows + n * size:rows + (n + 1) * size, 0:d], mate)
        c.start()
        ends.pop()
        return c

    def fold(which, term, before=()):
        copies = []
        size = rows // 2
        for n in range(2):
            if before:
                before[n].wait_send()
            sbuf[n * size:(n + 1) * size] = term(slice(rows + n * size, rows + (n + 1) * size)).astype(BF)
            c = remote(sbuf.at[n * size:(n + 1) * size], rbuf.at[which, n * size:(n + 1) * size], mate)
            c.start()
            copies.append(c)
            if not before:
                ends.pop()
        for n in range(2):
            rs = slice(n * size, (n + 1) * size)
            part[rs, :] = term(rs)
        return copies

    loads["res"].wait()
    for n in range(DEAL_CUTS):
        res_back.start(n)
    loads["ffn"].wait()
    loads["grd"].wait()
    half = rows // 2
    joins = []

    def chunk(n, m):
        return pl.ds(pl.multiple_of(n * half + m * cut, cut), cut)

    for n in range(2):

        def norm_3(m, carry, n=n):
            rs = chunk(n, m)
            g = grd[rs, :].astype(F32)
            dx, gx = norm_back_rows(part[rs, :], g, gains(3))
            low = dx.astype(BF)
            dfull[rs, :] = low
            sums[3:4, :] += column_sums(gx)
            sums[7:8, :] += column_sums(g)
            sums[9:10, :] += column_sums(low.astype(F32))
            return carry

        lax.fori_loop(0, half // cut, norm_3, 0)
        joins.append(join(dfull, half, n))
    loads["w2"].wait()
    loads["dg"].wait()
    for c in joins:
        c.wait_recv()
    w = widths[2]
    for k in range(LANES):
        cols = slice(k * w, (k + 1) * w)

        def hidden_units(r, carry, cols=cols, k=k):
            rs = pl.ds(pl.multiple_of(r * QB, QB), QB)
            low = (jnp.dot(dfull[rs, :], w2[:, cols], preferred_element_type=F32) * dg[rs, cols].astype(F32)).astype(BF)
            dg[rs, cols] = low
            sums[16 + k:17 + k, 0:w] += column_sums(low.astype(F32))
            return carry

        lax.fori_loop(0, 2 * rows // QB, hidden_units, 0)
    loads["act"].wait()
    res_back.merge(0)
    res_back.merge(1)

    def rows_back(q):
        if q == 3:
            res_back.merge(2)
        elif q == 1:
            res_back.merge(3)
        elif q == 2:
            res_back.home(0)
            res_back.home(1)

    grads(3, dfull, act, rows_back)
    for c in joins:
        c.wait_send()
    loads["xin"].start()
    res_back.sent()
    loads["h"].start()
    loads["w1"].wait()
    copies = fold(0, lambda rs: dot_t(dg[rs, :], w1[...]))
    res_back.home(2)
    res_back.home(3)
    for k in range(LANES):
        pass_on(3, k)
    loads["xmid"].wait()
    grads(2, xmid, dg)
    for side in (2, 4):
        pl.semaphore_signal(room, inc=1, device_id=(dp ^ side, lane), device_id_type=MESH)
    loads["first"].wait()
    loads["attn"].wait()
    joins = []
    for n in range(2):
        copies[n].wait_recv()

        def middle(m, carry, n=n):
            rs = chunk(n, m)
            g = part[rs, :] + rbuf[0, rs].astype(F32)
            dx, gx = norm_back_rows(first[rs, :], g, gains(2))
            sums[2:3, :] += column_sums(gx)
            sums[6:7, :] += column_sums(g)
            f = grd[rs, :].astype(F32) + dx
            first[rs, :] = f
            dx, gx = norm_back_rows(attn[rs, :], f, gains(1))
            sums[1:2, :] += column_sums(gx)
            sums[5:6, :] += column_sums(f)
            low = dx.astype(BF)
            dqkv[rs, 0:d] = low
            sums[8:9, :] += column_sums(low.astype(F32))
            return carry

        lax.fori_loop(0, half // cut, middle, 0)
        joins.append(join(dqkv, half, n))
    loads["wo"].wait()
    loads["heads"].wait()
    for c in joins:
        c.wait_recv()
    width = heads.shape[1]

    def to_heads(r, carry):
        rs = pl.ds(pl.multiple_of(r * QB, QB), QB)
        xmid[rs, 0:width] = jnp.dot(dqkv[rs, 0:d], wo[...], preferred_element_type=F32).astype(BF)
        return carry

    lax.fori_loop(0, 2 * rows // QB, to_heads, 0)
    grads(1, dqkv, heads)
    for c in joins:
        c.wait_send()
    loads["qkv"].wait()
    loads["lse"].wait()
    def settle_all(g):
        for k in (1, 2, 3, 0):
            settle(g, k)

    def pass_all(g):
        for k in range(LANES):
            pass_on(g, k)

    def group_3():
        total(3)
        for k in range(1, LANES):
            pl.semaphore_signal(free, inc=1, device_id=(dp, lax.rem(lane + k, LANES)), device_id_type=MESH)

    events = [[lambda: settle_all(3)], [lambda: pass_all(2)], [group_3, lambda: pass_all(1)], []]
    loads["xin"].wait()
    loads["wq"].wait()
    proj = widths[0]
    kpos = held.places(0, 2 * rows, 1)
    for pair in range(width // PAIR):
        dkv[...] = jnp.zeros_like(dkv)

        def attend(i, carry, pair=pair):
            attn_back(i, pair, held, kpos, lse, xmid, qkv, dqkv, dkv)
            return carry

        lax.fori_loop(0, 2 * rows // QB, attend, 0)
        at = 3 * pair * PAIR
        dqkv[:, at + PAIR:at + 2 * PAIR] = dkv[0].astype(BF)
        dqkv[:, at + 2 * PAIR:at + 3 * PAIR] = dkv[1].astype(BF)
        if pair == 0:
            pl.semaphore_wait(room, 2)
        cols = slice(pair * proj, (pair + 1) * proj)
        for q in (3, 1 if pair < 2 else 2, 2 if pair < 2 else 1, 0):
            dg[per * q:per * (q + 1), cols] = dot_g(dfull[:, per * q:per * (q + 1)], dqkv[:, cols]).astype(BF)
            if q == 3:
                firsts[0][pair][0].start()
            elif (q == 1) == (pair < 2) and q:
                firsts[0][pair][1].start()
        for e in events[pair]:
            e()
    copies = fold(1, lambda rs: dot_t(dqkv[rs, :], wq[...]), copies)
    sums[10:12, :] += jnp.concatenate([column_sums(dqkv[:, 0:d].astype(F32)),
                                       jnp.concatenate([column_sums(dqkv[:, d:3 * d // 2].astype(F32)), jnp.zeros((1, d // 2), F32)], axis=1)], axis=0)
    loads["h"].wait()
    for n in range(2):
        copies[n].wait_recv()

        def start_rows(m, carry, n=n):
            rs = chunk(n, m)
            g = part[rs, :] + rbuf[1, rs].astype(F32)
            dx, gx = norm_back_rows(h[rs, :].astype(F32), g, gains(0))
            sums[0:1, :] += column_sums(gx)
            sums[4:5, :] += column_sums(g)
            f = first[rs, :] + dx
            for q in range(4):
                cols = pl.ds(pl.multiple_of((chip ^ q) * quarter, quarter), quarter)
                h[rs, cols] = f[:, q * quarter:(q + 1) * quarter].astype(BF)
            return carry

        lax.fori_loop(0, half // cut, start_rows, 0)
        for m in range(half // cut):
            grad_back.start(n * (half // cut) + m)
    vec_all[...] = jnp.zeros_like(vec_all)
    for q in range(4):
        cols = pl.ds(pl.multiple_of((chip ^ q) * quarter, quarter), quarter)
        vec_all[0:10, cols] = sums[0:10, q * quarter:(q + 1) * quarter]
    hw = widths[1]
    for k in range(LANES):
        owner = lax.rem(lane + LANES - k, LANES)
        cols = pl.ds(pl.multiple_of(owner * 2 * hw + core * hw, hw), hw)
        for row, t in ((10, 0), (11, 2)):
            at = (3 * k + t) * hw
            vec_all[row:row + 1, cols] = sums[10 + at // d:11 + at // d, at % d:at % d + hw]
        vec_all[pl.ds(12 + owner, 1), pl.ds(pl.multiple_of(core * w, w), w)] = sums[16 + k:17 + k, 0:w]
    partners = [mate, (dp ^ 2, lane), (dp ^ 4, lane), (dp, lane ^ 1), (dp, lane ^ 2)]
    rounds = [remote(vec_all, sums_in.at[i], partners[i]) for i in range(5)]

    def vec_round(i):
        rounds[i].wait()
        vec_all[...] = vec_all[...] + sums_in[i]
        if i < 4:
            rounds[i + 1].start()

    rounds[0].start()
    settle_all(2)
    vec_round(0)
    grad_back.merge(0)
    settle_all(1)
    close(3)
    vec_round(1)
    grad_back.merge(1)
    pass_on(0, 0)
    pass_on(0, 1)
    grad_back.merge(2)
    grad_back.home(0)
    vec_round(2)
    pass_on(0, 2)
    pass_on(0, 3)
    grad_back.merge(3)
    grad_back.home(1)
    vec_round(3)
    total(2)
    grad_back.home(2)
    total(1)
    grad_back.home(3)
    pl.semaphore_wait(free, LANES - 1)
    settle_all(0)
    vec_round(4)
    vec_o[...] = vec_all[...]
    close(2)
    close(1)
    total(0)
    close(0)
    res_back.finish()
    grad_back.sent()
    grad_back.finish()
    for c in out_copies:
        c.wait()
    for c in ends:
        if not any(c is r for r in rounds):
            c.wait_send()


def attn_back(i, pair, held, kpos, lse, grads, qkv, dqkv, dkv):
    begin = pl.multiple_of(i * QB, QB)
    rs = pl.ds(begin, QB)
    bias = held.bias(begin, kpos)
    lane = lax.broadcasted_iota(jnp.int32, (1, PAIR), 1)
    at = 3 * pair * PAIR
    query = qkv[rs, at:at + PAIR]
    key, value = qkv[:, at + PAIR:at + 2 * PAIR], qkv[:, at + 2 * PAIR:at + 3 * PAIR]
    grad = grads[rs, pair * PAIR:(pair + 1) * PAIR]
    dq = jnp.zeros(query.shape, F32)
    dk = jnp.zeros(key.shape, F32)
    dv = jnp.zeros(key.shape, F32)
    for side in range(2):
        mine = (lane >= side * DH) & (lane < (side + 1) * DH)
        piece = jnp.where(mine, query * 0.125, 0.0).astype(BF)
        gpart = jnp.where(mine, grad, jnp.zeros_like(grad))
        score = dot_t(piece, key) + bias
        index = pair * 2 + side
        prob = jnp.exp(score - lse[rs, index:index + 1])
        gprob = dot_t(gpart, value)
        inner = jnp.sum(prob * gprob, axis=-1, keepdims=True)
        gscore = (prob * (gprob - inner)).astype(BF)
        dq += jnp.dot(gscore, jnp.where(mine, key, jnp.zeros_like(key)), preferred_element_type=F32)
        dk += dot_g(gscore, piece)
        dv += dot_g(prob.astype(BF), gpart)
    dqkv[rs, at:at + PAIR] = (dq * 0.125).astype(BF)
    dkv[0] += dk
    dkv[1] += dv


def backward_call(widths, lengths, deal, ln_gain, saved):
    (wq, wo, w1, w2, h, xin, qkv, heads, lse, attn, first, xmid, act, dg, ffn, res, grd) = saved
    rows, d = h.shape
    per, wd = d // 4, d // 8
    shape, vm = jax.ShapeDtypeStruct, pltpu.VMEM
    like = lambda x: vm(x.shape, x.dtype)
    out = [shape((3, wd, 2 * widths[1]), F32), shape((2 * widths[1], wd), F32), shape((wd, 2 * widths[2]), F32), shape((2 * widths[3], wd), F32),
           shape((rows, d), BF), shape((rows, d), BF), shape((16, d), F32), shape((2, rows, d), BF), shape((8, 128), F32)]
    scratch = [like(x) for x in (wq, wo, w1, w2, ffn, grd, act, dg, xmid, first, attn, heads, qkv, lse, xin, h)]
    scratch += [vm(qkv.shape, BF), vm((2, 2 * rows, PAIR), F32), vm((rows, d), BF), vm((2, rows, d), BF), vm((2, rows, d), BF)]
    order = (3, 2, 1)
    scratch += [vm((2, per, LANES * widths[g]), BF) for g in order]
    scratch += [vm((per, LANES * widths[g]), BF) for g in order]
    scratch += [vm((LANES - 1, per, widths[g]), BF) for g in order]
    scratch += [vm((2, wd, w), BF) for w in widths]
    scratch += [vm((2 * widths[3], wd), F32), vm((2 * widths[1], wd), F32), vm((24, d), F32), vm((5, 16, d), F32), vm((16, d), F32), vm((8, d), F32),
                pltpu.SemaphoreType.REGULAR, pltpu.SemaphoreType.REGULAR, pltpu.SemaphoreType.DMA((BWD_SEMS,))]
    return pl.pallas_call(
        partial(backward_kernel, widths),
        in_specs=[SMEM, SMEM, IN_VMEM] + [ANY] * 17,
        out_specs=[ANY] * 6 + [IN_VMEM, ANY, IN_VMEM],
        out_shape=out,
        scratch_shapes=scratch,
        compiler_params=pltpu.CompilerParams(collective_id=2, has_side_effects=True, vmem_limit_bytes=67043328),
        name="backward",
    )(lengths, deal, ln_gain, *saved)


def feature_turn(x):
    n = lax.axis_size("dp") // 2
    chip = lax.axis_index("dp") // 2
    lead = x.shape[:-1]
    width = x.shape[-1] // n
    bits = n.bit_length() - 1
    y = x.reshape(lead + (2,) * bits + (width,))
    for b in range(bits):
        axis = len(lead) + bits - 1 - b
        y = jnp.where((chip >> b) & 1 == 1, jnp.flip(y, axis), y)
    return y.reshape(x.shape)


def body(tokens, cotangent, lengths, deal, w_qkv, w_o, w_1, w_2, b_qv, b_o, b_1, b_2, ln_gain, ln_bias):
    n_dp, lanes = lax.axis_size("dp"), lax.axis_size("tensor")
    dp, lane = lax.axis_index("dp"), lax.axis_index("tensor")
    core, chip = dp % 2, dp // 2
    rows = tokens.shape[0]
    both = ("dp", "tensor")
    near, far = deal_perms(n_dp)
    back_near, back_far = [(b, a) for a, b in near], [(b, a) for a, b in far]

    if n_dp == 8 and lanes == LANES:
        hw, fw = w_o.shape[0] // 2, w_1.shape[1] // 2
        widths = (3 * hw, hw, fw, fw)
        saved = forward_call(widths, tokens, cotangent, lengths, deal, w_qkv, w_o, w_1, w_2, b_qv, b_1[None], b_o[None], b_2[None], ln_gain, ln_bias)
        qkv_grad, out_grad, up_grad, down_grad, output, input_grad, vector, _, _ = backward_call(widths, lengths, deal, ln_gain, saved[:17])
        mine = lambda x: lax.dynamic_slice_in_dim(x.reshape(-1, lanes, x.shape[-1] // lanes), lane, 1, 1)[:, 0]
        bias_1_total = lax.dynamic_slice_in_dim(vector, 12 + lane, 1, 0)[0]
        return (output, input_grad, qkv_grad, out_grad, up_grad, down_grad, mine(vector[10:12]), vector[8], bias_1_total, vector[9],
                vector[0:4], vector[4:8])

    per = lengths.shape[0] // n_dp

    def pack_ends(pack):
        picked = lax.dynamic_slice_in_dim(deal, pack * per, per)
        lookup = picked[:, None] == jnp.arange(lengths.shape[0], dtype=jnp.int32)[None, :]
        lens = jnp.sum(jnp.where(lookup, lengths[None, :], 0), axis=1)
        ends = jnp.sum(jnp.where(jnp.arange(per)[:, None] >= jnp.arange(per)[None, :], lens[None, :], 0), axis=1)
        return ends, ends - lens, jnp.sum(jnp.where(lens == HALF, ends - lens, 0))

    half = lane % 2
    ends, starts, cut = pack_ends(chip * 2 + lane // 2)
    _, _, cut_home = pack_ends(dp)
    index = jnp.arange(rows, dtype=jnp.int32)
    slots = jnp.concatenate([core * rows + index, (1 - core) * rows + index])
    place = jnp.where(slots >= cut, slots + HALF * half, slots + HALF * (1 - half))
    seg_start = jnp.max(jnp.where(place[:, None] >= starts[None, :], starts[None, :], 0), axis=1)
    qpos, qstart, kpos = place[:, None], seg_start[:, None], place[None, :]
    keep = ((core * rows + index) >= cut)[:, None]
    keep_home = (((lane % 2) * rows + index) >= cut_home)[:, None]

    def deal_in(x):
        moved = lax.all_to_all(x, "dp", split_axis=0, concat_axis=0, tiled=True)
        return jnp.where(keep, lax.ppermute(moved, both, near), lax.ppermute(moved, both, far))

    def deal_out(x):
        moved = jnp.where(keep_home, lax.ppermute(x, both, back_near), lax.ppermute(x, both, back_far))
        return lax.all_to_all(moved, "dp", split_axis=0, concat_axis=0, tiled=True)

    def halves(x):
        w = x.shape[-1] // 2
        return (lax.dynamic_slice_in_dim(x, core * w, w, x.ndim - 1), lax.dynamic_slice_in_dim(x, (1 - core) * w, w, x.ndim - 1))

    qm, qo = halves(w_qkv)
    om, oo = halves(w_o.T)
    um, uo = halves(w_1)
    dm, do = halves(w_2.T)
    own = jnp.concatenate([qm[0], qm[1], qm[2], om, um, dm], axis=1)
    other = jnp.concatenate([qo[0], qo[1], qo[2], oo, uo, do], axis=1)
    hw, fw = om.shape[1], um.shape[1]
    widths = (3 * hw, hw, fw, fw)
    small = jnp.concatenate([halves(b_qv[0:1])[0], halves(b_qv[1:2])[0], halves(b_1[None])[0]], axis=1)
    small = jnp.concatenate([small, jnp.zeros((7, small.shape[1]), F32)])
    order = (lane - jnp.arange(lanes)) % lanes
    gain, shift = feature_turn(ln_gain), feature_turn(ln_bias)
    bias_o, bias_2 = feature_turn(b_o[None])[0], feature_turn(b_2[None])[0]

    def join(x):
        return jnp.concatenate([x, swap_dp(x, 1)], axis=0)

    def fold(x):
        return x[:rows] + swap_dp(x[rows:].astype(BF), 1).astype(F32)

    mm = partial(jnp.dot, preferred_element_type=F32)
    mm_t = lambda a, b: lax.dot_general(a, b, (((1,), (1,)), ((), ())), preferred_element_type=F32)
    mm_g = lambda a, b: lax.dot_general(a, b, (((0,), (0,)), ((), ())), preferred_element_type=F32)
    if True:
        blocks = gather_weights(own, other)
        wq, wo, w1, w2 = (weight_of(blocks, sum(widths[:i]), w) for i, w in enumerate(widths))
        smalls = jnp.take(lax.all_gather(small[0], "tensor"), order, axis=0)
        bias_q, bias_v, bias_1 = smalls[:, :hw], smalls[:, hw:2 * hw], smalls[:, 2 * hw:].reshape(-1)
        bias_qkv = jnp.concatenate([bias_q, jnp.zeros_like(bias_q), bias_v], axis=1).reshape(-1)
        hidden = feature_turn(deal_in(tokens)).astype(F32)
        normed_in = join(scaled_norm(hidden, gain[0], shift[0]).astype(BF))
        qkv = (mm(normed_in, wq) + bias_qkv).astype(BF)
        heads_out, lse = attn_forward(qpos, qstart, kpos, qkv)
        attn_out = fold(mm_t(heads_out, wo)) + bias_o
        first_sum = hidden + scaled_norm(attn_out, gain[1], shift[1])
        normed_mid = join(scaled_norm(first_sum, gain[2], shift[2]).astype(BF))
        pre_act = mm(normed_mid, w1) + bias_1
        cdf = 0.5 + 0.5 * lax.erf(pre_act * 0.7071067811865476)
        act = (pre_act * cdf).astype(BF)
        dgelu = (cdf + pre_act * (0.3989422804014327 * jnp.exp(-0.5 * pre_act * pre_act))).astype(BF)
        ffn_out = fold(mm_t(act, w2)) + bias_2
        result = feature_turn((first_sum + scaled_norm(ffn_out, gain[3], shift[3])).astype(BF))
        grad_result = feature_turn(deal_in(cotangent)).astype(F32)

    grad_ffn, gain_3, shift_3 = norm_back(ffn_out, gain[3], shift[3], grad_result)
    grad_ffn_low = grad_ffn.astype(BF)
    bias_2_grad = jnp.sum(grad_ffn_low.astype(F32), axis=0)
    grad_ffn_full = join(grad_ffn_low)
    grad_act = mm(grad_ffn_full, w2)
    down_part = mm_g(grad_ffn_full, act).astype(BF)
    grad_pre = (grad_act * dgelu.astype(F32)).astype(BF)
    bias_1_grad = jnp.sum(grad_pre.astype(F32), axis=0)
    grad_mid = fold(mm_t(grad_pre, w1))
    up_part = mm_g(normed_mid, grad_pre).astype(BF)
    grad_first_part, gain_2, shift_2 = norm_back(first_sum, gain[2], shift[2], grad_mid)
    grad_first = grad_result + grad_first_part
    grad_attn, gain_1, shift_1 = norm_back(attn_out, gain[1], shift[1], grad_first)
    grad_attn_low = grad_attn.astype(BF)
    bias_o_grad = jnp.sum(grad_attn_low.astype(F32), axis=0)
    grad_attn_full = join(grad_attn_low)
    grad_heads = mm(grad_attn_full, wo).astype(BF)
    out_part = mm_g(grad_attn_full, heads_out).astype(BF)
    grad_qkv = attn_backward(qpos, qstart, kpos, lse, grad_heads, qkv)
    bias_qkv_grad = jnp.sum(grad_qkv.astype(F32), axis=0).reshape(lanes, 3, hw)
    grad_in = fold(mm_t(grad_qkv, wq))
    qkv_part = mm_g(normed_in, grad_qkv).astype(BF)
    grad_hidden_part, gain_0, shift_0 = norm_back(hidden, gain[0], shift[0], grad_in)
    grad_hidden = feature_turn((grad_first + grad_hidden_part).astype(BF))

    def by_lane(x):
        x = jnp.take(x.reshape(lanes, -1), order, axis=0)
        both_halves = jnp.stack([jnp.where(core == 0, x, 0.0), jnp.where(core == 1, x, 0.0)], axis=1)
        return both_halves.reshape(-1)

    d = tokens.shape[1]
    stack = jnp.stack([gain_0, gain_1, gain_2, gain_3, shift_0, shift_1, shift_2, shift_3, bias_o_grad, bias_2_grad])
    vector = jnp.concatenate([feature_turn(stack).reshape(-1), by_lane(bias_qkv_grad[:, 0]), by_lane(bias_qkv_grad[:, 2]), by_lane(bias_1_grad)])
    parts = [qkv_part, out_part, up_part, down_part]
    output, input_grad = deal_out(result), deal_out(grad_hidden)
    vector = lax.psum(vector, both)
    shards = [scatter_grads([p.astype(F32)]) for p in parts]
    gain_total, shift_total = vector[:4 * d].reshape(4, d), vector[4 * d:8 * d].reshape(4, d)
    bias_o_total, bias_2_total = vector[8 * d:9 * d], vector[9 * d:10 * d]
    mine = lambda x: lax.dynamic_slice_in_dim(x.reshape(lanes, -1), lane, 1, 0)[0]
    bias_qv_total = jnp.stack([mine(vector[10 * d:11 * d]), mine(vector[11 * d:12 * d])])
    bias_1_total = mine(vector[12 * d:])

    spread = lambda x: jnp.concatenate([x[0], x[1]], axis=-1)
    qkv_grad, out_grad, up_grad, down_grad = shards
    qkv_out = jnp.stack([spread(qkv_grad[:, :, i * hw:(i + 1) * hw]) for i in range(3)])
    return (
        output, input_grad, qkv_out, spread(out_grad).T, spread(up_grad), spread(down_grad).T,
        bias_qv_total, bias_o_total, bias_1_total, bias_2_total, gain_total, shift_total,
    )


def solution(mesh):
    rows = P(("dp", "tensor"), None)
    weights = (P(None, "dp", "tensor"), P("tensor", "dp"), P("dp", "tensor"), P("tensor", "dp"))
    vectors = (P(None, "tensor"), P(), P("tensor"), P(), P(), P())
    return jax.shard_map(
        body,
        mesh=mesh,
        in_specs=(rows, rows, P(), P()) + weights + vectors,
        out_specs=(rows, rows) + weights + vectors,
        check_vma=False,
    )
```

```python
from functools import partial

import jax
import jax.numpy as jnp
from jax import lax
from jax.experimental import pallas as pl
from jax.experimental.pallas import tpu as pltpu
from jax.sharding import PartitionSpec as P

DH = 64
HALF = 1024
NORM_EPS = 1e-05
MASKED_OUT = -1e30
BF, F32 = jnp.bfloat16, jnp.float32
QB = 256


def scaled_norm(values, norm_gain, norm_shift):
    peak = jnp.max(jnp.abs(values), axis=-1, keepdims=True) + NORM_EPS
    scaled = values / peak
    centred = scaled - jnp.mean(scaled, axis=-1, keepdims=True)
    spread = jnp.mean(centred * centred, axis=-1, keepdims=True)
    return centred * lax.rsqrt(spread + NORM_EPS) * norm_gain + norm_shift


def norm_back(values, norm_gain, norm_shift, row_grad):
    result, pull = jax.vjp(scaled_norm, values, norm_gain, norm_shift)
    return pull(row_grad)


PAIR = 2 * DH


def attn_fwd_kernel(qpos_ref, qstart_ref, kpos_ref, qkv_ref, o_ref, lse_ref):
    first = pl.multiple_of(pl.program_id(0) * QB, QB)
    kpos = kpos_ref[...]
    allowed = (kpos <= qpos_ref[...]) & (kpos >= qstart_ref[...])
    bias = jnp.where(allowed, 0.0, MASKED_OUT)
    lane = lax.broadcasted_iota(jnp.int32, (1, PAIR), 1)
    wide = lax.broadcasted_iota(jnp.int32, lse_ref.shape, 1)
    stats = jnp.zeros(lse_ref.shape, F32)
    for pair in range(o_ref.shape[1] // PAIR):
        at = 3 * pair * PAIR
        query = qkv_ref[pl.ds(first, QB), at:at + PAIR]
        key, value = qkv_ref[:, at + PAIR:at + 2 * PAIR], qkv_ref[:, at + 2 * PAIR:at + 3 * PAIR]
        total = jnp.zeros(query.shape, F32)
        for side in range(2):
            mine = (lane >= side * DH) & (lane < (side + 1) * DH)
            part = jnp.where(mine, query * 0.125, 0.0).astype(BF)
            score = lax.dot_general(part, key, (((1,), (1,)), ((), ())), preferred_element_type=F32) + bias
            peak = jnp.max(score, axis=-1, keepdims=True)
            expo = jnp.exp(score - peak)
            norm = jnp.sum(expo, axis=-1, keepdims=True)
            prob = (expo * (1.0 / norm)).astype(BF)
            total += jnp.dot(prob, jnp.where(mine, value, jnp.zeros_like(value)), preferred_element_type=F32)
            stats = jnp.where(wide == pair * 2 + side, peak + jnp.log(norm), stats)
        o_ref[:, pair * PAIR:(pair + 1) * PAIR] = total.astype(BF)
    lse_ref[...] = stats


def attn_forward(qpos, qstart, kpos, qkv):
    rows, width = qkv.shape[0], qkv.shape[1] // 3
    col = pl.BlockSpec((QB, 1), lambda i: (i, 0))
    full = pl.BlockSpec(qkv.shape, lambda i: (0, 0))
    return pl.pallas_call(
        attn_fwd_kernel,
        grid=(rows // QB,),
        in_specs=[col, col, pl.BlockSpec((1, rows), lambda i: (0, 0)), full],
        out_specs=[pl.BlockSpec((QB, width), lambda i: (i, 0)), pl.BlockSpec((QB, 128), lambda i: (i, 0))],
        out_shape=[jax.ShapeDtypeStruct((rows, width), BF), jax.ShapeDtypeStruct((rows, 128), F32)],
        cost_estimate=pl.CostEstimate(flops=4 * rows * rows * width, bytes_accessed=8 * rows * width, transcendentals=rows * rows * width // DH),
        compiler_params=pltpu.CompilerParams(vmem_limit_bytes=48 << 20),
        name="attn_fwd",
    )(qpos, qstart, kpos, qkv)


def attn_bwd_kernel(qpos_ref, qstart_ref, kpos_ref, lse_ref, g_ref, qkv_ref, d_ref, dk_acc, dv_acc):
    step = pl.program_id(0)
    first = pl.multiple_of(step * QB, QB)

    @pl.when(step == 0)
    def _():
        dk_acc[...] = jnp.zeros_like(dk_acc)
        dv_acc[...] = jnp.zeros_like(dv_acc)

    kpos = kpos_ref[...]
    allowed = (kpos <= qpos_ref[...]) & (kpos >= qstart_ref[...])
    bias = jnp.where(allowed, 0.0, MASKED_OUT)
    lane = lax.broadcasted_iota(jnp.int32, (1, PAIR), 1)
    for pair in range(g_ref.shape[1] // PAIR):
        at = 3 * pair * PAIR
        query = qkv_ref[pl.ds(first, QB), at:at + PAIR]
        key, value = qkv_ref[:, at + PAIR:at + 2 * PAIR], qkv_ref[:, at + 2 * PAIR:at + 3 * PAIR]
        cols = slice(pair * PAIR, (pair + 1) * PAIR)
        grad = g_ref[:, cols]
        dq = jnp.zeros(query.shape, F32)
        dk = jnp.zeros(key.shape, F32)
        dv = jnp.zeros(key.shape, F32)
        for side in range(2):
            mine = (lane >= side * DH) & (lane < (side + 1) * DH)
            part = jnp.where(mine, query * 0.125, 0.0).astype(BF)
            gpart = jnp.where(mine, grad, jnp.zeros_like(grad))
            score = lax.dot_general(part, key, (((1,), (1,)), ((), ())), preferred_element_type=F32) + bias
            index = pair * 2 + side
            prob = jnp.exp(score - lse_ref[:, index:index + 1])
            gprob = lax.dot_general(gpart, value, (((1,), (1,)), ((), ())), preferred_element_type=F32)
            inner = jnp.sum(prob * gprob, axis=-1, keepdims=True)
            gscore = (prob * (gprob - inner)).astype(BF)
            dq += jnp.dot(gscore, jnp.where(mine, key, jnp.zeros_like(key)), preferred_element_type=F32)
            dk += lax.dot_general(gscore, part, (((0,), (0,)), ((), ())), preferred_element_type=F32)
            dv += lax.dot_general(prob.astype(BF), gpart, (((0,), (0,)), ((), ())), preferred_element_type=F32)
        d_ref[pl.ds(first, QB), at:at + PAIR] = (dq * 0.125).astype(BF)
        dk_acc[:, cols] += dk
        dv_acc[:, cols] += dv

    @pl.when(step == pl.num_programs(0) - 1)
    def _():
        for pair in range(g_ref.shape[1] // PAIR):
            at = 3 * pair * PAIR
            cols = slice(pair * PAIR, (pair + 1) * PAIR)
            d_ref[:, at + PAIR:at + 2 * PAIR] = dk_acc[:, cols].astype(BF)
            d_ref[:, at + 2 * PAIR:at + 3 * PAIR] = dv_acc[:, cols].astype(BF)


def attn_backward(qpos, qstart, kpos, lse, grad, qkv):
    rows, width = grad.shape
    col = pl.BlockSpec((QB, 1), lambda i: (i, 0))
    full = pl.BlockSpec(qkv.shape, lambda i: (0, 0))
    return pl.pallas_call(
        attn_bwd_kernel,
        grid=(rows // QB,),
        in_specs=[col, col, pl.BlockSpec((1, rows), lambda i: (0, 0)), pl.BlockSpec((QB, 128), lambda i: (i, 0)),
                  pl.BlockSpec((QB, width), lambda i: (i, 0)), full],
        out_specs=full,
        out_shape=jax.ShapeDtypeStruct(qkv.shape, BF),
        scratch_shapes=[pltpu.VMEM((rows, width), F32), pltpu.VMEM((rows, width), F32)],
        cost_estimate=pl.CostEstimate(flops=10 * rows * rows * width, bytes_accessed=14 * rows * width, transcendentals=rows * rows * width // DH),
        compiler_params=pltpu.CompilerParams(vmem_limit_bytes=48 << 20),
        name="attn_bwd",
    )(qpos, qstart, kpos, lse, grad, qkv)


def swap_dp(x, bit):
    n = lax.axis_size("dp")
    return lax.ppermute(x, "dp", [(i, i ^ bit) for i in range(n)])


def turn(x, shift):
    n = lax.axis_size("tensor")
    return lax.ppermute(x, "tensor", [(i, (i + shift) % n) for i in range(n)])


def chip_bits():
    n = lax.axis_size("dp")
    return [1 << b for b in range(1, n.bit_length() - 1)]


def core_pair(mine, other):
    core = lax.axis_index("dp") % 2
    return jnp.where(core == 0, jnp.stack([mine, other]), jnp.stack([other, mine]))


def gather_weights(mine, other):
    pair = core_pair(mine, swap_dp(other, 1)).reshape(2 * mine.shape[0], mine.shape[1])
    lanes = lax.axis_size("tensor")
    column = jnp.stack([pair] + [turn(pair, k) for k in range(1, lanes)])
    bits = chip_bits()
    if len(bits) == 2:
        low, high = bits
        first, second = swap_dp(column, low), swap_dp(column, high)
        mid = lanes // 2
        far = jnp.concatenate([swap_dp(first[:mid], high), swap_dp(second[mid:], low)])
        return {0: column, low: first, high: second, low | high: far}
    blocks = {0: column}
    for bit in bits:
        got = swap_dp(jnp.stack([blocks[m] for m in sorted(blocks)]), bit)
        blocks.update({m | bit: got[i] for i, m in enumerate(sorted(blocks))})
    return blocks


def weight_of(blocks, start, width):
    out = []
    for mask in sorted(blocks):
        part = blocks[mask][:, :, start:start + width]
        out.append(jnp.concatenate([part[k] for k in range(part.shape[0])], axis=1))
    return jnp.concatenate(out, axis=0)


def scatter_grads(parts):
    lanes = lax.axis_size("tensor")
    bits = chip_bits()
    count = 1 << len(bits)
    feats = parts[0].shape[0]
    per = feats // count

    def block(mask_index, k):
        cut = []
        for p in parts:
            w = p.shape[1] // lanes
            cut.append(p[mask_index * per:(mask_index + 1) * per, k * w:(k + 1) * w])
        return jnp.concatenate(cut, axis=1) if len(cut) > 1 else cut[0]

    def col(mask_index, ks):
        return jnp.stack([block(mask_index, k) for k in ks])

    if len(bits) == 2:
        low, high = bits
        mid = lanes // 2
        ka, kb = list(range(mid)), list(range(mid, lanes))
        sent_a = jnp.stack([col(1, ka), col(3, ka)]).astype(BF)
        sent_b = jnp.stack([col(2, kb), col(3, kb)]).astype(BF)
        got_a, got_b = swap_dp(sent_a, low), swap_dp(sent_b, high)
        pass_a = (col(2, ka) + got_a[1].astype(F32)).astype(BF)
        pass_b = (col(1, kb) + got_b[1].astype(F32)).astype(BF)
        end_a, end_b = swap_dp(pass_a, high), swap_dp(pass_b, low)
        keep_a = col(0, ka) + got_a[0].astype(F32) + end_a.astype(F32)
        keep_b = col(0, kb) + got_b[0].astype(F32) + end_b.astype(F32)
        total = [keep_a[i] for i in range(mid)] + [keep_b[i] for i in range(lanes - mid)]
    else:
        sums = {m: col(m, range(lanes)) for m in range(count)}
        for level in reversed(range(len(bits))):
            keys = [m for m in sorted(sums) if m >> level & 1]
            got = swap_dp(jnp.stack([sums[m] for m in keys]).astype(BF), bits[level])
            sums = {m ^ (1 << level): sums[m ^ (1 << level)] + got[i].astype(F32) for i, m in enumerate(keys)}
        total = [sums[0][k] for k in range(lanes)]
    own = total[0]
    for k in range(1, lanes):
        own = own + turn(total[k].astype(BF), -k).astype(F32)
    rows = own.shape[0] // 2
    core = lax.axis_index("dp") % 2
    mine = lax.dynamic_slice_in_dim(own, core * rows, rows, 0)
    other = lax.dynamic_slice_in_dim(own, (1 - core) * rows, rows, 0)
    return core_pair(mine, swap_dp(other.astype(BF), 1).astype(F32))


def deal_perms(n_dp):
    near, far = [], []
    for chip in range(n_dp // 2):
        for c in range(2):
            for j in range(4):
                source = (chip * 2 + c) * 4 + j
                near.append((source, (chip * 2 + j % 2) * 4 + 2 * c + j // 2))
                far.append((source, (chip * 2 + j % 2) * 4 + 2 * c + 1 - j // 2))
    return near, far


MESH = pl.DeviceIdType.MESH
LANES = 4
ANY = pl.BlockSpec(memory_space=pl.ANY)
IN_VMEM = pl.BlockSpec(memory_space=pltpu.VMEM)


def greet(dp, lane, n_dp):
    barrier = pltpu.get_barrier_semaphore()
    count = 0
    for d in range(1, n_dp):
        pl.semaphore_signal(barrier, inc=1, device_id=(dp ^ d, lane), device_id_type=MESH)
        count += 1
    for k in range(1, LANES):
        for c in range(2):
            pl.semaphore_signal(barrier, inc=1, device_id=(dp ^ c, lax.rem(lane + k, LANES)), device_id_type=MESH)
            count += 1
    return barrier, count


def send(src, dst, send_sem, recv_sem, device):
    return pltpu.make_async_remote_copy(src_ref=src, dst_ref=dst, send_sem=send_sem, recv_sem=recv_sem, device_id=device, device_id_type=MESH)


DEAL_CUTS = 4
SMEM = pl.BlockSpec(memory_space=pltpu.SMEM)


class Pack:
    def __init__(self, lengths, deal, dp, lane, rows):
        core = dp % 2
        per = lengths.shape[0] // 8
        first = ((dp // 2) * 2 + lane // 2) * per
        self.starts, end, self.cut = [], 0, 0
        for j in range(per):
            size = lengths[deal[first + j]]
            self.starts.append(end)
            self.cut = self.cut + jnp.where(size == HALF, end, 0)
            end = end + size
        self.half, self.offset, self.rows = lane % 2, core * rows, rows

    def slots(self, begin, count, axis):
        shape = (count, 1) if axis == 0 else (1, count)
        return (self.offset + begin + lax.broadcasted_iota(jnp.int32, shape, axis)) & (2 * self.rows - 1)

    def places(self, begin, count, axis):
        slot = self.slots(begin, count, axis)
        return slot + HALF * jnp.where(slot >= self.cut, self.half, 1 - self.half)

    def seen_from(self, places):
        out = jnp.zeros(places.shape, jnp.int32)
        for start in self.starts:
            out = jnp.maximum(out, jnp.where(places >= start, start, 0))
        return out

    def bias(self, begin, kpos):
        at = self.places(begin, QB, 0)
        return jnp.where((kpos <= at) & (kpos >= self.seen_from(at)), 0.0, MASKED_OUT)


def relative(vec, chip, sources):
    quarter = vec.shape[1] // 4
    for q in range(4):
        cols = pl.ds(pl.multiple_of((chip ^ q) * quarter, quarter), quarter)
        at = 0
        for src in sources:
            count = src.shape[0]
            vec[at:at + count, q * quarter:(q + 1) * quarter] = src[:, cols]
            at += count


def norm_parts(x):
    peak = jnp.max(jnp.abs(x), axis=-1, keepdims=True) + NORM_EPS
    u = x * (1.0 / peak)
    c = u - jnp.mean(u, axis=-1, keepdims=True)
    return c, lax.rsqrt(jnp.mean(c * c, axis=-1, keepdims=True) + NORM_EPS)


def norm_rows(x, gain, shift):
    c, r = norm_parts(x)
    return c * r * gain + shift


def dot_t(a, b):
    return lax.dot_general(a, b, (((1,), (1,)), ((), ())), preferred_element_type=F32)


class Sems:
    def __init__(self, ref):
        self.ref, self.used = ref, 0

    def take(self, count=1):
        self.used += count
        return self.used - count


FWD_SEMS = 320


def forward_kernel(widths, lengths, deal, w_qkv, w_o, w_1, w_2, b_qv, b_1, b_o, b_2, ln_gain, ln_bias, tok, cot, *rest):
    outs, rest = rest[:18], rest[18:]
    (wq_o, wo_o, w1_o, w2_o, h_o, xin_o, qkv_o, heads_o, lse_o, attn_o, first_o, xmid_o, act_o, dg_o, ffn_o, res_o, grd_o, small_o) = outs
    (wq, wo, w1, w2, moved, cand, h, xin, qkv, heads, lse, part, sbuf, rbuf, first, xmid, act, dg, stage, small_in, own, other, small, vec, sem_ref) = rest
    mats = (wq, wo, w1, w2)
    sems = Sems(sem_ref)
    dp, lane = lax.axis_index("dp"), lax.axis_index("tensor")
    n_dp = 8
    core, chip = dp % 2, dp // 2
    rows, d = tok.shape
    wd = own.shape[0]
    quarter = d // 4
    up = lax.rem(lane + 1, LANES)
    n_g = len(widths)
    mate = (dp ^ 1, lane)
    ends = []

    def local(src, dst):
        c = pltpu.make_async_copy(src, dst, sem_ref.at[sems.take()])
        return c

    def remote(src, dst, device):
        s, r = sems.take(), sems.take()
        c = send(src, dst, sem_ref.at[s], sem_ref.at[r], device)
        ends.append(c.wait_send)
        return c

    barrier, count = greet(dp, lane, n_dp)
    rows_of = lambda x: jnp.transpose(x.astype(F32)).astype(BF)
    for half, dst in ((core, own), (1 - core, other)):
        at = 0
        part_of = lambda w: pl.ds(pl.multiple_of(half * w, w), w)
        for t in range(3):
            dst[:, at:at + widths[1]] = w_qkv[t, :, part_of(widths[1])]
            at += widths[1]
        for src, w, turned in ((w_o, widths[1], True), (w_1, widths[2], False), (w_2, widths[3], True)):
            dst[:, at:at + w] = rows_of(src[part_of(w), :]) if turned else src[:, part_of(w)]
            at += w
    at = 0
    small[...] = jnp.zeros_like(small)
    for src, w in ((b_qv.at[0:1], widths[1]), (b_qv.at[1:2], widths[1]), (b_1, widths[2])):
        small[0:1, at:at + w] = src[:, pl.ds(pl.multiple_of(core * w, w), w)]
        at += w
    relative(vec, chip, (ln_gain, ln_bias, b_o, b_2))
    held = Pack(lengths, deal, dp, lane, rows)
    pl.semaphore_wait(barrier, count)
    block = rows // n_dp
    here = pl.ds(pl.multiple_of(dp * block, block), block)
    deals = []
    for i, src in enumerate((tok, cot)):
        stay = local(src.at[here], moved.at[i, here])
        copies = []
        for k in range(1, n_dp):
            there = pl.ds(pl.multiple_of((dp ^ k) * block, block), block)
            copies.append(remote(src.at[there], moved.at[i, here], (dp ^ k, lane)))
        deals.append((stay, copies))

    def deal_start(i):
        deals[i][0].start()
        for c in deals[i][1]:
            c.start()

    deal_start(0)
    feat = pl.ds(pl.multiple_of(core * wd, wd), wd)
    at, stays, pairs = 0, [], []
    for g, w in enumerate(widths):
        dst = mats[g].at[feat, 0:w]
        stays.append(local(own.at[:, at:at + w], dst))
        pairs.append(remote(other.at[:, at:at + w], dst, mate))
        stays[g].start()
        pairs[g].start()
        at += w
    n_s = small.shape[0]
    smalls = [remote(small, small_in.at[k], (dp, lax.rem(lane + k, LANES))) for k in range(1, LANES)]
    for c in smalls:
        c.start()
    small_in[0] = small[...]

    def area(g, q, k):
        w = widths[g]
        return mats[g].at[2 * wd * q:2 * wd * (q + 1), k * w:(k + 1) * w]

    turns = [[remote(area(g, 0, t), area(g, 0, t + 1), (dp, up)) for t in range(LANES - 1)] for g in range(n_g)]
    planes = [[[remote(area(g, 0, k), area(g, side, k), (dp ^ (2 * side), lane)) for side in (1, 2)] for k in range(LANES)] for g in range(n_g)]
    fars = []
    for g in range(n_g):
        fars.append([])
        for k in range(LANES):
            side, via = (1, 2) if k < LANES // 2 else (2, 1)
            fars[g].append(remote(area(g, side, k), area(g, 3, k), (dp ^ (2 * via), lane)))

    def plane(g, k):
        for c in planes[g][k]:
            c.start()

    def pair_in(g):
        stays[g].wait()
        pairs[g].wait_recv()
        turns[g][0].start()

    def turn_in(g, t):
        turns[g][t].wait_recv()
        if t < LANES - 2:
            turns[g][t + 1].start()

    def far_go(g, k):
        planes[g][k][0 if k < LANES // 2 else 1].wait_recv()
        fars[g][k].start()

    def all_in(g):
        for k in range(LANES):
            planes[g][k][1 if k < LANES // 2 else 0].wait_recv()
            fars[g][k].wait_recv()

    pack = lane // 2
    spot = chip * 2 + lane % 2
    to_near = (spot, core + 1)
    slot = jnp.where(lane // 2 == core, 1, 0)
    is_self = (lane == 3 * core) & (spot == dp)
    is_near = lane == pack + 1
    straight = core == pack
    split = jnp.where(jnp.logical_not(is_near) & jnp.logical_not(straight), 2 * HALF, held.cut)
    cut = rows // DEAL_CUTS

    class Route:
        def __init__(self, i):
            self.i = i
            a0, f0 = sems.take(DEAL_CUTS), sems.take(DEAL_CUTS)
            got = sems.take(2 * DEAL_CUTS)
            self.near, self.self_, self.hand, self.pick, self.wait0, self.wait1 = [], [], [], [], [], []
            for n in range(DEAL_CUTS):
                rs = slice(n * cut, (n + 1) * cut)
                src = moved.at[i, rs]
                last = (dp, 3 * pack)
                self.near.append(send(src, cand.at[i, slot, rs], sem_ref.at[a0 + n], sem_ref.at[got + n * 2 + slot], to_near))
                self.self_.append(pltpu.make_async_copy(src, cand.at[i, 0, rs], sem_ref.at[got + n * 2]))
                self.hand.append(send(cand.at[i, 0, rs], cand.at[i, 1, rs], sem_ref.at[f0 + n], sem_ref.at[got + n * 2 + 1], last))
                self.pick.append(send(stage.at[0, rs], cand.at[i, 1, rs], sem_ref.at[f0 + n], sem_ref.at[got + n * 2 + 1], last))
                self.wait0.append(send(src, cand.at[i, 0, rs], sem_ref.at[a0 + n], sem_ref.at[got + n * 2], to_near))
                self.wait1.append(send(src, cand.at[i, 1, rs], sem_ref.at[a0 + n], sem_ref.at[got + n * 2 + 1], to_near))

        def start(self):
            for n in range(DEAL_CUTS):
                self.near[n].start()
                pl.when(is_self)(lambda: self.self_[n].start())

        def arrive(self, n):
            pl.when(is_self)(lambda: self.self_[n].wait())
            pl.when(is_near)(lambda: self.wait0[n].wait_recv())
            pl.when(is_near & straight)(lambda: self.hand[n].start())
            self.wait1[n].wait_recv()

            def choose_far():
                rs = slice(n * cut, (n + 1) * cut)
                on = held.slots(n * cut, cut, 0) >= held.cut
                stage[0, rs] = jnp.where(on, cand[self.i, 1, rs].astype(F32), cand[self.i, 0, rs].astype(F32)).astype(BF)
                self.pick[n].start()

            pl.when(is_near & jnp.logical_not(straight))(choose_far)

        def finish(self, picked=True):
            for n in range(DEAL_CUTS):
                self.near[n].wait_send()
                pl.when(is_near & straight)(lambda: self.hand[n].wait_send())
                if picked:
                    pl.when(is_near & jnp.logical_not(straight))(lambda: self.pick[n].wait_send())

    routes = [Route(0), Route(1)]

    def deal_on(i):
        deals[i][0].wait()
        for c in deals[i][1]:
            c.wait_recv()
        routes[i].start()

    def choose(i, n):
        rs = slice(n * cut, (n + 1) * cut)
        on = held.slots(n * cut, cut, 0) >= split
        parts = []
        for q in range(4):
            cols = pl.ds(pl.multiple_of((chip ^ q) * quarter, quarter), quarter)
            parts.append(jnp.where(on, cand[i, 0, rs, cols].astype(F32), cand[i, 1, rs, cols].astype(F32)))
        return jnp.concatenate(parts, axis=1)

    out_copies = []

    def put(src, dst):
        c = local(src, dst)
        c.start()
        out_copies.append(c)

    early = (0, 1)

    def forward_on(groups, t):
        for g in groups:
            turn_in(g, t)
        for g in groups:
            plane(g, t + 1)

    for g in range(4):
        pair_in(g)
        if g < 3:
            plane(g, 0)
    forward_on(early, 0)
    forward_on((2,), 0)
    forward_on(early, 1)
    turn_in(3, 0)
    deal_on(0)
    forward_on((2,), 1)
    forward_on(early, 2)
    for k in range(LANES):
        for g in early:
            far_go(g, k)
    plane(3, 0)
    deal_start(1)
    joins = []

    def join_send(x, n, size):
        c = remote(x.at[n * size:(n + 1) * size], x.at[rows + n * size:rows + (n + 1) * size], mate)
        c.start()
        joins.append(c)

    gains = lambda i: vec[i:i + 1, :]
    for n in range(DEAL_CUTS):
        rs = slice(n * cut, (n + 1) * cut)
        routes[0].arrive(n)
        x = choose(0, n)
        h[rs, :] = x.astype(BF)
        xin[rs, :] = norm_rows(x, gains(0), gains(4)).astype(BF)
        join_send(xin, n, cut)
        if n == 1:
            forward_on((2,), 2)
        if n == 2:
            turn_in(3, 1)
    plane(3, 1)
    for c in smalls:
        c.wait_recv()
    all_in(0)
    for c in joins:
        c.wait_recv()
    put(wq, wq_o)
    put(h, h_o)
    put(xin, xin_o)
    w = widths[0]
    third = w // 3
    for k in range(LANES):
        cols = slice(k * w, (k + 1) * w)
        row = small_in[k, 0:1, :]
        bias = jnp.concatenate([row[:, 0:third], jnp.zeros((1, third), F32), row[:, third:2 * third]], axis=1)

        def project(r, carry, cols=cols, bias=bias):
            rs = pl.ds(pl.multiple_of(r * QB, QB), QB)
            qkv[rs, cols] = (jnp.dot(xin[rs, :], wq[:, cols], preferred_element_type=F32) + bias).astype(BF)
            return carry

        lax.fori_loop(0, 2 * rows // QB, project, 0)
        far_go(2, k)
    put(qkv, qkv_o)
    plane(3, 2)

    kpos = held.places(0, 2 * rows, 1)

    def beside(i):
        if i == 0:
            deal_on(1)
        elif i == 1:
            forward_on((3,), 2)
        elif i == 2:
            far_go(3, 0)
            far_go(3, 1)

    def attend(i, carry):
        begin = pl.multiple_of(i * QB, QB)
        attn_block(pl.ds(begin, QB), held.bias(begin, kpos), qkv, heads, lse)
        for n in range(3):
            pl.when(i == n)(lambda: beside(n))
        return carry

    lax.fori_loop(0, 2 * rows // QB, attend, 0)
    put(heads, heads_o)
    put(lse, lse_o)
    all_in(1)
    put(wo, wo_o)

    def fold(x, w_ref, which):
        copies = []
        per = 2
        size = rows // per
        for n in range(per):
            rs = slice(rows + n * size, rows + (n + 1) * size)
            sbuf[which, n * size:(n + 1) * size] = dot_t(x[rs, :], w_ref[...]).astype(BF)
            c = remote(sbuf.at[which, n * size:(n + 1) * size], rbuf.at[which, n * size:(n + 1) * size], mate)
            c.start()
            copies.append(c)
        for n in range(per):
            rs = slice(n * size, (n + 1) * size)
            part[rs, :] = dot_t(x[rs, :], w_ref[...])
        return copies

    copies = fold(heads, wo, 0)
    joins.clear()
    size = rows // 2
    for n in range(2):
        copies[n].wait_recv()

        def middle(m, carry, n=n):
            rs = pl.ds(pl.multiple_of(n * size + m * cut, cut), cut)
            y = part[rs, :] + rbuf[0, rs].astype(F32) + gains(8)
            part[rs, :] = y
            f = h[rs, :].astype(F32) + norm_rows(y, gains(1), gains(5))
            first[rs, :] = f
            xmid[rs, :] = norm_rows(f, gains(2), gains(6)).astype(BF)
            return carry

        lax.fori_loop(0, size // cut, middle, 0)
        join_send(xmid, n, size)
    attn_put = local(part, attn_o)
    attn_put.start()
    put(first, first_o)
    all_in(2)
    put(w1, w1_o)
    for c in joins:
        c.wait_recv()
    put(xmid, xmid_o)
    w = widths[2]
    for k in range(LANES):
        cols = slice(k * w, (k + 1) * w)
        bias = small_in[k, 0:1, 2 * third:2 * third + w]

        def hidden_units(r, carry, cols=cols, bias=bias):
            rs = pl.ds(pl.multiple_of(r * QB, QB), QB)
            pre = jnp.dot(xmid[rs, :], w1[:, cols], preferred_element_type=F32) + bias
            cdf = 0.5 + 0.5 * lax.erf(pre * 0.7071067811865476)
            act[rs, cols] = (pre * cdf).astype(BF)
            dg[rs, cols] = (cdf + pre * (0.3989422804014327 * jnp.exp(-0.5 * pre * pre))).astype(BF)
            return carry

        lax.fori_loop(0, 2 * rows // QB, hidden_units, 0)
        if k < 2:
            far_go(3, k + 2)
        if k == 1:
            routes[0].finish()
        if k > 1:
            routes[1].arrive(2 * k - 4)
            routes[1].arrive(2 * k - 3)
    put(act, act_o)
    put(dg, dg_o)
    all_in(3)
    put(w2, w2_o)
    attn_put.wait()
    copies = fold(act, w2, 1)
    for n in range(DEAL_CUTS):
        rs = slice(n * cut, (n + 1) * cut)
        stage[1, rs] = choose(1, n).astype(BF)
    put(stage.at[1], grd_o)
    for n in range(DEAL_CUTS):
        pl.when(is_near & jnp.logical_not(straight))(lambda: routes[1].pick[n].wait_send())
    for n in range(2):
        copies[n].wait_recv()

        def last(m, carry, n=n):
            rs = pl.ds(pl.multiple_of(n * size + m * cut, cut), cut)
            y = part[rs, :] + rbuf[1, rs].astype(F32) + gains(9)
            part[rs, :] = y
            out = first[rs, :] + norm_rows(y, gains(3), gains(7))
            for q in range(4):
                cols = pl.ds(pl.multiple_of((chip ^ q) * quarter, quarter), quarter)
                stage[0, rs, cols] = out[:, q * quarter:(q + 1) * quarter].astype(BF)
            return carry

        lax.fori_loop(0, size // cut, last, 0)
    put(part, ffn_o)
    put(stage.at[0], res_o)
    put(small_in, small_o)
    for c in out_copies:
        c.wait()
    routes[1].finish(False)
    for wait in ends:
        wait()


def attn_block(rs, bias, qkv, heads, lse):
    lane = lax.broadcasted_iota(jnp.int32, (1, PAIR), 1)
    wide = lax.broadcasted_iota(jnp.int32, (QB, 128), 1)
    stats = jnp.zeros((QB, 128), F32)
    for pair in range(heads.shape[1] // PAIR):
        at = 3 * pair * PAIR
        query = qkv[rs, at:at + PAIR]
        key, value = qkv[:, at + PAIR:at + 2 * PAIR], qkv[:, at + 2 * PAIR:at + 3 * PAIR]
        total = jnp.zeros(query.shape, F32)
        for side in range(2):
            mine = (lane >= side * DH) & (lane < (side + 1) * DH)
            piece = jnp.where(mine, query * 0.125, 0.0).astype(BF)
            score = dot_t(piece, key) + bias
            peak = jnp.max(score, axis=-1, keepdims=True)
            expo = jnp.exp(score - peak)
            norm = jnp.sum(expo, axis=-1, keepdims=True)
            prob = (expo * (1.0 / norm)).astype(BF)
            total += jnp.dot(prob, jnp.where(mine, value, jnp.zeros_like(value)), preferred_element_type=F32)
            stats = jnp.where(wide == pair * 2 + side, peak + jnp.log(norm), stats)
        heads[rs, pair * PAIR:(pair + 1) * PAIR] = total.astype(BF)
    lse[rs, :] = stats


def forward_call(widths, tok, cot, lengths, deal, w_qkv, w_o, w_1, w_2, b_qv, b_1, b_o, b_2, ln_gain, ln_bias):
    rows, d = tok.shape
    both = 2 * rows
    vm = pltpu.VMEM
    hidden = LANES * widths[2]
    small = (8, 2 * widths[1] + widths[2])
    mats = [(d, LANES * w) for w in widths]
    shape = jax.ShapeDtypeStruct
    out = [shape(m, BF) for m in mats] + [
        shape((rows, d), BF), shape((both, d), BF), shape((both, LANES * widths[0]), BF), shape((both, LANES * widths[1]), BF), shape((both, 128), F32),
        shape((rows, d), F32), shape((rows, d), F32), shape((both, d), BF), shape((both, hidden), BF), shape((both, hidden), BF),
        shape((rows, d), F32), shape((rows, d), BF), shape((rows, d), BF), shape((LANES,) + small, F32)]
    scratch = [vm(m, BF) for m in mats] + [
        vm((2, rows, d), BF), vm((2, 2, rows, d), BF), vm((rows, d), BF), vm((both, d), BF), vm((both, LANES * widths[0]), BF),
        vm((both, LANES * widths[1]), BF), vm((both, 128), F32), vm((rows, d), F32), vm((2, rows, d), BF), vm((2, rows, d), BF),
        vm((rows, d), F32), vm((both, d), BF), vm((both, hidden), BF), vm((both, hidden), BF), vm((2, rows, d), BF),
        vm((LANES,) + small, F32), vm((d // 8, sum(widths)), BF), vm((d // 8, sum(widths)), BF), vm(small, F32), vm((16, d), F32),
        pltpu.SemaphoreType.DMA((FWD_SEMS,))]
    return pl.pallas_call(
        partial(forward_kernel, widths),
        in_specs=[SMEM, SMEM] + [IN_VMEM] * 10 + [ANY, ANY],
        out_specs=[ANY] * len(out),
        out_shape=out,
        scratch_shapes=scratch,
        compiler_params=pltpu.CompilerParams(collective_id=1, has_side_effects=True, vmem_limit_bytes=67043328),
        name="forward",
    )(lengths, deal, w_qkv, w_o, w_1, w_2, b_qv, b_1, b_o, b_2, ln_gain, ln_bias, tok, cot)


def norm_back_rows(x, grad, gain):
    mag = jnp.abs(x)
    top = jnp.max(mag, axis=-1, keepdims=True)
    inv = 1.0 / (top + NORM_EPS)
    u = x * inv
    c = u - jnp.mean(u, axis=-1, keepdims=True)
    r = lax.rsqrt(jnp.mean(c * c, axis=-1, keepdims=True) + NORM_EPS)
    xhat = c * r
    t = grad * gain
    gx = grad * xhat
    along = jnp.mean(t * xhat, axis=-1, keepdims=True)
    du = r * (t - jnp.mean(t, axis=-1, keepdims=True) - xhat * along)
    at_top = mag == top
    ties = jnp.sum(jnp.where(at_top, 1.0, 0.0), axis=-1, keepdims=True)
    pull = x.shape[-1] * NORM_EPS * along * r * r * inv / ties
    side = jnp.where(x > 0, -pull, jnp.where(x < 0, pull, 0.0))
    return du * inv + jnp.where(at_top, side, 0.0), gx


BWD_SEMS = 420


def dot_g(a, b):
    return lax.dot_general(a, b, (((0,), (0,)), ((), ())), preferred_element_type=F32)


def column_sums(x):
    return jnp.sum(x, axis=0, keepdims=True)


def backward_kernel(widths, lengths, deal, ln_gain, *rest):
    ins, rest = rest[:17], rest[17:]
    (wq_i, wo_i, w1_i, w2_i, h_i, xin_i, qkv_i, heads_i, lse_i, attn_i, first_i, xmid_i, act_i, dg_i, ffn_i, res_i, grd_i) = ins
    outs, rest = rest[:9], rest[9:]
    (qkv_o, wo_o, w1_o, w2_o, out_o, ig_o, vec_o, home_o, _) = outs
    (wq, wo, w1, w2, part, grd, act, dg, xmid, first, attn, heads, qkv, lse, dfull, res, dqkv, dkv, sbuf, rbuf, zin,
     fl3, fl2, fl1, sl3, sl2, sl1, tl3, tl2, tl1, third0, third1, third2, third3, tall, wide_o, sums, sums_in, vec_all, vec, room, free, sem_ref) = rest
    xin, h = dfull, res
    mats = (dg, wo, w1, w2)
    thirds = (third0, third1, third2, third3)
    n_g = len(widths)
    sems = Sems(sem_ref)
    dp, lane = lax.axis_index("dp"), lax.axis_index("tensor")
    n_dp = 8
    core, chip = dp % 2, dp // 2
    rows, d = grd.shape
    quarter = d // 4
    per = 2 * (d // n_dp)
    wd = d // n_dp
    mate = (dp ^ 1, lane)
    cut = rows // DEAL_CUTS
    ends = []

    def local(src, dst):
        return pltpu.make_async_copy(src, dst, sem_ref.at[sems.take()])

    def remote(src, dst, device):
        a, b = sems.take(), sems.take()
        c = send(src, dst, sem_ref.at[a], sem_ref.at[b], device)
        ends.append(c)
        return c

    loads = {}
    for name, src, dst in (("ffn", ffn_i, part), ("grd", grd_i, grd), ("res", res_i, res), ("w2", w2_i, w2), ("dg", dg_i, dg), ("act", act_i, act),
                           ("w1", w1_i, w1), ("xmid", xmid_i, xmid), ("first", first_i, first), ("attn", attn_i, attn), ("wo", wo_i, wo),
                           ("heads", heads_i, heads), ("qkv", qkv_i, qkv), ("lse", lse_i, lse), ("wq", wq_i, wq), ("xin", xin_i, xin), ("h", h_i, h)):
        loads[name] = local(src, dst)
        if name not in ("xin", "h"):
            loads[name].start()
    barrier, count = greet(dp, lane, n_dp)
    held = Pack(lengths, deal, dp, lane, rows)
    relative(vec, chip, (ln_gain,))
    pl.semaphore_wait(barrier, count)
    gains = lambda i: vec[i:i + 1, :]
    sums[...] = jnp.zeros_like(sums)
    pack = lane // 2
    is_near = lane == pack + 1
    is_far = lane == 3 * pack
    block = rows // n_dp

    class Back:
        def __init__(self, i, src, same, other, out):
            self.i, self.src, self.same, self.other = i, src, same, other
            self.out = out
            z0, z1, m0, o0, h0 = [sems.take(DEAL_CUTS) for _ in range(5)]
            a0, a1 = sems.take(n_dp), sems.take(n_dp)
            self.a0, self.a1 = a0, a1
            spot = chip * 2 + pack
            kappa = core
            self.up_, self.keep_, self.give_ = [], [], []
            for n in range(DEAL_CUTS):
                rs = slice(n * cut, (n + 1) * cut)
                self.up_.append(send(src.at[rs], zin.at[i, rs], sem_ref.at[z0 + n], sem_ref.at[z1 + n], (dp, pack + 1)))
                self.keep_.append(send(same.at[rs], home_o.at[i, rs], sem_ref.at[m0 + n], sem_ref.at[h0 + n], (spot, kappa + 2 * pack)))
                self.give_.append(send(other.at[rs], home_o.at[i, rs], sem_ref.at[o0 + n], sem_ref.at[h0 + n], (spot, kappa + 2 * (1 - pack))))
            here = pl.ds(pl.multiple_of(dp * block, block), block)
            self.go_, self.stay_, self.got_ = [], [], []
            for a in range(n_dp):
                src_rows = home_o.at[i, a * block:(a + 1) * block]
                self.go_.append(send(src_rows, out.at[here], sem_ref.at[a0 + a], sem_ref.at[a1 + dp], (a, lane)))
                self.stay_.append(pltpu.make_async_copy(src_rows, out.at[here], sem_ref.at[a0 + a]))
                self.got_.append(send(src_rows, out.at[a * block:(a + 1) * block], sem_ref.at[a0 + a], sem_ref.at[a1 + a], (a, lane)))

        def start(self, n):
            pl.when(is_far)(lambda: self.up_[n].start())

        def merge(self, n):
            rs = slice(n * cut, (n + 1) * cut)

            def work():
                self.up_[n].wait_recv()
                on = held.slots(n * cut, cut, 0) >= held.cut
                mine, theirs = self.src[rs, :].astype(F32), zin[self.i, rs].astype(F32)
                self.same[rs, :] = jnp.where(on, theirs, mine).astype(BF)
                self.other[rs, :] = jnp.where(on, mine, theirs).astype(BF)
                self.keep_[n].start()
                self.give_[n].start()

            pl.when(is_near)(work)

        def home(self, n):
            self.keep_[n].wait_recv()
            for a in range(n * cut // block, (n + 1) * cut // block):
                pl.when(dp != a)(lambda: self.go_[a].start())
                pl.when(dp == a)(lambda: self.stay_[a].start())

        def sent(self):
            for n in range(DEAL_CUTS):
                pl.when(is_far)(lambda: self.up_[n].wait_send())

                def both(n=n):
                    self.keep_[n].wait_send()
                    self.give_[n].wait_send()

                pl.when(is_near)(both)

        def finish(self):
            for a in range(n_dp):
                pl.when(dp == a)(lambda: self.stay_[a].wait())

                def other(a=a):
                    self.go_[a].wait_send()
                    self.got_[a].wait_recv()

                pl.when(dp != a)(other)

    res_back = Back(0, res, dqkv.at[0:rows, 0:d], dqkv.at[rows:2 * rows, 0:d], out_o)
    grad_back = Back(1, h, act.at[0:rows, 0:d], act.at[rows:2 * rows, 0:d], ig_o)

    fls, sls, tls = (None, fl1, fl2, fl3), (None, sl1, sl2, sl3), (tl3, tl1, tl2, tl3)

    def first_place(g, i, k):
        w = widths[g]
        if g:
            return fls[g].at[i, :, k * w:(k + 1) * w]
        at = per * (2 * i + k // 2)
        return act.at[at:at + per, d + (k % 2) * w:d + (k % 2 + 1) * w]

    def second_place(g, k):
        w = widths[g]
        return sls[g].at[:, k * w:(k + 1) * w] if g else xmid.at[per * k:per * (k + 1), d // 2:d // 2 + w]

    def area(g, q, k):
        w = widths[g]
        return mats[g].at[per * q:per * (q + 1), k * w:(k + 1) * w]

    def first_pair(g, k):
        side = 1 if k < 2 else 2
        return [remote(area(g, q, k), first_place(g, i, k), (dp ^ (2 * side), lane)) for i, q in enumerate((3, side))]

    firsts = [[first_pair(g, k) for k in range(LANES)] for g in range(n_g)]
    seconds = [[remote(area(g, 2 if k < 2 else 1, k), second_place(g, k), (dp ^ (4 if k < 2 else 2), lane)) for k in range(LANES)]
               for g in range(n_g)]
    turns = [[None] + [remote(area(g, 0, k), tls[g].at[k - 1, :, 0:widths[g]], (dp, lax.rem(lane + LANES - k, LANES))) for k in range(1, LANES)]
             for g in range(n_g)]
    lasts = [remote(thirds[g].at[0], thirds[g].at[1], mate) for g in range(n_g)]

    def pass_on(g, k):
        firsts[g][k][0].wait_recv()
        here = area(g, 2 if k < 2 else 1, k)
        here[...] = (here[...].astype(F32) + first_place(g, 0, k)[...].astype(F32)).astype(BF)
        seconds[g][k].start()

    def settle(g, k):
        firsts[g][k][1].wait_recv()
        seconds[g][k].wait_recv()
        here = area(g, 0, k)
        here[...] = (here[...].astype(F32) + first_place(g, 1, k)[...].astype(F32) + second_place(g, k)[...].astype(F32)).astype(BF)
        if k:
            turns[g][k].start()

    out_copies = []

    def put(src, dst):
        c = local(src, dst)
        c.start()
        out_copies.append(c)

    mine = pl.ds(pl.multiple_of(core * wd, wd), wd)
    theirs = pl.ds(pl.multiple_of((1 - core) * wd, wd), wd)

    def lay(g, half, value):
        w = widths[g]
        if g == 3:
            tall[pl.ds(pl.multiple_of(half * w, w), w), :] = jnp.transpose(value)
        elif g == 1:
            wide_o[pl.ds(pl.multiple_of(half * w, w), w), :] = jnp.transpose(value)
        elif g == 2:
            attn[0:wd, pl.ds(pl.multiple_of(half * w, w), w)] = value
        else:
            for t in range(3):
                attn[wd * (t + 1):wd * (t + 2), pl.ds(pl.multiple_of(half * (w // 3), w // 3), w // 3)] = value[:, t * (w // 3):(t + 1) * (w // 3)]

    def total(g):
        w = widths[g]
        for k in range(1, LANES):
            turns[g][k].wait_recv()

        def add(rs):
            v = mats[g][rs, 0:w].astype(F32)
            for k in range(LANES - 1):
                v = v + tls[g][k, rs, 0:w].astype(F32)
            return v

        thirds[g][0] = add(theirs).astype(BF)
        lasts[g].start()
        lay(g, core, add(mine))

    def close(g):
        lasts[g].wait_recv()
        lay(g, 1 - core, thirds[g][1].astype(F32))
        if g == 3:
            put(tall, w2_o)
        elif g == 1:
            put(wide_o, wo_o)
        elif g == 2:
            put(attn.at[0:wd, 0:2 * widths[2]], w1_o)
        else:
            for t in range(3):
                put(attn.at[wd * (t + 1):wd * (t + 2), 0:2 * widths[1]], qkv_o.at[t])

    def blocks(g, a, b, q):
        w = widths[g]

        def one(k, carry):
            cols = pl.ds(pl.multiple_of(k * w, w), w)
            mats[g][per * q:per * (q + 1), cols] = dot_g(a[:, per * q:per * (q + 1)], b[:, cols]).astype(BF)
            return carry

        lax.fori_loop(0, LANES, one, 0)

    def grads(g, a, b, between=None):
        for q in (3, 1, 2, 0):
            blocks(g, a, b, q)
            if between:
                between(q)
            if q:
                for k in range(LANES):
                    if q == 3:
                        firsts[g][k][0].start()
                    elif (q == 1) == (k < 2):
                        firsts[g][k][1].start()

    def join(x, size, n):
        c = remote(x.at[n * size:(n + 1) * size, 0:d], x.at[rows + n * size:rows + (n + 1) * size, 0:d], mate)
        c.start()
        ends.pop()
        return c

    def fold(which, term, before=()):
        copies = []
        size = rows // 2
        for n in range(2):
            if before:
                before[n].wait_send()
            sbuf[n * size:(n + 1) * size] = term(slice(rows + n * size, rows + (n + 1) * size)).astype(BF)
            c = remote(sbuf.at[n * size:(n + 1) * size], rbuf.at[which, n * size:(n + 1) * size], mate)
            c.start()
            copies.append(c)
            if not before:
                ends.pop()
        for n in range(2):
            rs = slice(n * size, (n + 1) * size)
            part[rs, :] = term(rs)
        return copies

    loads["res"].wait()
    for n in range(DEAL_CUTS):
        res_back.start(n)
    loads["ffn"].wait()
    loads["grd"].wait()
    half = rows // 2
    joins = []

    def chunk(n, m):
        return pl.ds(pl.multiple_of(n * half + m * cut, cut), cut)

    for n in range(2):

        def norm_3(m, carry, n=n):
            rs = chunk(n, m)
            g = grd[rs, :].astype(F32)
            dx, gx = norm_back_rows(part[rs, :], g, gains(3))
            low = dx.astype(BF)
            dfull[rs, :] = low
            sums[3:4, :] += column_sums(gx)
            sums[7:8, :] += column_sums(g)
            sums[9:10, :] += column_sums(low.astype(F32))
            return carry

        lax.fori_loop(0, half // cut, norm_3, 0)
        joins.append(join(dfull, half, n))
    loads["w2"].wait()
    loads["dg"].wait()
    for c in joins:
        c.wait_recv()
    w = widths[2]
    for k in range(LANES):
        cols = slice(k * w, (k + 1) * w)

        def hidden_units(r, carry, cols=cols, k=k):
            rs = pl.ds(pl.multiple_of(r * QB, QB), QB)
            low = (jnp.dot(dfull[rs, :], w2[:, cols], preferred_element_type=F32) * dg[rs, cols].astype(F32)).astype(BF)
            dg[rs, cols] = low
            sums[16 + k:17 + k, 0:w] += column_sums(low.astype(F32))
            return carry

        lax.fori_loop(0, 2 * rows // QB, hidden_units, 0)
    loads["act"].wait()
    res_back.merge(0)
    res_back.merge(1)

    def rows_back(q):
        if q == 3:
            res_back.merge(2)
        elif q == 1:
            res_back.merge(3)

    grads(3, dfull, act, rows_back)
    for c in joins:
        c.wait_send()
    loads["xin"].start()
    res_back.sent()
    loads["h"].start()
    loads["w1"].wait()
    copies = fold(0, lambda rs: dot_t(dg[rs, :], w1[...]))
    for k in range(LANES):
        pass_on(3, k)
    loads["xmid"].wait()
    grads(2, xmid, dg)
    for side in (2, 4):
        pl.semaphore_signal(room, inc=1, device_id=(dp ^ side, lane), device_id_type=MESH)
    loads["first"].wait()
    loads["attn"].wait()
    joins = []
    for n in range(2):
        copies[n].wait_recv()

        def middle(m, carry, n=n):
            rs = chunk(n, m)
            g = part[rs, :] + rbuf[0, rs].astype(F32)
            dx, gx = norm_back_rows(first[rs, :], g, gains(2))
            sums[2:3, :] += column_sums(gx)
            sums[6:7, :] += column_sums(g)
            f = grd[rs, :].astype(F32) + dx
            first[rs, :] = f
            dx, gx = norm_back_rows(attn[rs, :], f, gains(1))
            sums[1:2, :] += column_sums(gx)
            sums[5:6, :] += column_sums(f)
            low = dx.astype(BF)
            dqkv[rs, 0:d] = low
            sums[8:9, :] += column_sums(low.astype(F32))
            return carry

        lax.fori_loop(0, half // cut, middle, 0)
        joins.append(join(dqkv, half, n))
    loads["wo"].wait()
    loads["heads"].wait()
    for c in joins:
        c.wait_recv()
    width = heads.shape[1]

    def to_heads(r, carry):
        rs = pl.ds(pl.multiple_of(r * QB, QB), QB)
        xmid[rs, 0:width] = jnp.dot(dqkv[rs, 0:d], wo[...], preferred_element_type=F32).astype(BF)
        return carry

    lax.fori_loop(0, 2 * rows // QB, to_heads, 0)
    grads(1, dqkv, heads)
    for c in joins:
        c.wait_send()
    loads["qkv"].wait()
    loads["lse"].wait()
    def settle_all(g):
        for k in (1, 2, 3, 0):
            settle(g, k)

    def pass_all(g):
        for k in range(LANES):
            pass_on(g, k)

    def group_3():
        total(3)
        for k in range(1, LANES):
            pl.semaphore_signal(free, inc=1, device_id=(dp, lax.rem(lane + k, LANES)), device_id_type=MESH)

    events = [[lambda: settle_all(3)], [lambda: pass_all(2)], [group_3, lambda: pass_all(1)], [lambda: settle_all(2)] + [lambda n=n: res_back.home(n) for n in range(DEAL_CUTS)]]
    loads["xin"].wait()
    loads["wq"].wait()
    proj = widths[0]
    kpos = held.places(0, 2 * rows, 1)
    for pair in range(width // PAIR):
        dkv[...] = jnp.zeros_like(dkv)

        def attend(i, carry, pair=pair):
            attn_back(i, pair, held, kpos, lse, xmid, qkv, dqkv, dkv)
            return carry

        lax.fori_loop(0, 2 * rows // QB, attend, 0)
        at = 3 * pair * PAIR
        dqkv[:, at + PAIR:at + 2 * PAIR] = dkv[0].astype(BF)
        dqkv[:, at + 2 * PAIR:at + 3 * PAIR] = dkv[1].astype(BF)
        if pair == 0:
            pl.semaphore_wait(room, 2)
        cols = slice(pair * proj, (pair + 1) * proj)
        for q in (3, 1 if pair < 2 else 2, 2 if pair < 2 else 1, 0):
            dg[per * q:per * (q + 1), cols] = dot_g(dfull[:, per * q:per * (q + 1)], dqkv[:, cols]).astype(BF)
            if q == 3:
                firsts[0][pair][0].start()
            elif (q == 1) == (pair < 2) and q:
                firsts[0][pair][1].start()
        for e in events[pair]:
            e()
    copies = fold(1, lambda rs: dot_t(dqkv[rs, :], wq[...]), copies)
    sums[10:12, :] += jnp.concatenate([column_sums(dqkv[:, 0:d].astype(F32)),
                                       jnp.concatenate([column_sums(dqkv[:, d:3 * d // 2].astype(F32)), jnp.zeros((1, d // 2), F32)], axis=1)], axis=0)
    loads["h"].wait()
    for n in range(2):
        copies[n].wait_recv()

        def start_rows(m, carry, n=n):
            rs = chunk(n, m)
            g = part[rs, :] + rbuf[1, rs].astype(F32)
            dx, gx = norm_back_rows(h[rs, :].astype(F32), g, gains(0))
            sums[0:1, :] += column_sums(gx)
            sums[4:5, :] += column_sums(g)
            f = first[rs, :] + dx
            for q in range(4):
                cols = pl.ds(pl.multiple_of((chip ^ q) * quarter, quarter), quarter)
                h[rs, cols] = f[:, q * quarter:(q + 1) * quarter].astype(BF)
            return carry

        lax.fori_loop(0, half // cut, start_rows, 0)
        for m in range(half // cut):
            grad_back.start(n * (half // cut) + m)
    vec_all[...] = jnp.zeros_like(vec_all)
    for q in range(4):
        cols = pl.ds(pl.multiple_of((chip ^ q) * quarter, quarter), quarter)
        vec_all[0:10, cols] = sums[0:10, q * quarter:(q + 1) * quarter]
    hw = widths[1]
    for k in range(LANES):
        owner = lax.rem(lane + LANES - k, LANES)
        cols = pl.ds(pl.multiple_of(owner * 2 * hw + core * hw, hw), hw)
        for row, t in ((10, 0), (11, 2)):
            at = (3 * k + t) * hw
            vec_all[row:row + 1, cols] = sums[10 + at // d:11 + at // d, at % d:at % d + hw]
        vec_all[pl.ds(12 + owner, 1), pl.ds(pl.multiple_of(core * w, w), w)] = sums[16 + k:17 + k, 0:w]
    partners = [mate, (dp ^ 2, lane), (dp ^ 4, lane), (dp, lane ^ 1), (dp, lane ^ 2)]
    rounds = [remote(vec_all, sums_in.at[i], partners[i]) for i in range(5)]

    def vec_round(i):
        rounds[i].wait()
        vec_all[...] = vec_all[...] + sums_in[i]
        if i < 4:
            rounds[i + 1].start()

    rounds[0].start()
    vec_round(0)
    grad_back.merge(0)
    settle_all(1)
    close(3)
    vec_round(1)
    grad_back.merge(1)
    pass_on(0, 0)
    pass_on(0, 1)
    grad_back.merge(2)
    grad_back.home(0)
    vec_round(2)
    pass_on(0, 2)
    pass_on(0, 3)
    grad_back.merge(3)
    grad_back.home(1)
    vec_round(3)
    total(2)
    grad_back.home(2)
    total(1)
    grad_back.home(3)
    pl.semaphore_wait(free, LANES - 1)
    settle_all(0)
    vec_round(4)
    vec_o[...] = vec_all[...]
    close(2)
    close(1)
    total(0)
    close(0)
    res_back.finish()
    grad_back.sent()
    grad_back.finish()
    for c in out_copies:
        c.wait()
    for c in ends:
        if not any(c is r for r in rounds):
            c.wait_send()


def attn_back(i, pair, held, kpos, lse, grads, qkv, dqkv, dkv):
    begin = pl.multiple_of(i * QB, QB)
    rs = pl.ds(begin, QB)
    bias = held.bias(begin, kpos)
    lane = lax.broadcasted_iota(jnp.int32, (1, PAIR), 1)
    at = 3 * pair * PAIR
    query = qkv[rs, at:at + PAIR]
    key, value = qkv[:, at + PAIR:at + 2 * PAIR], qkv[:, at + 2 * PAIR:at + 3 * PAIR]
    grad = grads[rs, pair * PAIR:(pair + 1) * PAIR]
    dq = jnp.zeros(query.shape, F32)
    dk = jnp.zeros(key.shape, F32)
    dv = jnp.zeros(key.shape, F32)
    for side in range(2):
        mine = (lane >= side * DH) & (lane < (side + 1) * DH)
        piece = jnp.where(mine, query * 0.125, 0.0).astype(BF)
        gpart = jnp.where(mine, grad, jnp.zeros_like(grad))
        score = dot_t(piece, key) + bias
        index = pair * 2 + side
        prob = jnp.exp(score - lse[rs, index:index + 1])
        gprob = dot_t(gpart, value)
        inner = jnp.sum(prob * gprob, axis=-1, keepdims=True)
        gscore = (prob * (gprob - inner)).astype(BF)
        dq += jnp.dot(gscore, jnp.where(mine, key, jnp.zeros_like(key)), preferred_element_type=F32)
        dk += dot_g(gscore, piece)
        dv += dot_g(prob.astype(BF), gpart)
    dqkv[rs, at:at + PAIR] = (dq * 0.125).astype(BF)
    dkv[0] += dk
    dkv[1] += dv


def backward_call(widths, lengths, deal, ln_gain, saved):
    (wq, wo, w1, w2, h, xin, qkv, heads, lse, attn, first, xmid, act, dg, ffn, res, grd) = saved
    rows, d = h.shape
    per, wd = d // 4, d // 8
    shape, vm = jax.ShapeDtypeStruct, pltpu.VMEM
    like = lambda x: vm(x.shape, x.dtype)
    out = [shape((3, wd, 2 * widths[1]), F32), shape((2 * widths[1], wd), F32), shape((wd, 2 * widths[2]), F32), shape((2 * widths[3], wd), F32),
           shape((rows, d), BF), shape((rows, d), BF), shape((16, d), F32), shape((2, rows, d), BF), shape((8, 128), F32)]
    scratch = [like(x) for x in (wq, wo, w1, w2, ffn, grd, act, dg, xmid, first, attn, heads, qkv, lse, xin, h)]
    scratch += [vm(qkv.shape, BF), vm((2, 2 * rows, PAIR), F32), vm((rows, d), BF), vm((2, rows, d), BF), vm((2, rows, d), BF)]
    order = (3, 2, 1)
    scratch += [vm((2, per, LANES * widths[g]), BF) for g in order]
    scratch += [vm((per, LANES * widths[g]), BF) for g in order]
    scratch += [vm((LANES - 1, per, widths[g]), BF) for g in order]
    scratch += [vm((2, wd, w), BF) for w in widths]
    scratch += [vm((2 * widths[3], wd), F32), vm((2 * widths[1], wd), F32), vm((24, d), F32), vm((5, 16, d), F32), vm((16, d), F32), vm((8, d), F32),
                pltpu.SemaphoreType.REGULAR, pltpu.SemaphoreType.REGULAR, pltpu.SemaphoreType.DMA((BWD_SEMS,))]
    return pl.pallas_call(
        partial(backward_kernel, widths),
        in_specs=[SMEM, SMEM, IN_VMEM] + [ANY] * 17,
        out_specs=[ANY] * 6 + [IN_VMEM, ANY, IN_VMEM],
        out_shape=out,
        scratch_shapes=scratch,
        compiler_params=pltpu.CompilerParams(collective_id=2, has_side_effects=True, vmem_limit_bytes=67043328),
        name="backward",
    )(lengths, deal, ln_gain, *saved)


def feature_turn(x):
    n = lax.axis_size("dp") // 2
    chip = lax.axis_index("dp") // 2
    lead = x.shape[:-1]
    width = x.shape[-1] // n
    bits = n.bit_length() - 1
    y = x.reshape(lead + (2,) * bits + (width,))
    for b in range(bits):
        axis = len(lead) + bits - 1 - b
        y = jnp.where((chip >> b) & 1 == 1, jnp.flip(y, axis), y)
    return y.reshape(x.shape)


def body(tokens, cotangent, lengths, deal, w_qkv, w_o, w_1, w_2, b_qv, b_o, b_1, b_2, ln_gain, ln_bias):
    n_dp, lanes = lax.axis_size("dp"), lax.axis_size("tensor")
    dp, lane = lax.axis_index("dp"), lax.axis_index("tensor")
    core, chip = dp % 2, dp // 2
    rows = tokens.shape[0]
    both = ("dp", "tensor")
    near, far = deal_perms(n_dp)
    back_near, back_far = [(b, a) for a, b in near], [(b, a) for a, b in far]

    if n_dp == 8 and lanes == LANES:
        hw, fw = w_o.shape[0] // 2, w_1.shape[1] // 2
        widths = (3 * hw, hw, fw, fw)
        saved = forward_call(widths, tokens, cotangent, lengths, deal, w_qkv, w_o, w_1, w_2, b_qv, b_1[None], b_o[None], b_2[None], ln_gain, ln_bias)
        qkv_grad, out_grad, up_grad, down_grad, output, input_grad, vector, _, _ = backward_call(widths, lengths, deal, ln_gain, saved[:17])
        mine = lambda x: lax.dynamic_slice_in_dim(x.reshape(-1, lanes, x.shape[-1] // lanes), lane, 1, 1)[:, 0]
        bias_1_total = lax.dynamic_slice_in_dim(vector, 12 + lane, 1, 0)[0]
        return (output, input_grad, qkv_grad, out_grad, up_grad, down_grad, mine(vector[10:12]), vector[8], bias_1_total, vector[9],
                vector[0:4], vector[4:8])

    per = lengths.shape[0] // n_dp

    def pack_ends(pack):
        picked = lax.dynamic_slice_in_dim(deal, pack * per, per)
        lookup = picked[:, None] == jnp.arange(lengths.shape[0], dtype=jnp.int32)[None, :]
        lens = jnp.sum(jnp.where(lookup, lengths[None, :], 0), axis=1)
        ends = jnp.sum(jnp.where(jnp.arange(per)[:, None] >= jnp.arange(per)[None, :], lens[None, :], 0), axis=1)
        return ends, ends - lens, jnp.sum(jnp.where(lens == HALF, ends - lens, 0))

    half = lane % 2
    ends, starts, cut = pack_ends(chip * 2 + lane // 2)
    _, _, cut_home = pack_ends(dp)
    index = jnp.arange(rows, dtype=jnp.int32)
    slots = jnp.concatenate([core * rows + index, (1 - core) * rows + index])
    place = jnp.where(slots >= cut, slots + HALF * half, slots + HALF * (1 - half))
    seg_start = jnp.max(jnp.where(place[:, None] >= starts[None, :], starts[None, :], 0), axis=1)
    qpos, qstart, kpos = place[:, None], seg_start[:, None], place[None, :]
    keep = ((core * rows + index) >= cut)[:, None]
    keep_home = (((lane % 2) * rows + index) >= cut_home)[:, None]

    def deal_in(x):
        moved = lax.all_to_all(x, "dp", split_axis=0, concat_axis=0, tiled=True)
        return jnp.where(keep, lax.ppermute(moved, both, near), lax.ppermute(moved, both, far))

    def deal_out(x):
        moved = jnp.where(keep_home, lax.ppermute(x, both, back_near), lax.ppermute(x, both, back_far))
        return lax.all_to_all(moved, "dp", split_axis=0, concat_axis=0, tiled=True)

    def halves(x):
        w = x.shape[-1] // 2
        return (lax.dynamic_slice_in_dim(x, core * w, w, x.ndim - 1), lax.dynamic_slice_in_dim(x, (1 - core) * w, w, x.ndim - 1))

    qm, qo = halves(w_qkv)
    om, oo = halves(w_o.T)
    um, uo = halves(w_1)
    dm, do = halves(w_2.T)
    own = jnp.concatenate([qm[0], qm[1], qm[2], om, um, dm], axis=1)
    other = jnp.concatenate([qo[0], qo[1], qo[2], oo, uo, do], axis=1)
    hw, fw = om.shape[1], um.shape[1]
    widths = (3 * hw, hw, fw, fw)
    small = jnp.concatenate([halves(b_qv[0:1])[0], halves(b_qv[1:2])[0], halves(b_1[None])[0]], axis=1)
    small = jnp.concatenate([small, jnp.zeros((7, small.shape[1]), F32)])
    order = (lane - jnp.arange(lanes)) % lanes
    gain, shift = feature_turn(ln_gain), feature_turn(ln_bias)
    bias_o, bias_2 = feature_turn(b_o[None])[0], feature_turn(b_2[None])[0]

    def join(x):
        return jnp.concatenate([x, swap_dp(x, 1)], axis=0)

    def fold(x):
        return x[:rows] + swap_dp(x[rows:].astype(BF), 1).astype(F32)

    mm = partial(jnp.dot, preferred_element_type=F32)
    mm_t = lambda a, b: lax.dot_general(a, b, (((1,), (1,)), ((), ())), preferred_element_type=F32)
    mm_g = lambda a, b: lax.dot_general(a, b, (((0,), (0,)), ((), ())), preferred_element_type=F32)
    if True:
        blocks = gather_weights(own, other)
        wq, wo, w1, w2 = (weight_of(blocks, sum(widths[:i]), w) for i, w in enumerate(widths))
        smalls = jnp.take(lax.all_gather(small[0], "tensor"), order, axis=0)
        bias_q, bias_v, bias_1 = smalls[:, :hw], smalls[:, hw:2 * hw], smalls[:, 2 * hw:].reshape(-1)
        bias_qkv = jnp.concatenate([bias_q, jnp.zeros_like(bias_q), bias_v], axis=1).reshape(-1)
        hidden = feature_turn(deal_in(tokens)).astype(F32)
        normed_in = join(scaled_norm(hidden, gain[0], shift[0]).astype(BF))
        qkv = (mm(normed_in, wq) + bias_qkv).astype(BF)
        heads_out, lse = attn_forward(qpos, qstart, kpos, qkv)
        attn_out = fold(mm_t(heads_out, wo)) + bias_o
        first_sum = hidden + scaled_norm(attn_out, gain[1], shift[1])
        normed_mid = join(scaled_norm(first_sum, gain[2], shift[2]).astype(BF))
        pre_act = mm(normed_mid, w1) + bias_1
        cdf = 0.5 + 0.5 * lax.erf(pre_act * 0.7071067811865476)
        act = (pre_act * cdf).astype(BF)
        dgelu = (cdf + pre_act * (0.3989422804014327 * jnp.exp(-0.5 * pre_act * pre_act))).astype(BF)
        ffn_out = fold(mm_t(act, w2)) + bias_2
        result = feature_turn((first_sum + scaled_norm(ffn_out, gain[3], shift[3])).astype(BF))
        grad_result = feature_turn(deal_in(cotangent)).astype(F32)

    grad_ffn, gain_3, shift_3 = norm_back(ffn_out, gain[3], shift[3], grad_result)
    grad_ffn_low = grad_ffn.astype(BF)
    bias_2_grad = jnp.sum(grad_ffn_low.astype(F32), axis=0)
    grad_ffn_full = join(grad_ffn_low)
    grad_act = mm(grad_ffn_full, w2)
    down_part = mm_g(grad_ffn_full, act).astype(BF)
    grad_pre = (grad_act * dgelu.astype(F32)).astype(BF)
    bias_1_grad = jnp.sum(grad_pre.astype(F32), axis=0)
    grad_mid = fold(mm_t(grad_pre, w1))
    up_part = mm_g(normed_mid, grad_pre).astype(BF)
    grad_first_part, gain_2, shift_2 = norm_back(first_sum, gain[2], shift[2], grad_mid)
    grad_first = grad_result + grad_first_part
    grad_attn, gain_1, shift_1 = norm_back(attn_out, gain[1], shift[1], grad_first)
    grad_attn_low = grad_attn.astype(BF)
    bias_o_grad = jnp.sum(grad_attn_low.astype(F32), axis=0)
    grad_attn_full = join(grad_attn_low)
    grad_heads = mm(grad_attn_full, wo).astype(BF)
    out_part = mm_g(grad_attn_full, heads_out).astype(BF)
    grad_qkv = attn_backward(qpos, qstart, kpos, lse, grad_heads, qkv)
    bias_qkv_grad = jnp.sum(grad_qkv.astype(F32), axis=0).reshape(lanes, 3, hw)
    grad_in = fold(mm_t(grad_qkv, wq))
    qkv_part = mm_g(normed_in, grad_qkv).astype(BF)
    grad_hidden_part, gain_0, shift_0 = norm_back(hidden, gain[0], shift[0], grad_in)
    grad_hidden = feature_turn((grad_first + grad_hidden_part).astype(BF))

    def by_lane(x):
        x = jnp.take(x.reshape(lanes, -1), order, axis=0)
        both_halves = jnp.stack([jnp.where(core == 0, x, 0.0), jnp.where(core == 1, x, 0.0)], axis=1)
        return both_halves.reshape(-1)

    d = tokens.shape[1]
    stack = jnp.stack([gain_0, gain_1, gain_2, gain_3, shift_0, shift_1, shift_2, shift_3, bias_o_grad, bias_2_grad])
    vector = jnp.concatenate([feature_turn(stack).reshape(-1), by_lane(bias_qkv_grad[:, 0]), by_lane(bias_qkv_grad[:, 2]), by_lane(bias_1_grad)])
    parts = [qkv_part, out_part, up_part, down_part]
    output, input_grad = deal_out(result), deal_out(grad_hidden)
    vector = lax.psum(vector, both)
    shards = [scatter_grads([p.astype(F32)]) for p in parts]
    gain_total, shift_total = vector[:4 * d].reshape(4, d), vector[4 * d:8 * d].reshape(4, d)
    bias_o_total, bias_2_total = vector[8 * d:9 * d], vector[9 * d:10 * d]
    mine = lambda x: lax.dynamic_slice_in_dim(x.reshape(lanes, -1), lane, 1, 0)[0]
    bias_qv_total = jnp.stack([mine(vector[10 * d:11 * d]), mine(vector[11 * d:12 * d])])
    bias_1_total = mine(vector[12 * d:])

    spread = lambda x: jnp.concatenate([x[0], x[1]], axis=-1)
    qkv_grad, out_grad, up_grad, down_grad = shards
    qkv_out = jnp.stack([spread(qkv_grad[:, :, i * hw:(i + 1) * hw]) for i in range(3)])
    return (
        output, input_grad, qkv_out, spread(out_grad).T, spread(up_grad), spread(down_grad).T,
        bias_qv_total, bias_o_total, bias_1_total, bias_2_total, gain_total, shift_total,
    )


def solution(mesh):
    rows = P(("dp", "tensor"), None)
    weights = (P(None, "dp", "tensor"), P("tensor", "dp"), P("dp", "tensor"), P("tensor", "dp"))
    vectors = (P(None, "tensor"), P(), P("tensor"), P(), P(), P())
    return jax.shard_map(
        body,
        mesh=mesh,
        in_specs=(rows, rows, P(), P()) + weights + vectors,
        out_specs=(rows, rows) + weights + vectors,
        check_vma=False,
    )
```

```python
from functools import partial

import jax
import jax.numpy as jnp
from jax import lax
from jax.experimental import pallas as pl
from jax.experimental.pallas import tpu as pltpu
from jax.sharding import PartitionSpec as P

DH = 64
HALF = 1024
NORM_EPS = 1e-05
MASKED_OUT = -1e30
BF, F32 = jnp.bfloat16, jnp.float32
QB = 256


def scaled_norm(values, norm_gain, norm_shift):
    peak = jnp.max(jnp.abs(values), axis=-1, keepdims=True) + NORM_EPS
    scaled = values / peak
    centred = scaled - jnp.mean(scaled, axis=-1, keepdims=True)
    spread = jnp.mean(centred * centred, axis=-1, keepdims=True)
    return centred * lax.rsqrt(spread + NORM_EPS) * norm_gain + norm_shift


def norm_back(values, norm_gain, norm_shift, row_grad):
    result, pull = jax.vjp(scaled_norm, values, norm_gain, norm_shift)
    return pull(row_grad)


PAIR = 2 * DH


def attn_fwd_kernel(qpos_ref, qstart_ref, kpos_ref, qkv_ref, o_ref, lse_ref):
    first = pl.multiple_of(pl.program_id(0) * QB, QB)
    kpos = kpos_ref[...]
    allowed = (kpos <= qpos_ref[...]) & (kpos >= qstart_ref[...])
    bias = jnp.where(allowed, 0.0, MASKED_OUT)
    lane = lax.broadcasted_iota(jnp.int32, (1, PAIR), 1)
    wide = lax.broadcasted_iota(jnp.int32, lse_ref.shape, 1)
    stats = jnp.zeros(lse_ref.shape, F32)
    for pair in range(o_ref.shape[1] // PAIR):
        at = 3 * pair * PAIR
        query = qkv_ref[pl.ds(first, QB), at:at + PAIR]
        key, value = qkv_ref[:, at + PAIR:at + 2 * PAIR], qkv_ref[:, at + 2 * PAIR:at + 3 * PAIR]
        total = jnp.zeros(query.shape, F32)
        for side in range(2):
            mine = (lane >= side * DH) & (lane < (side + 1) * DH)
            part = jnp.where(mine, query * 0.125, 0.0).astype(BF)
            score = lax.dot_general(part, key, (((1,), (1,)), ((), ())), preferred_element_type=F32) + bias
            peak = jnp.max(score, axis=-1, keepdims=True)
            expo = jnp.exp(score - peak)
            norm = jnp.sum(expo, axis=-1, keepdims=True)
            prob = (expo * (1.0 / norm)).astype(BF)
            total += jnp.dot(prob, jnp.where(mine, value, jnp.zeros_like(value)), preferred_element_type=F32)
            stats = jnp.where(wide == pair * 2 + side, peak + jnp.log(norm), stats)
        o_ref[:, pair * PAIR:(pair + 1) * PAIR] = total.astype(BF)
    lse_ref[...] = stats


def attn_forward(qpos, qstart, kpos, qkv):
    rows, width = qkv.shape[0], qkv.shape[1] // 3
    col = pl.BlockSpec((QB, 1), lambda i: (i, 0))
    full = pl.BlockSpec(qkv.shape, lambda i: (0, 0))
    return pl.pallas_call(
        attn_fwd_kernel,
        grid=(rows // QB,),
        in_specs=[col, col, pl.BlockSpec((1, rows), lambda i: (0, 0)), full],
        out_specs=[pl.BlockSpec((QB, width), lambda i: (i, 0)), pl.BlockSpec((QB, 128), lambda i: (i, 0))],
        out_shape=[jax.ShapeDtypeStruct((rows, width), BF), jax.ShapeDtypeStruct((rows, 128), F32)],
        cost_estimate=pl.CostEstimate(flops=4 * rows * rows * width, bytes_accessed=8 * rows * width, transcendentals=rows * rows * width // DH),
        compiler_params=pltpu.CompilerParams(vmem_limit_bytes=48 << 20),
        name="attn_fwd",
    )(qpos, qstart, kpos, qkv)


def attn_bwd_kernel(qpos_ref, qstart_ref, kpos_ref, lse_ref, g_ref, qkv_ref, d_ref, dk_acc, dv_acc):
    step = pl.program_id(0)
    first = pl.multiple_of(step * QB, QB)

    @pl.when(step == 0)
    def _():
        dk_acc[...] = jnp.zeros_like(dk_acc)
        dv_acc[...] = jnp.zeros_like(dv_acc)

    kpos = kpos_ref[...]
    allowed = (kpos <= qpos_ref[...]) & (kpos >= qstart_ref[...])
    bias = jnp.where(allowed, 0.0, MASKED_OUT)
    lane = lax.broadcasted_iota(jnp.int32, (1, PAIR), 1)
    for pair in range(g_ref.shape[1] // PAIR):
        at = 3 * pair * PAIR
        query = qkv_ref[pl.ds(first, QB), at:at + PAIR]
        key, value = qkv_ref[:, at + PAIR:at + 2 * PAIR], qkv_ref[:, at + 2 * PAIR:at + 3 * PAIR]
        cols = slice(pair * PAIR, (pair + 1) * PAIR)
        grad = g_ref[:, cols]
        dq = jnp.zeros(query.shape, F32)
        dk = jnp.zeros(key.shape, F32)
        dv = jnp.zeros(key.shape, F32)
        for side in range(2):
            mine = (lane >= side * DH) & (lane < (side + 1) * DH)
            part = jnp.where(mine, query * 0.125, 0.0).astype(BF)
            gpart = jnp.where(mine, grad, jnp.zeros_like(grad))
            score = lax.dot_general(part, key, (((1,), (1,)), ((), ())), preferred_element_type=F32) + bias
            index = pair * 2 + side
            prob = jnp.exp(score - lse_ref[:, index:index + 1])
            gprob = lax.dot_general(gpart, value, (((1,), (1,)), ((), ())), preferred_element_type=F32)
            inner = jnp.sum(prob * gprob, axis=-1, keepdims=True)
            gscore = (prob * (gprob - inner)).astype(BF)
            dq += jnp.dot(gscore, jnp.where(mine, key, jnp.zeros_like(key)), preferred_element_type=F32)
            dk += lax.dot_general(gscore, part, (((0,), (0,)), ((), ())), preferred_element_type=F32)
            dv += lax.dot_general(prob.astype(BF), gpart, (((0,), (0,)), ((), ())), preferred_element_type=F32)
        d_ref[pl.ds(first, QB), at:at + PAIR] = (dq * 0.125).astype(BF)
        dk_acc[:, cols] += dk
        dv_acc[:, cols] += dv

    @pl.when(step == pl.num_programs(0) - 1)
    def _():
        for pair in range(g_ref.shape[1] // PAIR):
            at = 3 * pair * PAIR
            cols = slice(pair * PAIR, (pair + 1) * PAIR)
            d_ref[:, at + PAIR:at + 2 * PAIR] = dk_acc[:, cols].astype(BF)
            d_ref[:, at + 2 * PAIR:at + 3 * PAIR] = dv_acc[:, cols].astype(BF)


def attn_backward(qpos, qstart, kpos, lse, grad, qkv):
    rows, width = grad.shape
    col = pl.BlockSpec((QB, 1), lambda i: (i, 0))
    full = pl.BlockSpec(qkv.shape, lambda i: (0, 0))
    return pl.pallas_call(
        attn_bwd_kernel,
        grid=(rows // QB,),
        in_specs=[col, col, pl.BlockSpec((1, rows), lambda i: (0, 0)), pl.BlockSpec((QB, 128), lambda i: (i, 0)),
                  pl.BlockSpec((QB, width), lambda i: (i, 0)), full],
        out_specs=full,
        out_shape=jax.ShapeDtypeStruct(qkv.shape, BF),
        scratch_shapes=[pltpu.VMEM((rows, width), F32), pltpu.VMEM((rows, width), F32)],
        cost_estimate=pl.CostEstimate(flops=10 * rows * rows * width, bytes_accessed=14 * rows * width, transcendentals=rows * rows * width // DH),
        compiler_params=pltpu.CompilerParams(vmem_limit_bytes=48 << 20),
        name="attn_bwd",
    )(qpos, qstart, kpos, lse, grad, qkv)


def swap_dp(x, bit):
    n = lax.axis_size("dp")
    return lax.ppermute(x, "dp", [(i, i ^ bit) for i in range(n)])


def turn(x, shift):
    n = lax.axis_size("tensor")
    return lax.ppermute(x, "tensor", [(i, (i + shift) % n) for i in range(n)])


def chip_bits():
    n = lax.axis_size("dp")
    return [1 << b for b in range(1, n.bit_length() - 1)]


def core_pair(mine, other):
    core = lax.axis_index("dp") % 2
    return jnp.where(core == 0, jnp.stack([mine, other]), jnp.stack([other, mine]))


def gather_weights(mine, other):
    pair = core_pair(mine, swap_dp(other, 1)).reshape(2 * mine.shape[0], mine.shape[1])
    lanes = lax.axis_size("tensor")
    column = jnp.stack([pair] + [turn(pair, k) for k in range(1, lanes)])
    bits = chip_bits()
    if len(bits) == 2:
        low, high = bits
        first, second = swap_dp(column, low), swap_dp(column, high)
        mid = lanes // 2
        far = jnp.concatenate([swap_dp(first[:mid], high), swap_dp(second[mid:], low)])
        return {0: column, low: first, high: second, low | high: far}
    blocks = {0: column}
    for bit in bits:
        got = swap_dp(jnp.stack([blocks[m] for m in sorted(blocks)]), bit)
        blocks.update({m | bit: got[i] for i, m in enumerate(sorted(blocks))})
    return blocks


def weight_of(blocks, start, width):
    out = []
    for mask in sorted(blocks):
        part = blocks[mask][:, :, start:start + width]
        out.append(jnp.concatenate([part[k] for k in range(part.shape[0])], axis=1))
    return jnp.concatenate(out, axis=0)


def scatter_grads(parts):
    lanes = lax.axis_size("tensor")
    bits = chip_bits()
    count = 1 << len(bits)
    feats = parts[0].shape[0]
    per = feats // count

    def block(mask_index, k):
        cut = []
        for p in parts:
            w = p.shape[1] // lanes
            cut.append(p[mask_index * per:(mask_index + 1) * per, k * w:(k + 1) * w])
        return jnp.concatenate(cut, axis=1) if len(cut) > 1 else cut[0]

    def col(mask_index, ks):
        return jnp.stack([block(mask_index, k) for k in ks])

    if len(bits) == 2:
        low, high = bits
        mid = lanes // 2
        ka, kb = list(range(mid)), list(range(mid, lanes))
        sent_a = jnp.stack([col(1, ka), col(3, ka)]).astype(BF)
        sent_b = jnp.stack([col(2, kb), col(3, kb)]).astype(BF)
        got_a, got_b = swap_dp(sent_a, low), swap_dp(sent_b, high)
        pass_a = (col(2, ka) + got_a[1].astype(F32)).astype(BF)
        pass_b = (col(1, kb) + got_b[1].astype(F32)).astype(BF)
        end_a, end_b = swap_dp(pass_a, high), swap_dp(pass_b, low)
        keep_a = col(0, ka) + got_a[0].astype(F32) + end_a.astype(F32)
        keep_b = col(0, kb) + got_b[0].astype(F32) + end_b.astype(F32)
        total = [keep_a[i] for i in range(mid)] + [keep_b[i] for i in range(lanes - mid)]
    else:
        sums = {m: col(m, range(lanes)) for m in range(count)}
        for level in reversed(range(len(bits))):
            keys = [m for m in sorted(sums) if m >> level & 1]
            got = swap_dp(jnp.stack([sums[m] for m in keys]).astype(BF), bits[level])
            sums = {m ^ (1 << level): sums[m ^ (1 << level)] + got[i].astype(F32) for i, m in enumerate(keys)}
        total = [sums[0][k] for k in range(lanes)]
    own = total[0]
    for k in range(1, lanes):
        own = own + turn(total[k].astype(BF), -k).astype(F32)
    rows = own.shape[0] // 2
    core = lax.axis_index("dp") % 2
    mine = lax.dynamic_slice_in_dim(own, core * rows, rows, 0)
    other = lax.dynamic_slice_in_dim(own, (1 - core) * rows, rows, 0)
    return core_pair(mine, swap_dp(other.astype(BF), 1).astype(F32))


def deal_perms(n_dp):
    near, far = [], []
    for chip in range(n_dp // 2):
        for c in range(2):
            for j in range(4):
                source = (chip * 2 + c) * 4 + j
                near.append((source, (chip * 2 + j % 2) * 4 + 2 * c + j // 2))
                far.append((source, (chip * 2 + j % 2) * 4 + 2 * c + 1 - j // 2))
    return near, far


MESH = pl.DeviceIdType.MESH
LANES = 4
ANY = pl.BlockSpec(memory_space=pl.ANY)
IN_VMEM = pl.BlockSpec(memory_space=pltpu.VMEM)


def greet(dp, lane, n_dp):
    barrier = pltpu.get_barrier_semaphore()
    count = 0
    for d in range(1, n_dp):
        pl.semaphore_signal(barrier, inc=1, device_id=(dp ^ d, lane), device_id_type=MESH)
        count += 1
    for k in range(1, LANES):
        for c in range(2):
            pl.semaphore_signal(barrier, inc=1, device_id=(dp ^ c, lax.rem(lane + k, LANES)), device_id_type=MESH)
            count += 1
    return barrier, count


def send(src, dst, send_sem, recv_sem, device):
    return pltpu.make_async_remote_copy(src_ref=src, dst_ref=dst, send_sem=send_sem, recv_sem=recv_sem, device_id=device, device_id_type=MESH)


DEAL_CUTS = 4
SMEM = pl.BlockSpec(memory_space=pltpu.SMEM)


class Pack:
    def __init__(self, lengths, deal, dp, lane, rows):
        core = dp % 2
        per = lengths.shape[0] // 8
        first = ((dp // 2) * 2 + lane // 2) * per
        self.starts, end, self.cut = [], 0, 0
        for j in range(per):
            size = lengths[deal[first + j]]
            self.starts.append(end)
            self.cut = self.cut + jnp.where(size == HALF, end, 0)
            end = end + size
        self.half, self.offset, self.rows = lane % 2, core * rows, rows

    def slots(self, begin, count, axis):
        shape = (count, 1) if axis == 0 else (1, count)
        return (self.offset + begin + lax.broadcasted_iota(jnp.int32, shape, axis)) & (2 * self.rows - 1)

    def places(self, begin, count, axis):
        slot = self.slots(begin, count, axis)
        return slot + HALF * jnp.where(slot >= self.cut, self.half, 1 - self.half)

    def seen_from(self, places):
        out = jnp.zeros(places.shape, jnp.int32)
        for start in self.starts:
            out = jnp.maximum(out, jnp.where(places >= start, start, 0))
        return out

    def bias(self, begin, kpos):
        at = self.places(begin, QB, 0)
        return jnp.where((kpos <= at) & (kpos >= self.seen_from(at)), 0.0, MASKED_OUT)


def relative(vec, chip, sources):
    quarter = vec.shape[1] // 4
    for q in range(4):
        cols = pl.ds(pl.multiple_of((chip ^ q) * quarter, quarter), quarter)
        at = 0
        for src in sources:
            count = src.shape[0]
            vec[at:at + count, q * quarter:(q + 1) * quarter] = src[:, cols]
            at += count


def norm_parts(x):
    peak = jnp.max(jnp.abs(x), axis=-1, keepdims=True) + NORM_EPS
    u = x * (1.0 / peak)
    c = u - jnp.mean(u, axis=-1, keepdims=True)
    return c, lax.rsqrt(jnp.mean(c * c, axis=-1, keepdims=True) + NORM_EPS)


def norm_rows(x, gain, shift):
    c, r = norm_parts(x)
    return c * r * gain + shift


def dot_t(a, b):
    return lax.dot_general(a, b, (((1,), (1,)), ((), ())), preferred_element_type=F32)


class Sems:
    def __init__(self, ref):
        self.ref, self.used = ref, 0

    def take(self, count=1):
        self.used += count
        return self.used - count


FWD_SEMS = 320


def forward_kernel(widths, lengths, deal, w_qkv, w_o, w_1, w_2, b_qv, b_1, b_o, b_2, ln_gain, ln_bias, tok, cot, *rest):
    outs, rest = rest[:18], rest[18:]
    (wq_o, wo_o, w1_o, w2_o, h_o, xin_o, qkv_o, heads_o, lse_o, attn_o, first_o, xmid_o, act_o, dg_o, ffn_o, res_o, grd_o, small_o) = outs
    (wq, wo, w1, w2, moved, cand, h, xin, qkv, heads, lse, part, sbuf, rbuf, first, xmid, act, dg, stage, small_in, own, other, small, vec, sem_ref) = rest
    mats = (wq, wo, w1, w2)
    sems = Sems(sem_ref)
    dp, lane = lax.axis_index("dp"), lax.axis_index("tensor")
    n_dp = 8
    core, chip = dp % 2, dp // 2
    rows, d = tok.shape
    wd = own.shape[0]
    quarter = d // 4
    up = lax.rem(lane + 1, LANES)
    n_g = len(widths)
    mate = (dp ^ 1, lane)
    ends = []

    def local(src, dst):
        c = pltpu.make_async_copy(src, dst, sem_ref.at[sems.take()])
        return c

    def remote(src, dst, device):
        s, r = sems.take(), sems.take()
        c = send(src, dst, sem_ref.at[s], sem_ref.at[r], device)
        ends.append(c.wait_send)
        return c

    barrier, count = greet(dp, lane, n_dp)
    rows_of = lambda x: jnp.transpose(x.astype(F32)).astype(BF)
    for half, dst in ((core, own), (1 - core, other)):
        at = 0
        part_of = lambda w: pl.ds(pl.multiple_of(half * w, w), w)
        for t in range(3):
            dst[:, at:at + widths[1]] = w_qkv[t, :, part_of(widths[1])]
            at += widths[1]
        for src, w, turned in ((w_o, widths[1], True), (w_1, widths[2], False), (w_2, widths[3], True)):
            dst[:, at:at + w] = rows_of(src[part_of(w), :]) if turned else src[:, part_of(w)]
            at += w
    at = 0
    small[...] = jnp.zeros_like(small)
    for src, w in ((b_qv.at[0:1], widths[1]), (b_qv.at[1:2], widths[1]), (b_1, widths[2])):
        small[0:1, at:at + w] = src[:, pl.ds(pl.multiple_of(core * w, w), w)]
        at += w
    relative(vec, chip, (ln_gain, ln_bias, b_o, b_2))
    held = Pack(lengths, deal, dp, lane, rows)
    pl.semaphore_wait(barrier, count)
    block = rows // n_dp
    here = pl.ds(pl.multiple_of(dp * block, block), block)
    deals = []
    for i, src in enumerate((tok, cot)):
        stay = local(src.at[here], moved.at[i, here])
        copies = []
        for k in range(1, n_dp):
            there = pl.ds(pl.multiple_of((dp ^ k) * block, block), block)
            copies.append(remote(src.at[there], moved.at[i, here], (dp ^ k, lane)))
        deals.append((stay, copies))

    def deal_start(i):
        deals[i][0].start()
        for c in deals[i][1]:
            c.start()

    deal_start(0)
    feat = pl.ds(pl.multiple_of(core * wd, wd), wd)
    at, stays, pairs = 0, [], []
    for g, w in enumerate(widths):
        dst = mats[g].at[feat, 0:w]
        stays.append(local(own.at[:, at:at + w], dst))
        pairs.append(remote(other.at[:, at:at + w], dst, mate))
        stays[g].start()
        pairs[g].start()
        at += w
    n_s = small.shape[0]
    smalls = [remote(small, small_in.at[k], (dp, lax.rem(lane + k, LANES))) for k in range(1, LANES)]
    for c in smalls:
        c.start()
    small_in[0] = small[...]

    def area(g, q, k):
        w = widths[g]
        return mats[g].at[2 * wd * q:2 * wd * (q + 1), k * w:(k + 1) * w]

    turns = [[remote(area(g, 0, t), area(g, 0, t + 1), (dp, up)) for t in range(LANES - 1)] for g in range(n_g)]
    planes = [[[remote(area(g, 0, k), area(g, side, k), (dp ^ (2 * side), lane)) for side in (1, 2)] for k in range(LANES)] for g in range(n_g)]
    fars = []
    for g in range(n_g):
        fars.append([])
        for k in range(LANES):
            side, via = (1, 2) if k < LANES // 2 else (2, 1)
            fars[g].append(remote(area(g, side, k), area(g, 3, k), (dp ^ (2 * via), lane)))

    def plane(g, k):
        for c in planes[g][k]:
            c.start()

    def pair_in(g):
        stays[g].wait()
        pairs[g].wait_recv()
        turns[g][0].start()

    def turn_in(g, t):
        turns[g][t].wait_recv()
        if t < LANES - 2:
            turns[g][t + 1].start()

    def far_go(g, k):
        planes[g][k][0 if k < LANES // 2 else 1].wait_recv()
        fars[g][k].start()

    def all_in(g):
        for k in range(LANES):
            planes[g][k][1 if k < LANES // 2 else 0].wait_recv()
            fars[g][k].wait_recv()

    pack = lane // 2
    spot = chip * 2 + lane % 2
    to_near = (spot, core + 1)
    slot = jnp.where(lane // 2 == core, 1, 0)
    is_self = (lane == 3 * core) & (spot == dp)
    is_near = lane == pack + 1
    straight = core == pack
    split = jnp.where(jnp.logical_not(is_near) & jnp.logical_not(straight), 2 * HALF, held.cut)
    cut = rows // DEAL_CUTS

    class Route:
        def __init__(self, i):
            self.i = i
            a0, f0 = sems.take(DEAL_CUTS), sems.take(DEAL_CUTS)
            got = sems.take(2 * DEAL_CUTS)
            self.near, self.self_, self.hand, self.pick, self.wait0, self.wait1 = [], [], [], [], [], []
            for n in range(DEAL_CUTS):
                rs = slice(n * cut, (n + 1) * cut)
                src = moved.at[i, rs]
                last = (dp, 3 * pack)
                self.near.append(send(src, cand.at[i, slot, rs], sem_ref.at[a0 + n], sem_ref.at[got + n * 2 + slot], to_near))
                self.self_.append(pltpu.make_async_copy(src, cand.at[i, 0, rs], sem_ref.at[got + n * 2]))
                self.hand.append(send(cand.at[i, 0, rs], cand.at[i, 1, rs], sem_ref.at[f0 + n], sem_ref.at[got + n * 2 + 1], last))
                self.pick.append(send(stage.at[0, rs], cand.at[i, 1, rs], sem_ref.at[f0 + n], sem_ref.at[got + n * 2 + 1], last))
                self.wait0.append(send(src, cand.at[i, 0, rs], sem_ref.at[a0 + n], sem_ref.at[got + n * 2], to_near))
                self.wait1.append(send(src, cand.at[i, 1, rs], sem_ref.at[a0 + n], sem_ref.at[got + n * 2 + 1], to_near))

        def start(self):
            for n in range(DEAL_CUTS):
                self.near[n].start()
                pl.when(is_self)(lambda: self.self_[n].start())

        def arrive(self, n):
            pl.when(is_self)(lambda: self.self_[n].wait())
            pl.when(is_near)(lambda: self.wait0[n].wait_recv())
            pl.when(is_near & straight)(lambda: self.hand[n].start())
            self.wait1[n].wait_recv()

            def choose_far():
                rs = slice(n * cut, (n + 1) * cut)
                on = held.slots(n * cut, cut, 0) >= held.cut
                stage[0, rs] = jnp.where(on, cand[self.i, 1, rs].astype(F32), cand[self.i, 0, rs].astype(F32)).astype(BF)
                self.pick[n].start()

            pl.when(is_near & jnp.logical_not(straight))(choose_far)

        def finish(self, picked=True):
            for n in range(DEAL_CUTS):
                self.near[n].wait_send()
                pl.when(is_near & straight)(lambda: self.hand[n].wait_send())
                if picked:
                    pl.when(is_near & jnp.logical_not(straight))(lambda: self.pick[n].wait_send())

    routes = [Route(0), Route(1)]

    def deal_on(i):
        deals[i][0].wait()
        for c in deals[i][1]:
            c.wait_recv()
        routes[i].start()

    def choose(i, n):
        rs = slice(n * cut, (n + 1) * cut)
        on = held.slots(n * cut, cut, 0) >= split
        parts = []
        for q in range(4):
            cols = pl.ds(pl.multiple_of((chip ^ q) * quarter, quarter), quarter)
            parts.append(jnp.where(on, cand[i, 0, rs, cols].astype(F32), cand[i, 1, rs, cols].astype(F32)))
        return jnp.concatenate(parts, axis=1)

    out_copies = []

    def put(src, dst):
        c = local(src, dst)
        c.start()
        out_copies.append(c)

    early = (0, 1)

    def forward_on(groups, t):
        for g in groups:
            turn_in(g, t)
        for g in groups:
            plane(g, t + 1)

    for g in range(4):
        pair_in(g)
        if g < 3:
            plane(g, 0)
    forward_on(early, 0)
    forward_on((2,), 0)
    forward_on(early, 1)
    turn_in(3, 0)
    forward_on((2,), 1)
    deal_on(0)
    forward_on(early, 2)
    for k in range(LANES):
        for g in early:
            far_go(g, k)
    plane(3, 0)
    deal_start(1)
    joins = []

    def join_send(x, n, size):
        c = remote(x.at[n * size:(n + 1) * size], x.at[rows + n * size:rows + (n + 1) * size], mate)
        c.start()
        joins.append(c)

    gains = lambda i: vec[i:i + 1, :]
    for n in range(DEAL_CUTS):
        rs = slice(n * cut, (n + 1) * cut)
        routes[0].arrive(n)
        x = choose(0, n)
        h[rs, :] = x.astype(BF)
        xin[rs, :] = norm_rows(x, gains(0), gains(4)).astype(BF)
        join_send(xin, n, cut)
        if n == 1:
            forward_on((2,), 2)
        if n == 2:
            turn_in(3, 1)
    plane(3, 1)
    for c in smalls:
        c.wait_recv()
    all_in(0)
    for c in joins:
        c.wait_recv()
    put(wq, wq_o)
    put(h, h_o)
    put(xin, xin_o)
    w = widths[0]
    third = w // 3
    for k in range(LANES):
        cols = slice(k * w, (k + 1) * w)
        row = small_in[k, 0:1, :]
        bias = jnp.concatenate([row[:, 0:third], jnp.zeros((1, third), F32), row[:, third:2 * third]], axis=1)

        def project(r, carry, cols=cols, bias=bias):
            rs = pl.ds(pl.multiple_of(r * QB, QB), QB)
            qkv[rs, cols] = (jnp.dot(xin[rs, :], wq[:, cols], preferred_element_type=F32) + bias).astype(BF)
            return carry

        lax.fori_loop(0, 2 * rows // QB, project, 0)
        far_go(2, k)
    put(qkv, qkv_o)
    plane(3, 2)

    kpos = held.places(0, 2 * rows, 1)

    def beside(i):
        if i == 0:
            deal_on(1)
        elif i == 1:
            forward_on((3,), 2)
        elif i == 2:
            far_go(3, 0)
            far_go(3, 1)

    def attend(i, carry):
        begin = pl.multiple_of(i * QB, QB)
        attn_block(pl.ds(begin, QB), held.bias(begin, kpos), qkv, heads, lse)
        for n in range(3):
            pl.when(i == n)(lambda: beside(n))
        return carry

    lax.fori_loop(0, 2 * rows // QB, attend, 0)
    put(heads, heads_o)
    put(lse, lse_o)
    all_in(1)
    put(wo, wo_o)

    def fold(x, w_ref, which):
        copies = []
        per = 2
        size = rows // per
        for n in range(per):
            rs = slice(rows + n * size, rows + (n + 1) * size)
            sbuf[which, n * size:(n + 1) * size] = dot_t(x[rs, :], w_ref[...]).astype(BF)
            c = remote(sbuf.at[which, n * size:(n + 1) * size], rbuf.at[which, n * size:(n + 1) * size], mate)
            c.start()
            copies.append(c)
        for n in range(per):
            rs = slice(n * size, (n + 1) * size)
            part[rs, :] = dot_t(x[rs, :], w_ref[...])
        return copies

    copies = fold(heads, wo, 0)
    joins.clear()
    size = rows // 2
    for n in range(2):
        copies[n].wait_recv()

        def middle(m, carry, n=n):
            rs = pl.ds(pl.multiple_of(n * size + m * cut, cut), cut)
            y = part[rs, :] + rbuf[0, rs].astype(F32) + gains(8)
            part[rs, :] = y
            f = h[rs, :].astype(F32) + norm_rows(y, gains(1), gains(5))
            first[rs, :] = f
            xmid[rs, :] = norm_rows(f, gains(2), gains(6)).astype(BF)
            return carry

        lax.fori_loop(0, size // cut, middle, 0)
        join_send(xmid, n, size)
    attn_put = local(part, attn_o)
    attn_put.start()
    put(first, first_o)
    all_in(2)
    put(w1, w1_o)
    for c in joins:
        c.wait_recv()
    put(xmid, xmid_o)
    w = widths[2]
    for k in range(LANES):
        cols = slice(k * w, (k + 1) * w)
        bias = small_in[k, 0:1, 2 * third:2 * third + w]

        def hidden_units(r, carry, cols=cols, bias=bias):
            rs = pl.ds(pl.multiple_of(r * QB, QB), QB)
            pre = jnp.dot(xmid[rs, :], w1[:, cols], preferred_element_type=F32) + bias
            cdf = 0.5 + 0.5 * lax.erf(pre * 0.7071067811865476)
            act[rs, cols] = (pre * cdf).astype(BF)
            dg[rs, cols] = (cdf + pre * (0.3989422804014327 * jnp.exp(-0.5 * pre * pre))).astype(BF)
            return carry

        lax.fori_loop(0, 2 * rows // QB, hidden_units, 0)
        if k < 2:
            far_go(3, k + 2)
        if k == 1:
            routes[0].finish()
        if k > 1:
            routes[1].arrive(2 * k - 4)
            routes[1].arrive(2 * k - 3)
    put(act, act_o)
    put(dg, dg_o)
    all_in(3)
    put(w2, w2_o)
    attn_put.wait()
    copies = fold(act, w2, 1)
    for n in range(DEAL_CUTS):
        rs = slice(n * cut, (n + 1) * cut)
        stage[1, rs] = choose(1, n).astype(BF)
    put(stage.at[1], grd_o)
    for n in range(DEAL_CUTS):
        pl.when(is_near & jnp.logical_not(straight))(lambda: routes[1].pick[n].wait_send())
    for n in range(2):
        copies[n].wait_recv()

        def last(m, carry, n=n):
            rs = pl.ds(pl.multiple_of(n * size + m * cut, cut), cut)
            y = part[rs, :] + rbuf[1, rs].astype(F32) + gains(9)
            part[rs, :] = y
            out = first[rs, :] + norm_rows(y, gains(3), gains(7))
            for q in range(4):
                cols = pl.ds(pl.multiple_of((chip ^ q) * quarter, quarter), quarter)
                stage[0, rs, cols] = out[:, q * quarter:(q + 1) * quarter].astype(BF)
            return carry

        lax.fori_loop(0, size // cut, last, 0)
    put(part, ffn_o)
    put(stage.at[0], res_o)
    put(small_in, small_o)
    for c in out_copies:
        c.wait()
    routes[1].finish(False)
    for wait in ends:
        wait()


def attn_block(rs, bias, qkv, heads, lse):
    lane = lax.broadcasted_iota(jnp.int32, (1, PAIR), 1)
    wide = lax.broadcasted_iota(jnp.int32, (QB, 128), 1)
    stats = jnp.zeros((QB, 128), F32)
    for pair in range(heads.shape[1] // PAIR):
        at = 3 * pair * PAIR
        query = qkv[rs, at:at + PAIR]
        key, value = qkv[:, at + PAIR:at + 2 * PAIR], qkv[:, at + 2 * PAIR:at + 3 * PAIR]
        total = jnp.zeros(query.shape, F32)
        for side in range(2):
            mine = (lane >= side * DH) & (lane < (side + 1) * DH)
            piece = jnp.where(mine, query * 0.125, 0.0).astype(BF)
            score = dot_t(piece, key) + bias
            peak = jnp.max(score, axis=-1, keepdims=True)
            expo = jnp.exp(score - peak)
            norm = jnp.sum(expo, axis=-1, keepdims=True)
            prob = (expo * (1.0 / norm)).astype(BF)
            total += jnp.dot(prob, jnp.where(mine, value, jnp.zeros_like(value)), preferred_element_type=F32)
            stats = jnp.where(wide == pair * 2 + side, peak + jnp.log(norm), stats)
        heads[rs, pair * PAIR:(pair + 1) * PAIR] = total.astype(BF)
    lse[rs, :] = stats


def forward_call(widths, tok, cot, lengths, deal, w_qkv, w_o, w_1, w_2, b_qv, b_1, b_o, b_2, ln_gain, ln_bias):
    rows, d = tok.shape
    both = 2 * rows
    vm = pltpu.VMEM
    hidden = LANES * widths[2]
    small = (8, 2 * widths[1] + widths[2])
    mats = [(d, LANES * w) for w in widths]
    shape = jax.ShapeDtypeStruct
    out = [shape(m, BF) for m in mats] + [
        shape((rows, d), BF), shape((both, d), BF), shape((both, LANES * widths[0]), BF), shape((both, LANES * widths[1]), BF), shape((both, 128), F32),
        shape((rows, d), F32), shape((rows, d), F32), shape((both, d), BF), shape((both, hidden), BF), shape((both, hidden), BF),
        shape((rows, d), F32), shape((rows, d), BF), shape((rows, d), BF), shape((LANES,) + small, F32)]
    scratch = [vm(m, BF) for m in mats] + [
        vm((2, rows, d), BF), vm((2, 2, rows, d), BF), vm((rows, d), BF), vm((both, d), BF), vm((both, LANES * widths[0]), BF),
        vm((both, LANES * widths[1]), BF), vm((both, 128), F32), vm((rows, d), F32), vm((2, rows, d), BF), vm((2, rows, d), BF),
        vm((rows, d), F32), vm((both, d), BF), vm((both, hidden), BF), vm((both, hidden), BF), vm((2, rows, d), BF),
        vm((LANES,) + small, F32), vm((d // 8, sum(widths)), BF), vm((d // 8, sum(widths)), BF), vm(small, F32), vm((16, d), F32),
        pltpu.SemaphoreType.DMA((FWD_SEMS,))]
    return pl.pallas_call(
        partial(forward_kernel, widths),
        in_specs=[SMEM, SMEM] + [IN_VMEM] * 10 + [ANY, ANY],
        out_specs=[ANY] * len(out),
        out_shape=out,
        scratch_shapes=scratch,
        compiler_params=pltpu.CompilerParams(collective_id=1, has_side_effects=True, vmem_limit_bytes=67043328),
        name="forward",
    )(lengths, deal, w_qkv, w_o, w_1, w_2, b_qv, b_1, b_o, b_2, ln_gain, ln_bias, tok, cot)


def norm_back_rows(x, grad, gain):
    mag = jnp.abs(x)
    top = jnp.max(mag, axis=-1, keepdims=True)
    inv = 1.0 / (top + NORM_EPS)
    u = x * inv
    c = u - jnp.mean(u, axis=-1, keepdims=True)
    r = lax.rsqrt(jnp.mean(c * c, axis=-1, keepdims=True) + NORM_EPS)
    xhat = c * r
    t = grad * gain
    gx = grad * xhat
    along = jnp.mean(t * xhat, axis=-1, keepdims=True)
    du = r * (t - jnp.mean(t, axis=-1, keepdims=True) - xhat * along)
    at_top = mag == top
    ties = jnp.sum(jnp.where(at_top, 1.0, 0.0), axis=-1, keepdims=True)
    pull = x.shape[-1] * NORM_EPS * along * r * r * inv / ties
    side = jnp.where(x > 0, -pull, jnp.where(x < 0, pull, 0.0))
    return du * inv + jnp.where(at_top, side, 0.0), gx


BWD_SEMS = 420


def dot_g(a, b):
    return lax.dot_general(a, b, (((0,), (0,)), ((), ())), preferred_element_type=F32)


def column_sums(x):
    return jnp.sum(x, axis=0, keepdims=True)


def backward_kernel(widths, lengths, deal, ln_gain, *rest):
    ins, rest = rest[:17], rest[17:]
    (wq_i, wo_i, w1_i, w2_i, h_i, xin_i, qkv_i, heads_i, lse_i, attn_i, first_i, xmid_i, act_i, dg_i, ffn_i, res_i, grd_i) = ins
    outs, rest = rest[:9], rest[9:]
    (qkv_o, wo_o, w1_o, w2_o, out_o, ig_o, vec_o, home_o, _) = outs
    (wq, wo, w1, w2, part, grd, act, dg, xmid, first, attn, heads, qkv, lse, dfull, res, dqkv, dkv, sbuf, rbuf, zin,
     fl3, fl2, fl1, sl3, sl2, sl1, tl3, tl2, tl1, third0, third1, third2, third3, tall, wide_o, sums, sums_in, vec_all, vec, room, free, sem_ref) = rest
    xin, h = dfull, res
    mats = (dg, wo, w1, w2)
    thirds = (third0, third1, third2, third3)
    n_g = len(widths)
    sems = Sems(sem_ref)
    dp, lane = lax.axis_index("dp"), lax.axis_index("tensor")
    n_dp = 8
    core, chip = dp % 2, dp // 2
    rows, d = grd.shape
    quarter = d // 4
    per = 2 * (d // n_dp)
    wd = d // n_dp
    mate = (dp ^ 1, lane)
    cut = rows // DEAL_CUTS
    ends = []

    def local(src, dst):
        return pltpu.make_async_copy(src, dst, sem_ref.at[sems.take()])

    def remote(src, dst, device):
        a, b = sems.take(), sems.take()
        c = send(src, dst, sem_ref.at[a], sem_ref.at[b], device)
        ends.append(c)
        return c

    loads = {}
    for name, src, dst in (("ffn", ffn_i, part), ("grd", grd_i, grd), ("res", res_i, res), ("w2", w2_i, w2), ("dg", dg_i, dg), ("act", act_i, act),
                           ("w1", w1_i, w1), ("xmid", xmid_i, xmid), ("first", first_i, first), ("attn", attn_i, attn), ("wo", wo_i, wo),
                           ("heads", heads_i, heads), ("qkv", qkv_i, qkv), ("lse", lse_i, lse), ("wq", wq_i, wq), ("xin", xin_i, xin), ("h", h_i, h)):
        loads[name] = local(src, dst)
        if name not in ("xin", "h"):
            loads[name].start()
    barrier, count = greet(dp, lane, n_dp)
    held = Pack(lengths, deal, dp, lane, rows)
    relative(vec, chip, (ln_gain,))
    pl.semaphore_wait(barrier, count)
    gains = lambda i: vec[i:i + 1, :]
    sums[...] = jnp.zeros_like(sums)
    pack = lane // 2
    is_near = lane == pack + 1
    is_far = lane == 3 * pack
    block = rows // n_dp

    class Back:
        def __init__(self, i, src, same, other, out):
            self.i, self.src, self.same, self.other = i, src, same, other
            self.out = out
            z0, z1, m0, o0, h0 = [sems.take(DEAL_CUTS) for _ in range(5)]
            a0, a1 = sems.take(n_dp), sems.take(n_dp)
            self.a0, self.a1 = a0, a1
            spot = chip * 2 + pack
            kappa = core
            self.up_, self.keep_, self.give_ = [], [], []
            for n in range(DEAL_CUTS):
                rs = slice(n * cut, (n + 1) * cut)
                self.up_.append(send(src.at[rs], zin.at[i, rs], sem_ref.at[z0 + n], sem_ref.at[z1 + n], (dp, pack + 1)))
                self.keep_.append(send(same.at[rs], home_o.at[i, rs], sem_ref.at[m0 + n], sem_ref.at[h0 + n], (spot, kappa + 2 * pack)))
                self.give_.append(send(other.at[rs], home_o.at[i, rs], sem_ref.at[o0 + n], sem_ref.at[h0 + n], (spot, kappa + 2 * (1 - pack))))
            here = pl.ds(pl.multiple_of(dp * block, block), block)
            self.go_, self.stay_, self.got_ = [], [], []
            for a in range(n_dp):
                src_rows = home_o.at[i, a * block:(a + 1) * block]
                self.go_.append(send(src_rows, out.at[here], sem_ref.at[a0 + a], sem_ref.at[a1 + dp], (a, lane)))
                self.stay_.append(pltpu.make_async_copy(src_rows, out.at[here], sem_ref.at[a0 + a]))
                self.got_.append(send(src_rows, out.at[a * block:(a + 1) * block], sem_ref.at[a0 + a], sem_ref.at[a1 + a], (a, lane)))

        def start(self, n):
            pl.when(is_far)(lambda: self.up_[n].start())

        def merge(self, n):
            rs = slice(n * cut, (n + 1) * cut)

            def work():
                self.up_[n].wait_recv()
                on = held.slots(n * cut, cut, 0) >= held.cut
                mine, theirs = self.src[rs, :].astype(F32), zin[self.i, rs].astype(F32)
                self.same[rs, :] = jnp.where(on, theirs, mine).astype(BF)
                self.other[rs, :] = jnp.where(on, mine, theirs).astype(BF)
                self.keep_[n].start()
                self.give_[n].start()

            pl.when(is_near)(work)

        def home(self, n):
            self.keep_[n].wait_recv()
            for a in range(n * cut // block, (n + 1) * cut // block):
                pl.when(dp != a)(lambda: self.go_[a].start())
                pl.when(dp == a)(lambda: self.stay_[a].start())

        def sent(self):
            for n in range(DEAL_CUTS):
                pl.when(is_far)(lambda: self.up_[n].wait_send())

                def both(n=n):
                    self.keep_[n].wait_send()
                    self.give_[n].wait_send()

                pl.when(is_near)(both)

        def finish(self):
            for a in range(n_dp):
                pl.when(dp == a)(lambda: self.stay_[a].wait())

                def other(a=a):
                    self.go_[a].wait_send()
                    self.got_[a].wait_recv()

                pl.when(dp != a)(other)

    res_back = Back(0, res, dqkv.at[0:rows, 0:d], dqkv.at[rows:2 * rows, 0:d], out_o)
    grad_back = Back(1, h, act.at[0:rows, 0:d], act.at[rows:2 * rows, 0:d], ig_o)

    fls, sls, tls = (None, fl1, fl2, fl3), (None, sl1, sl2, sl3), (tl3, tl1, tl2, tl3)

    def first_place(g, i, k):
        w = widths[g]
        if g:
            return fls[g].at[i, :, k * w:(k + 1) * w]
        at = per * (2 * i + k // 2)
        return act.at[at:at + per, d + (k % 2) * w:d + (k % 2 + 1) * w]

    def second_place(g, k):
        w = widths[g]
        return sls[g].at[:, k * w:(k + 1) * w] if g else xmid.at[per * k:per * (k + 1), d // 2:d // 2 + w]

    def area(g, q, k):
        w = widths[g]
        return mats[g].at[per * q:per * (q + 1), k * w:(k + 1) * w]

    def first_pair(g, k):
        side = 1 if k < 2 else 2
        return [remote(area(g, q, k), first_place(g, i, k), (dp ^ (2 * side), lane)) for i, q in enumerate((3, side))]

    firsts = [[first_pair(g, k) for k in range(LANES)] for g in range(n_g)]
    seconds = [[remote(area(g, 2 if k < 2 else 1, k), second_place(g, k), (dp ^ (4 if k < 2 else 2), lane)) for k in range(LANES)]
               for g in range(n_g)]
    turns = [[None] + [remote(area(g, 0, k), tls[g].at[k - 1, :, 0:widths[g]], (dp, lax.rem(lane + LANES - k, LANES))) for k in range(1, LANES)]
             for g in range(n_g)]
    lasts = [remote(thirds[g].at[0], thirds[g].at[1], mate) for g in range(n_g)]

    def pass_on(g, k):
        firsts[g][k][0].wait_recv()
        here = area(g, 2 if k < 2 else 1, k)
        here[...] = (here[...].astype(F32) + first_place(g, 0, k)[...].astype(F32)).astype(BF)
        seconds[g][k].start()

    def settle(g, k):
        firsts[g][k][1].wait_recv()
        seconds[g][k].wait_recv()
        here = area(g, 0, k)
        here[...] = (here[...].astype(F32) + first_place(g, 1, k)[...].astype(F32) + second_place(g, k)[...].astype(F32)).astype(BF)
        if k:
            turns[g][k].start()

    out_copies = []

    def put(src, dst):
        c = local(src, dst)
        c.start()
        out_copies.append(c)

    mine = pl.ds(pl.multiple_of(core * wd, wd), wd)
    theirs = pl.ds(pl.multiple_of((1 - core) * wd, wd), wd)

    def lay(g, half, value):
        w = widths[g]
        if g == 3:
            tall[pl.ds(pl.multiple_of(half * w, w), w), :] = jnp.transpose(value)
        elif g == 1:
            wide_o[pl.ds(pl.multiple_of(half * w, w), w), :] = jnp.transpose(value)
        elif g == 2:
            attn[0:wd, pl.ds(pl.multiple_of(half * w, w), w)] = value
        else:
            for t in range(3):
                attn[wd * (t + 1):wd * (t + 2), pl.ds(pl.multiple_of(half * (w // 3), w // 3), w // 3)] = value[:, t * (w // 3):(t + 1) * (w // 3)]

    def total(g):
        w = widths[g]
        for k in range(1, LANES):
            turns[g][k].wait_recv()

        def add(rs):
            v = mats[g][rs, 0:w].astype(F32)
            for k in range(LANES - 1):
                v = v + tls[g][k, rs, 0:w].astype(F32)
            return v

        thirds[g][0] = add(theirs).astype(BF)
        lasts[g].start()
        lay(g, core, add(mine))

    def close(g):
        lasts[g].wait_recv()
        lay(g, 1 - core, thirds[g][1].astype(F32))
        if g == 3:
            put(tall, w2_o)
        elif g == 1:
            put(wide_o, wo_o)
        elif g == 2:
            put(attn.at[0:wd, 0:2 * widths[2]], w1_o)
        else:
            for t in range(3):
                put(attn.at[wd * (t + 1):wd * (t + 2), 0:2 * widths[1]], qkv_o.at[t])

    def blocks(g, a, b, q):
        w = widths[g]

        def one(k, carry):
            cols = pl.ds(pl.multiple_of(k * w, w), w)
            mats[g][per * q:per * (q + 1), cols] = dot_g(a[:, per * q:per * (q + 1)], b[:, cols]).astype(BF)
            return carry

        lax.fori_loop(0, LANES, one, 0)

    def grads(g, a, b, between=None):
        for q in (3, 1, 2, 0):
            blocks(g, a, b, q)
            if between:
                between(q)
            if q:
                for k in range(LANES):
                    if q == 3:
                        firsts[g][k][0].start()
                    elif (q == 1) == (k < 2):
                        firsts[g][k][1].start()

    def join(x, size, n):
        c = remote(x.at[n * size:(n + 1) * size, 0:d], x.at[rows + n * size:rows + (n + 1) * size, 0:d], mate)
        c.start()
        ends.pop()
        return c

    def fold(which, term, before=()):
        copies = []
        size = rows // 2
        for n in range(2):
            if before:
                before[n].wait_send()
            sbuf[n * size:(n + 1) * size] = term(slice(rows + n * size, rows + (n + 1) * size)).astype(BF)
            c = remote(sbuf.at[n * size:(n + 1) * size], rbuf.at[which, n * size:(n + 1) * size], mate)
            c.start()
            copies.append(c)
            if not before:
                ends.pop()
        for n in range(2):
            rs = slice(n * size, (n + 1) * size)
            part[rs, :] = term(rs)
        return copies

    loads["res"].wait()
    for n in range(DEAL_CUTS):
        res_back.start(n)
    loads["ffn"].wait()
    loads["grd"].wait()
    half = rows // 2
    joins = []

    def chunk(n, m):
        return pl.ds(pl.multiple_of(n * half + m * cut, cut), cut)

    for n in range(2):

        def norm_3(m, carry, n=n):
            rs = chunk(n, m)
            g = grd[rs, :].astype(F32)
            dx, gx = norm_back_rows(part[rs, :], g, gains(3))
            low = dx.astype(BF)
            dfull[rs, :] = low
            sums[3:4, :] += column_sums(gx)
            sums[7:8, :] += column_sums(g)
            sums[9:10, :] += column_sums(low.astype(F32))
            return carry

        lax.fori_loop(0, half // cut, norm_3, 0)
        joins.append(join(dfull, half, n))
    loads["w2"].wait()
    loads["dg"].wait()
    for c in joins:
        c.wait_recv()
    w = widths[2]
    for k in range(LANES):
        cols = slice(k * w, (k + 1) * w)

        def hidden_units(r, carry, cols=cols, k=k):
            rs = pl.ds(pl.multiple_of(r * QB, QB), QB)
            low = (jnp.dot(dfull[rs, :], w2[:, cols], preferred_element_type=F32) * dg[rs, cols].astype(F32)).astype(BF)
            dg[rs, cols] = low
            sums[16 + k:17 + k, 0:w] += column_sums(low.astype(F32))
            return carry

        lax.fori_loop(0, 2 * rows // QB, hidden_units, 0)
    loads["act"].wait()
    res_back.merge(0)
    res_back.merge(1)

    def rows_back(q):
        if q == 3:
            res_back.merge(2)
        elif q == 1:
            res_back.merge(3)

    grads(3, dfull, act, rows_back)
    for c in joins:
        c.wait_send()
    loads["xin"].start()
    res_back.sent()
    loads["h"].start()
    loads["w1"].wait()
    copies = fold(0, lambda rs: dot_t(dg[rs, :], w1[...]))
    for k in range(LANES):
        pass_on(3, k)
    loads["xmid"].wait()
    grads(2, xmid, dg)
    for side in (2, 4):
        pl.semaphore_signal(room, inc=1, device_id=(dp ^ side, lane), device_id_type=MESH)
    loads["first"].wait()
    loads["attn"].wait()
    joins = []
    for n in range(2):
        copies[n].wait_recv()

        def middle(m, carry, n=n):
            rs = chunk(n, m)
            g = part[rs, :] + rbuf[0, rs].astype(F32)
            dx, gx = norm_back_rows(first[rs, :], g, gains(2))
            sums[2:3, :] += column_sums(gx)
            sums[6:7, :] += column_sums(g)
            f = grd[rs, :].astype(F32) + dx
            first[rs, :] = f
            dx, gx = norm_back_rows(attn[rs, :], f, gains(1))
            sums[1:2, :] += column_sums(gx)
            sums[5:6, :] += column_sums(f)
            low = dx.astype(BF)
            dqkv[rs, 0:d] = low
            sums[8:9, :] += column_sums(low.astype(F32))
            return carry

        lax.fori_loop(0, half // cut, middle, 0)
        joins.append(join(dqkv, half, n))
    loads["wo"].wait()
    loads["heads"].wait()
    for c in joins:
        c.wait_recv()
    width = heads.shape[1]

    def to_heads(r, carry):
        rs = pl.ds(pl.multiple_of(r * QB, QB), QB)
        xmid[rs, 0:width] = jnp.dot(dqkv[rs, 0:d], wo[...], preferred_element_type=F32).astype(BF)
        return carry

    lax.fori_loop(0, 2 * rows // QB, to_heads, 0)
    grads(1, dqkv, heads)
    for c in joins:
        c.wait_send()
    loads["qkv"].wait()
    loads["lse"].wait()
    def settle_all(g):
        for k in (1, 2, 3, 0):
            settle(g, k)

    def pass_all(g):
        for k in range(LANES):
            pass_on(g, k)

    def group_3():
        total(3)
        for k in range(1, LANES):
            pl.semaphore_signal(free, inc=1, device_id=(dp, lax.rem(lane + k, LANES)), device_id_type=MESH)

    events = [[lambda: settle_all(3)], [lambda: pass_all(2)], [group_3, lambda: pass_all(1)], [lambda: settle_all(2), lambda: settle_all(1)] + [lambda n=n: res_back.home(n) for n in range(DEAL_CUTS)]]
    loads["xin"].wait()
    loads["wq"].wait()
    proj = widths[0]
    kpos = held.places(0, 2 * rows, 1)
    for pair in range(width // PAIR):
        dkv[...] = jnp.zeros_like(dkv)

        def attend(i, carry, pair=pair):
            attn_back(i, pair, held, kpos, lse, xmid, qkv, dqkv, dkv)
            return carry

        lax.fori_loop(0, 2 * rows // QB, attend, 0)
        at = 3 * pair * PAIR
        dqkv[:, at + PAIR:at + 2 * PAIR] = dkv[0].astype(BF)
        dqkv[:, at + 2 * PAIR:at + 3 * PAIR] = dkv[1].astype(BF)
        if pair == 0:
            pl.semaphore_wait(room, 2)
        cols = slice(pair * proj, (pair + 1) * proj)
        for q in (3, 1 if pair < 2 else 2, 2 if pair < 2 else 1, 0):
            dg[per * q:per * (q + 1), cols] = dot_g(dfull[:, per * q:per * (q + 1)], dqkv[:, cols]).astype(BF)
            if q == 3:
                firsts[0][pair][0].start()
            elif (q == 1) == (pair < 2) and q:
                firsts[0][pair][1].start()
        for e in events[pair]:
            e()
    copies = fold(1, lambda rs: dot_t(dqkv[rs, :], wq[...]), copies)
    sums[10:12, :] += jnp.concatenate([column_sums(dqkv[:, 0:d].astype(F32)),
                                       jnp.concatenate([column_sums(dqkv[:, d:3 * d // 2].astype(F32)), jnp.zeros((1, d // 2), F32)], axis=1)], axis=0)
    loads["h"].wait()
    for n in range(2):
        copies[n].wait_recv()

        def start_rows(m, carry, n=n):
            rs = chunk(n, m)
            g = part[rs, :] + rbuf[1, rs].astype(F32)
            dx, gx = norm_back_rows(h[rs, :].astype(F32), g, gains(0))
            sums[0:1, :] += column_sums(gx)
            sums[4:5, :] += column_sums(g)
            f = first[rs, :] + dx
            for q in range(4):
                cols = pl.ds(pl.multiple_of((chip ^ q) * quarter, quarter), quarter)
                h[rs, cols] = f[:, q * quarter:(q + 1) * quarter].astype(BF)
            return carry

        lax.fori_loop(0, half // cut, start_rows, 0)
        for m in range(half // cut):
            grad_back.start(n * (half // cut) + m)
    vec_all[...] = jnp.zeros_like(vec_all)
    for q in range(4):
        cols = pl.ds(pl.multiple_of((chip ^ q) * quarter, quarter), quarter)
        vec_all[0:10, cols] = sums[0:10, q * quarter:(q + 1) * quarter]
    hw = widths[1]
    for k in range(LANES):
        owner = lax.rem(lane + LANES - k, LANES)
        cols = pl.ds(pl.multiple_of(owner * 2 * hw + core * hw, hw), hw)
        for row, t in ((10, 0), (11, 2)):
            at = (3 * k + t) * hw
            vec_all[row:row + 1, cols] = sums[10 + at // d:11 + at // d, at % d:at % d + hw]
        vec_all[pl.ds(12 + owner, 1), pl.ds(pl.multiple_of(core * w, w), w)] = sums[16 + k:17 + k, 0:w]
    partners = [mate, (dp ^ 2, lane), (dp ^ 4, lane), (dp, lane ^ 1), (dp, lane ^ 2)]
    rounds = [remote(vec_all, sums_in.at[i], partners[i]) for i in range(5)]

    def vec_round(i):
        rounds[i].wait()
        vec_all[...] = vec_all[...] + sums_in[i]
        if i < 4:
            rounds[i + 1].start()

    rounds[0].start()
    vec_round(0)
    grad_back.merge(0)
    close(3)
    vec_round(1)
    grad_back.merge(1)
    pass_on(0, 0)
    pass_on(0, 1)
    grad_back.merge(2)
    grad_back.home(0)
    vec_round(2)
    pass_on(0, 2)
    pass_on(0, 3)
    grad_back.merge(3)
    grad_back.home(1)
    vec_round(3)
    total(2)
    grad_back.home(2)
    total(1)
    grad_back.home(3)
    pl.semaphore_wait(free, LANES - 1)
    settle_all(0)
    vec_round(4)
    vec_o[...] = vec_all[...]
    close(2)
    close(1)
    total(0)
    close(0)
    res_back.finish()
    grad_back.sent()
    grad_back.finish()
    for c in out_copies:
        c.wait()
    for c in ends:
        if not any(c is r for r in rounds):
            c.wait_send()


def attn_back(i, pair, held, kpos, lse, grads, qkv, dqkv, dkv):
    begin = pl.multiple_of(i * QB, QB)
    rs = pl.ds(begin, QB)
    bias = held.bias(begin, kpos)
    lane = lax.broadcasted_iota(jnp.int32, (1, PAIR), 1)
    at = 3 * pair * PAIR
    query = qkv[rs, at:at + PAIR]
    key, value = qkv[:, at + PAIR:at + 2 * PAIR], qkv[:, at + 2 * PAIR:at + 3 * PAIR]
    grad = grads[rs, pair * PAIR:(pair + 1) * PAIR]
    dq = jnp.zeros(query.shape, F32)
    dk = jnp.zeros(key.shape, F32)
    dv = jnp.zeros(key.shape, F32)
    for side in range(2):
        mine = (lane >= side * DH) & (lane < (side + 1) * DH)
        piece = jnp.where(mine, query * 0.125, 0.0).astype(BF)
        gpart = jnp.where(mine, grad, jnp.zeros_like(grad))
        score = dot_t(piece, key) + bias
        index = pair * 2 + side
        prob = jnp.exp(score - lse[rs, index:index + 1])
        gprob = dot_t(gpart, value)
        inner = jnp.sum(prob * gprob, axis=-1, keepdims=True)
        gscore = (prob * (gprob - inner)).astype(BF)
        dq += jnp.dot(gscore, jnp.where(mine, key, jnp.zeros_like(key)), preferred_element_type=F32)
        dk += dot_g(gscore, piece)
        dv += dot_g(prob.astype(BF), gpart)
    dqkv[rs, at:at + PAIR] = (dq * 0.125).astype(BF)
    dkv[0] += dk
    dkv[1] += dv


def backward_call(widths, lengths, deal, ln_gain, saved):
    (wq, wo, w1, w2, h, xin, qkv, heads, lse, attn, first, xmid, act, dg, ffn, res, grd) = saved
    rows, d = h.shape
    per, wd = d // 4, d // 8
    shape, vm = jax.ShapeDtypeStruct, pltpu.VMEM
    like = lambda x: vm(x.shape, x.dtype)
    out = [shape((3, wd, 2 * widths[1]), F32), shape((2 * widths[1], wd), F32), shape((wd, 2 * widths[2]), F32), shape((2 * widths[3], wd), F32),
           shape((rows, d), BF), shape((rows, d), BF), shape((16, d), F32), shape((2, rows, d), BF), shape((8, 128), F32)]
    scratch = [like(x) for x in (wq, wo, w1, w2, ffn, grd, act, dg, xmid, first, attn, heads, qkv, lse, xin, h)]
    scratch += [vm(qkv.shape, BF), vm((2, 2 * rows, PAIR), F32), vm((rows, d), BF), vm((2, rows, d), BF), vm((2, rows, d), BF)]
    order = (3, 2, 1)
    scratch += [vm((2, per, LANES * widths[g]), BF) for g in order]
    scratch += [vm((per, LANES * widths[g]), BF) for g in order]
    scratch += [vm((LANES - 1, per, widths[g]), BF) for g in order]
    scratch += [vm((2, wd, w), BF) for w in widths]
    scratch += [vm((2 * widths[3], wd), F32), vm((2 * widths[1], wd), F32), vm((24, d), F32), vm((5, 16, d), F32), vm((16, d), F32), vm((8, d), F32),
                pltpu.SemaphoreType.REGULAR, pltpu.SemaphoreType.REGULAR, pltpu.SemaphoreType.DMA((BWD_SEMS,))]
    return pl.pallas_call(
        partial(backward_kernel, widths),
        in_specs=[SMEM, SMEM, IN_VMEM] + [ANY] * 17,
        out_specs=[ANY] * 6 + [IN_VMEM, ANY, IN_VMEM],
        out_shape=out,
        scratch_shapes=scratch,
        compiler_params=pltpu.CompilerParams(collective_id=2, has_side_effects=True, vmem_limit_bytes=67043328),
        name="backward",
    )(lengths, deal, ln_gain, *saved)


def results_kernel(vec, *refs):
    lane = lax.axis_index("tensor")
    count = (len(refs) - 6) // 2
    for src, dst in zip(refs[:count], refs[count:2 * count]):
        dst[...] = src[...]
    qv, b_o, b_1, b_2, gain, shift = refs[2 * count:]
    part = qv.shape[1]
    qv[...] = vec[10:12, pl.ds(pl.multiple_of(lane * part, part), part)]
    b_o[...] = vec[8:9, :]
    b_1[...] = vec[pl.ds(12 + lane, 1), :]
    b_2[...] = vec[9:10, :]
    gain[...] = vec[0:4, :]
    shift[...] = vec[4:8, :]


def results_call(vec, large, part):
    d = vec.shape[1]
    shape = jax.ShapeDtypeStruct
    small = [shape((2, part), F32), shape((1, d), F32), shape((1, d), F32), shape((1, d), F32), shape((4, d), F32), shape((4, d), F32)]
    return pl.pallas_call(
        results_kernel,
        in_specs=[IN_VMEM] * (1 + len(large)),
        out_specs=[IN_VMEM] * (len(large) + 6),
        out_shape=[shape(x.shape, x.dtype) for x in large] + small,
        compiler_params=pltpu.CompilerParams(vmem_limit_bytes=67043328),
        name="results",
    )(vec, *large)


def feature_turn(x):
    n = lax.axis_size("dp") // 2
    chip = lax.axis_index("dp") // 2
    lead = x.shape[:-1]
    width = x.shape[-1] // n
    bits = n.bit_length() - 1
    y = x.reshape(lead + (2,) * bits + (width,))
    for b in range(bits):
        axis = len(lead) + bits - 1 - b
        y = jnp.where((chip >> b) & 1 == 1, jnp.flip(y, axis), y)
    return y.reshape(x.shape)


def body(tokens, cotangent, lengths, deal, w_qkv, w_o, w_1, w_2, b_qv, b_o, b_1, b_2, ln_gain, ln_bias):
    n_dp, lanes = lax.axis_size("dp"), lax.axis_size("tensor")
    dp, lane = lax.axis_index("dp"), lax.axis_index("tensor")
    core, chip = dp % 2, dp // 2
    rows = tokens.shape[0]
    both = ("dp", "tensor")
    near, far = deal_perms(n_dp)
    back_near, back_far = [(b, a) for a, b in near], [(b, a) for a, b in far]

    if n_dp == 8 and lanes == LANES:
        hw, fw = w_o.shape[0] // 2, w_1.shape[1] // 2
        widths = (3 * hw, hw, fw, fw)
        saved = forward_call(widths, tokens, cotangent, lengths, deal, w_qkv, w_o, w_1, w_2, b_qv, b_1[None], b_o[None], b_2[None], ln_gain, ln_bias)
        qkv_grad, out_grad, up_grad, down_grad, output, input_grad, vector, _, _ = backward_call(widths, lengths, deal, ln_gain, saved[:17])
        *large, qv, bias_o_sum, bias_1_sum, bias_2_sum, gain_sum, shift_sum = results_call(
            vector, (output, input_grad, qkv_grad, out_grad, up_grad, down_grad), b_qv.shape[1])
        return (*large, qv, bias_o_sum[0], bias_1_sum[0], bias_2_sum[0], gain_sum, shift_sum)

    per = lengths.shape[0] // n_dp

    def pack_ends(pack):
        picked = lax.dynamic_slice_in_dim(deal, pack * per, per)
        lookup = picked[:, None] == jnp.arange(lengths.shape[0], dtype=jnp.int32)[None, :]
        lens = jnp.sum(jnp.where(lookup, lengths[None, :], 0), axis=1)
        ends = jnp.sum(jnp.where(jnp.arange(per)[:, None] >= jnp.arange(per)[None, :], lens[None, :], 0), axis=1)
        return ends, ends - lens, jnp.sum(jnp.where(lens == HALF, ends - lens, 0))

    half = lane % 2
    ends, starts, cut = pack_ends(chip * 2 + lane // 2)
    _, _, cut_home = pack_ends(dp)
    index = jnp.arange(rows, dtype=jnp.int32)
    slots = jnp.concatenate([core * rows + index, (1 - core) * rows + index])
    place = jnp.where(slots >= cut, slots + HALF * half, slots + HALF * (1 - half))
    seg_start = jnp.max(jnp.where(place[:, None] >= starts[None, :], starts[None, :], 0), axis=1)
    qpos, qstart, kpos = place[:, None], seg_start[:, None], place[None, :]
    keep = ((core * rows + index) >= cut)[:, None]
    keep_home = (((lane % 2) * rows + index) >= cut_home)[:, None]

    def deal_in(x):
        moved = lax.all_to_all(x, "dp", split_axis=0, concat_axis=0, tiled=True)
        return jnp.where(keep, lax.ppermute(moved, both, near), lax.ppermute(moved, both, far))

    def deal_out(x):
        moved = jnp.where(keep_home, lax.ppermute(x, both, back_near), lax.ppermute(x, both, back_far))
        return lax.all_to_all(moved, "dp", split_axis=0, concat_axis=0, tiled=True)

    def halves(x):
        w = x.shape[-1] // 2
        return (lax.dynamic_slice_in_dim(x, core * w, w, x.ndim - 1), lax.dynamic_slice_in_dim(x, (1 - core) * w, w, x.ndim - 1))

    qm, qo = halves(w_qkv)
    om, oo = halves(w_o.T)
    um, uo = halves(w_1)
    dm, do = halves(w_2.T)
    own = jnp.concatenate([qm[0], qm[1], qm[2], om, um, dm], axis=1)
    other = jnp.concatenate([qo[0], qo[1], qo[2], oo, uo, do], axis=1)
    hw, fw = om.shape[1], um.shape[1]
    widths = (3 * hw, hw, fw, fw)
    small = jnp.concatenate([halves(b_qv[0:1])[0], halves(b_qv[1:2])[0], halves(b_1[None])[0]], axis=1)
    small = jnp.concatenate([small, jnp.zeros((7, small.shape[1]), F32)])
    order = (lane - jnp.arange(lanes)) % lanes
    gain, shift = feature_turn(ln_gain), feature_turn(ln_bias)
    bias_o, bias_2 = feature_turn(b_o[None])[0], feature_turn(b_2[None])[0]

    def join(x):
        return jnp.concatenate([x, swap_dp(x, 1)], axis=0)

    def fold(x):
        return x[:rows] + swap_dp(x[rows:].astype(BF), 1).astype(F32)

    mm = partial(jnp.dot, preferred_element_type=F32)
    mm_t = lambda a, b: lax.dot_general(a, b, (((1,), (1,)), ((), ())), preferred_element_type=F32)
    mm_g = lambda a, b: lax.dot_general(a, b, (((0,), (0,)), ((), ())), preferred_element_type=F32)
    if True:
        blocks = gather_weights(own, other)
        wq, wo, w1, w2 = (weight_of(blocks, sum(widths[:i]), w) for i, w in enumerate(widths))
        smalls = jnp.take(lax.all_gather(small[0], "tensor"), order, axis=0)
        bias_q, bias_v, bias_1 = smalls[:, :hw], smalls[:, hw:2 * hw], smalls[:, 2 * hw:].reshape(-1)
        bias_qkv = jnp.concatenate([bias_q, jnp.zeros_like(bias_q), bias_v], axis=1).reshape(-1)
        hidden = feature_turn(deal_in(tokens)).astype(F32)
        normed_in = join(scaled_norm(hidden, gain[0], shift[0]).astype(BF))
        qkv = (mm(normed_in, wq) + bias_qkv).astype(BF)
        heads_out, lse = attn_forward(qpos, qstart, kpos, qkv)
        attn_out = fold(mm_t(heads_out, wo)) + bias_o
        first_sum = hidden + scaled_norm(attn_out, gain[1], shift[1])
        normed_mid = join(scaled_norm(first_sum, gain[2], shift[2]).astype(BF))
        pre_act = mm(normed_mid, w1) + bias_1
        cdf = 0.5 + 0.5 * lax.erf(pre_act * 0.7071067811865476)
        act = (pre_act * cdf).astype(BF)
        dgelu = (cdf + pre_act * (0.3989422804014327 * jnp.exp(-0.5 * pre_act * pre_act))).astype(BF)
        ffn_out = fold(mm_t(act, w2)) + bias_2
        result = feature_turn((first_sum + scaled_norm(ffn_out, gain[3], shift[3])).astype(BF))
        grad_result = feature_turn(deal_in(cotangent)).astype(F32)

    grad_ffn, gain_3, shift_3 = norm_back(ffn_out, gain[3], shift[3], grad_result)
    grad_ffn_low = grad_ffn.astype(BF)
    bias_2_grad = jnp.sum(grad_ffn_low.astype(F32), axis=0)
    grad_ffn_full = join(grad_ffn_low)
    grad_act = mm(grad_ffn_full, w2)
    down_part = mm_g(grad_ffn_full, act).astype(BF)
    grad_pre = (grad_act * dgelu.astype(F32)).astype(BF)
    bias_1_grad = jnp.sum(grad_pre.astype(F32), axis=0)
    grad_mid = fold(mm_t(grad_pre, w1))
    up_part = mm_g(normed_mid, grad_pre).astype(BF)
    grad_first_part, gain_2, shift_2 = norm_back(first_sum, gain[2], shift[2], grad_mid)
    grad_first = grad_result + grad_first_part
    grad_attn, gain_1, shift_1 = norm_back(attn_out, gain[1], shift[1], grad_first)
    grad_attn_low = grad_attn.astype(BF)
    bias_o_grad = jnp.sum(grad_attn_low.astype(F32), axis=0)
    grad_attn_full = join(grad_attn_low)
    grad_heads = mm(grad_attn_full, wo).astype(BF)
    out_part = mm_g(grad_attn_full, heads_out).astype(BF)
    grad_qkv = attn_backward(qpos, qstart, kpos, lse, grad_heads, qkv)
    bias_qkv_grad = jnp.sum(grad_qkv.astype(F32), axis=0).reshape(lanes, 3, hw)
    grad_in = fold(mm_t(grad_qkv, wq))
    qkv_part = mm_g(normed_in, grad_qkv).astype(BF)
    grad_hidden_part, gain_0, shift_0 = norm_back(hidden, gain[0], shift[0], grad_in)
    grad_hidden = feature_turn((grad_first + grad_hidden_part).astype(BF))

    def by_lane(x):
        x = jnp.take(x.reshape(lanes, -1), order, axis=0)
        both_halves = jnp.stack([jnp.where(core == 0, x, 0.0), jnp.where(core == 1, x, 0.0)], axis=1)
        return both_halves.reshape(-1)

    d = tokens.shape[1]
    stack = jnp.stack([gain_0, gain_1, gain_2, gain_3, shift_0, shift_1, shift_2, shift_3, bias_o_grad, bias_2_grad])
    vector = jnp.concatenate([feature_turn(stack).reshape(-1), by_lane(bias_qkv_grad[:, 0]), by_lane(bias_qkv_grad[:, 2]), by_lane(bias_1_grad)])
    parts = [qkv_part, out_part, up_part, down_part]
    output, input_grad = deal_out(result), deal_out(grad_hidden)
    vector = lax.psum(vector, both)
    shards = [scatter_grads([p.astype(F32)]) for p in parts]
    gain_total, shift_total = vector[:4 * d].reshape(4, d), vector[4 * d:8 * d].reshape(4, d)
    bias_o_total, bias_2_total = vector[8 * d:9 * d], vector[9 * d:10 * d]
    mine = lambda x: lax.dynamic_slice_in_dim(x.reshape(lanes, -1), lane, 1, 0)[0]
    bias_qv_total = jnp.stack([mine(vector[10 * d:11 * d]), mine(vector[11 * d:12 * d])])
    bias_1_total = mine(vector[12 * d:])

    spread = lambda x: jnp.concatenate([x[0], x[1]], axis=-1)
    qkv_grad, out_grad, up_grad, down_grad = shards
    qkv_out = jnp.stack([spread(qkv_grad[:, :, i * hw:(i + 1) * hw]) for i in range(3)])
    return (
        output, input_grad, qkv_out, spread(out_grad).T, spread(up_grad), spread(down_grad).T,
        bias_qv_total, bias_o_total, bias_1_total, bias_2_total, gain_total, shift_total,
    )


def solution(mesh):
    rows = P(("dp", "tensor"), None)
    weights = (P(None, "dp", "tensor"), P("tensor", "dp"), P("dp", "tensor"), P("tensor", "dp"))
    vectors = (P(None, "tensor"), P(), P("tensor"), P(), P(), P())
    return jax.shard_map(
        body,
        mesh=mesh,
        in_specs=(rows, rows, P(), P()) + weights + vectors,
        out_specs=(rows, rows) + weights + vectors,
        check_vma=False,
    )
```
